32 devices in a mesh: dp: 16 (over z, y, core), seq: 2 (over x).
Axes of the slice: x: 2, y: 2, z: 4, core: 2. Of those that a mesh axis runs over, the one named last changes fastest.
Arguments:
- tokens: bfloat16 [16, 1024, 1024], P('dp', 'seq'), may hold values from -6 to 6
- cotangent: bfloat16 [16, 1024, 1024], P('dp', 'seq'), may hold values from -6 to 6
- doc_lengths: int32 [16, 8], P('dp'), may hold values from 1 to 512, 1024 in all within a row
- attn_gain: bfloat16 [1024], replicated, may hold values from 0.5 to 1.5
- w_query: bfloat16 [1024, 1024], replicated, may hold values from -0.1875 to 0.1875
- w_key: bfloat16 [1024, 512], replicated, may hold values from -0.1875 to 0.1875
- w_value: bfloat16 [1024, 512], replicated, may hold values from -0.1875 to 0.1875
- query_gain: bfloat16 [64], replicated, may hold values from 0.5 to 1.5
- key_gain: bfloat16 [64], replicated, may hold values from 0.5 to 1.5
- w_out: bfloat16 [1024, 1024], replicated, may hold values from -3 to 3
- ffn_gain: bfloat16 [1024], replicated, may hold values from 0.5 to 1.5
- w_gate: bfloat16 [1024, 4608], replicated, may hold values from -0.1875 to 0.1875
- w_up: bfloat16 [1024, 4608], replicated, may hold values from -0.1875 to 0.1875
- w_down: bfloat16 [4608, 1024], replicated, may hold values from -0.09375 to 0.09375
Outputs:
- output: float32 [16, 1024, 1024], P('dp', 'seq')
- d_tokens: float32 [16, 1024, 1024], P('dp', 'seq')
- d_attn_gain: float32 [1024], replicated
- d_w_query: float32 [1024, 1024], P('dp', 'seq')
- d_w_key: float32 [1024, 512], P('dp', 'seq')
- d_w_value: float32 [1024, 512], P('dp', 'seq')
- d_query_gain: float32 [64], replicated
- d_key_gain: float32 [64], replicated
- d_w_out: float32 [1024, 1024], P('dp', 'seq')
- d_ffn_gain: float32 [1024], replicated
- d_w_gate: float32 [1024, 4608], P('dp', 'seq')
- d_w_up: float32 [1024, 4608], P('dp', 'seq')
- d_w_down: float32 [4608, 1024], P('dp', 'seq')
The draws below stay inside these ranges and needn't reach their ends.
Inputs may be any that keep to these rules, and one draw needn't show every extreme that they name: `doc_lengths`: each row's 8 documents fill its 1024 positions, and one of them is 512 long.
All inputs are finite; a program needn't handle non-finite values.
Results may differ from the reference program's by a relative error of at most 0.014.
Values may be sent and summed in bfloat16 or wider, within the bound.
No kernel may reach another device: no remote copies, remote signals or barrier semaphores. Data moves between devices by JAX's collectives and lax.ppermute only.
A program may use at most 256 MiB of HBM per device.

```python
import math
import jax
import jax.numpy as jnp
import numpy as np
from jax import lax

D = 1024
HEADS = 16
KV = 8
HD = 64
FF = 4608
DOCS = 8
SEQ_LEN = 1024
ROWS = 16
QB = 512


def raised(array, rng, source, target, shards_of, factor):
    def block_of(dim):
        return (jnp.arange(array.shape[dim]) // (array.shape[dim] // shards_of)).reshape((-1,) + (1,) * (array.ndim - 1 - dim))

    first = jax.random.permutation(rng, shards_of)[block_of(target)]
    other_side = (block_of(target) + shards_of // 2) % shards_of
    return jnp.where((block_of(source) == first) | (block_of(source) == other_side), factor * array, array)


def steps_of(key, shape, split, low, top_value):
    loudness = 1.0
    for position, blocks in split:
        heights = jax.random.uniform(jax.random.fold_in(jax.random.fold_in(key, 6), position), (blocks,), jnp.float32, low / len(split), top_value / len(split))
        loudness = loudness * jnp.repeat(jnp.exp(heights), shape[position] // blocks).reshape((-1,) + (1,) * (len(shape) - 1 - position))
    return loudness


def profile(amount, total, reach, slope):
    portions = [(1 << 20) // math.isqrt(rank ** slope) + 1 for rank in range(2, amount + 1)]
    rest, counts = total - reach - (amount - 1), [1] * (amount - 1)
    while rest > 0:
        movable = [i for i in range(amount - 1) if counts[i] < reach]
        pool, left = sum([portions[i] for i in movable]), rest
        for i in movable:
            addition = min(reach - counts[i], max(1, left * portions[i] // pool), rest)
            counts[i] = counts[i] + addition
            rest = rest - addition
    return np.array([reach] + counts)


def uneven_parts(stream_key, count, total, limit, lean):
    if count == 2:
        one = jax.random.randint(stream_key, (), max(1, total - limit), min(limit, total - 1) + 1)
        return jnp.stack([one, total - one])
    tallies = jnp.asarray(profile(count, total, limit, lean), jnp.int32)
    pairs = (count - 1) // 2
    giver, receiver = tallies[1:1 + 2 * pairs:2], tallies[2:2 + 2 * pairs:2]
    slack = jnp.minimum(giver - 1, limit - receiver)
    moved = jax.random.randint(jax.random.fold_in(stream_key, 1), (pairs,), 0, 1 << 20) % (slack + 1)
    tallies = tallies.at[1:1 + 2 * pairs:2].set(giver - moved).at[2:2 + 2 * pairs:2].set(receiver + moved)
    return tallies[jax.random.permutation(jax.random.fold_in(stream_key, 2), count)]


def normal_values(rng, shape, scale, most, pieces=(), kind=jnp.bfloat16):
    values = scale * jax.random.normal(rng, shape, jnp.float32)
    if pieces:
        values = values * steps_of(rng, shape, pieces, -0.22, 0.18)
    return jnp.clip(values, -most, most).astype(kind)


def noise_with(stream_key, shape, scale, most, shards, heavy, held_as=jnp.bfloat16):
    values = scale * jax.random.normal(stream_key, shape, jnp.float32)
    if shards:
        values = values * steps_of(stream_key, shape, shards, -0.22, 0.18)
    return jnp.clip(raised(values, jax.random.fold_in(stream_key, 3), *heavy), -most, most).astype(held_as)


def setup_inputs(seed: int = 0) -> dict:
    seeds = jax.random.split(jax.random.key(seed), 15)
    tokens = noise_with(seeds[0], (ROWS, SEQ_LEN, D), 1.0, 6.0, ((0, 16), (1, 2)), (0, 2, 16, 2.0))
    cotangent = noise_with(seeds[1], (ROWS, SEQ_LEN, D), 1.0, 6.0, ((0, 16), (1, 2)), (1, 2, 2, 2.0))
    doc_lengths = jax.vmap(lambda own: uneven_parts(own, DOCS, SEQ_LEN, SEQ_LEN // 2, 2))(jax.random.split(seeds[2], ROWS)).reshape((ROWS, DOCS)).astype(jnp.int32)
    attn_gain = jnp.clip(1.0 + 0.1 * jax.random.normal(seeds[3], (D,), jnp.float32), 0.5, 1.5).astype(jnp.bfloat16)
    w_query = normal_values(seeds[4], (D, HEADS * HD), D ** -0.5, 0.1875)
    w_key = normal_values(seeds[5], (D, KV * HD), D ** -0.5, 0.1875)
    w_value = normal_values(seeds[6], (D, KV * HD), D ** -0.5, 0.1875)
    query_gain = jnp.clip(1.0 + 0.1 * jax.random.normal(seeds[7], (HD,), jnp.float32), 0.5, 1.5).astype(jnp.bfloat16)
    key_gain = jnp.clip(1.0 + 0.1 * jax.random.normal(seeds[8], (HD,), jnp.float32), 0.5, 1.5).astype(jnp.bfloat16)
    w_out = normal_values(seeds[9], (HEADS * HD, D), (max(1, HEADS * HD // 256)) ** -0.5, 3.0)
    ffn_gain = jnp.clip(1.0 + 0.1 * jax.random.normal(seeds[10], (D,), jnp.float32), 0.5, 1.5).astype(jnp.bfloat16)
    w_gate = normal_values(seeds[11], (D, FF), D ** -0.5, 0.1875)
    w_up = normal_values(seeds[12], (D, FF), D ** -0.5, 0.1875)
    w_down = normal_values(seeds[13], (FF, D), FF ** -0.5, 0.09375)
    return {"tokens": tokens, "cotangent": cotangent, "doc_lengths": doc_lengths, "attn_gain": attn_gain, "w_query": w_query, "w_key": w_key, "w_value": w_value, "query_gain": query_gain, "key_gain": key_gain, "w_out": w_out, "ffn_gain": ffn_gain, "w_gate": w_gate, "w_up": w_up, "w_down": w_down}


HIGH = lax.Precision.HIGHEST
EPSILON = 1e-06

@jax.custom_vjp
def low(v):
    return lax.optimization_barrier(v.astype(jnp.bfloat16)).astype(jnp.float32)

@jax.custom_vjp
def low_back(v):
    return v

def low_keep(v):
    return (low(v), None)

def low_pass(kept, grad):
    return (grad,)

def back_keep(v):
    return (v, None)

def back_low(kept, grad):
    return (low(grad),)
low.defvjp(low_keep, low_pass)
low_back.defvjp(back_keep, back_low)

def matmul(left, right):
    return jnp.dot(left, right, precision=HIGH, preferred_element_type=jnp.float32)

def rms_scale(values, gain):
    return values * lax.rsqrt(lax.optimization_barrier(jnp.mean(values * values, axis=-1, keepdims=True)) + EPSILON) * gain

def rope_tables(first, count, width):
    half = width // 2
    spread = jnp.exp(jnp.arange(half, dtype=jnp.float32) * (-2.0 * math.log(1000000.0) / width))
    places = (first + jnp.arange(count, dtype=jnp.int32)).astype(jnp.float32)
    angles = places[:, None] * spread[None, :]
    return (jnp.cos(angles)[:, None, :], jnp.sin(angles)[:, None, :])

def rotate(values, cosine, sine):
    half = values.shape[-1] // 2
    first_half = values[..., :half]
    second_half = values[..., half:]
    return jnp.concatenate([first_half * cosine - second_half * sine, second_half * cosine + first_half * sine], axis=-1)

def layer(row_input, segment, attn_gain, w_query, w_key, w_value, query_gain, key_gain, w_out, ffn_gain, w_gate, w_up, w_down):
    length = row_input.shape[0]
    group = HEADS // KV
    scale = HD ** (-0.5)
    normed = low(rms_scale(row_input, attn_gain))
    query_raw = low_back(matmul(normed, w_query)).reshape(length, HEADS, HD)
    key_raw = low_back(matmul(normed, w_key)).reshape(length, KV, HD)
    values = low_back(low(matmul(normed, w_value))).reshape(length, KV, HD)
    cosine, sine = rope_tables(0, length, HD)
    queries = low_back(low(rotate(rms_scale(query_raw, query_gain), cosine, sine)))
    keys = low_back(low(rotate(rms_scale(key_raw, key_gain), cosine, sine)))
    queries = queries.reshape(length, KV, group, HD)
    positions = jnp.arange(length, dtype=jnp.int32)

    def attend(begin):
        query_block = lax.dynamic_slice_in_dim(queries, begin, QB, 0)
        scores = low_back(jnp.einsum('qhgd,khd->hgqk', query_block, keys, precision=HIGH)) * scale
        rows_here = begin + jnp.arange(QB, dtype=jnp.int32)
        query_seg = lax.dynamic_slice_in_dim(segment, begin, QB, 0)
        allowed = (query_seg[:, None] == segment[None, :]) & (positions[None, :] <= rows_here[:, None])
        scores = jnp.where(allowed, scores, -jnp.inf)
        probs = jax.nn.softmax(scores, axis=-1)
        return jnp.einsum('hgqk,khd->qhgd', low(probs), values, precision=HIGH)
    starts = jnp.arange(length // QB, dtype=jnp.int32) * QB
    blocks_out = lax.map(jax.checkpoint(attend), starts)
    attended = low_back(low(blocks_out.reshape(length, HEADS * HD)))
    hidden = row_input + low_back(matmul(attended, w_out))
    hnormed = low(rms_scale(hidden, ffn_gain))
    gate = low_back(matmul(hnormed, w_gate))
    up_part = low_back(matmul(hnormed, w_up))
    act = low(jax.nn.silu(gate) * up_part)
    return hidden + low_back(matmul(act, w_down))

def reference(tokens, cotangent, doc_lengths, attn_gain, w_query, w_key, w_value, query_gain, key_gain, w_out, ffn_gain, w_gate, w_up, w_down):
    weights = tuple((w.astype(jnp.float32) for w in (attn_gain, w_query, w_key, w_value, query_gain, key_gain, w_out, ffn_gain, w_gate, w_up, w_down)))

    def row_step(totals, row):
        row_input, row_cot, lengths = row
        length = row_input.shape[0]
        ends = jnp.cumsum(lengths).astype(jnp.int32)
        positions = jnp.arange(length, dtype=jnp.int32)
        segment = lax.optimization_barrier(jnp.sum((ends[None, :] <= positions[:, None]).astype(jnp.int32), axis=1)).astype(jnp.int32)

        def forward(inputs, *params):
            return layer(inputs, segment, *params)
        result, pull = jax.vjp(forward, row_input.astype(jnp.float32), *weights)
        grads = pull(row_cot.astype(jnp.float32))
        updated = tuple((total + grad for total, grad in zip(totals, grads[1:])))
        return (updated, (result, grads[0]))
    zeros = tuple((jnp.zeros(w.shape, jnp.float32) for w in weights))
    totals, (results, input_grads) = lax.scan(row_step, zeros, (tokens, cotangent, doc_lengths))
    return (results, input_grads, totals[0], totals[1], totals[2], totals[3], totals[4], totals[5], totals[6], totals[7], totals[8], totals[9], totals[10])
```

```python
import math

import jax
import jax.numpy as jnp
from jax import lax
from jax.experimental import pallas as pl
from jax.experimental.pallas import tpu as pltpu
from jax.sharding import Mesh
from jax.sharding import PartitionSpec as P

EPSILON = 1e-06


def rms_scale(values, gain):
    return values * lax.rsqrt(jnp.mean(values * values, axis=-1, keepdims=True) + EPSILON) * gain


def norm_back(incoming, values, gain):
    inverse = lax.rsqrt(jnp.mean(values * values, axis=-1, keepdims=True) + EPSILON)
    unit = values * inverse
    scaled = incoming * gain
    d_values = inverse * (scaled - unit * jnp.mean(scaled * unit, axis=-1, keepdims=True))
    return (d_values, incoming * unit)


def rope_tables(first, count, width):
    half = width // 2
    spread = jnp.exp(jnp.arange(half, dtype=jnp.float32) * (-2.0 * math.log(1000000.0) / width))
    places = (first + jnp.arange(count, dtype=jnp.int32)).astype(jnp.float32)
    angles = places[:, None] * spread[None, :]
    return (jnp.cos(angles)[:, None, :], jnp.sin(angles)[:, None, :])


def rotate(values, cosine, sine):
    half = values.shape[-1] // 2
    first_half = values[..., :half]
    second_half = values[..., half:]
    return jnp.concatenate(
        [first_half * cosine - second_half * sine, second_half * cosine + first_half * sine],
        axis=-1,
    )


def reduce_grads(grads):
    partial_sum = lax.psum_scatter(grads, "dp", scatter_dimension=0, tiled=True)
    return lax.psum_scatter(partial_sum, "seq", scatter_dimension=1, tiled=True)


def general_body(
    tokens,
    cotangent,
    doc_lengths,
    attn_gain,
    w_query,
    w_key,
    w_value,
    query_gain,
    key_gain,
    w_out,
    ffn_gain,
    w_gate,
    w_up,
    w_down,
):
    shards = lax.axis_size("seq")
    local = tokens.shape[1]
    length = local * shards
    head_size = query_gain.shape[0]
    kv_count = w_key.shape[1] // head_size
    head_count = w_query.shape[1] // head_size
    group = head_count // kv_count
    kv_local = kv_count // shards
    block = min(512, length)
    num_blocks = length // block
    scale = head_size ** (-0.5)
    f32 = jnp.float32
    bf16 = jnp.bfloat16
    gain_attn = attn_gain.astype(f32)
    gain_query = query_gain.astype(f32)
    gain_key = key_gain.astype(f32)
    gain_ffn = ffn_gain.astype(f32)
    inputs = tokens[0].astype(f32)
    normed = rms_scale(inputs, gain_attn).astype(bf16)
    query_raw = jnp.dot(normed, w_query, preferred_element_type=f32).reshape(
        local, head_count, head_size
    )
    key_raw = jnp.dot(normed, w_key, preferred_element_type=f32).reshape(local, kv_count, head_size)
    values = (
        jnp.dot(normed, w_value, preferred_element_type=f32)
        .astype(bf16)
        .reshape(local, kv_count, head_size)
    )
    cosine, sine = rope_tables(lax.axis_index("seq") * local, local, head_size)
    query_rot = rotate(rms_scale(query_raw, gain_query), cosine, sine).astype(bf16)
    key_rot = rotate(rms_scale(key_raw, gain_key), cosine, sine).astype(bf16)
    packed_query = query_rot.reshape(local, kv_count, group * head_size)
    packed_kv = jnp.concatenate([key_rot, values], axis=2)
    query_heads, kv_heads = (
        lax.all_to_all(packed_query, "seq", split_axis=1, concat_axis=0, tiled=True),
        lax.all_to_all(packed_kv, "seq", split_axis=1, concat_axis=0, tiled=True),
    )
    query_all = query_heads.reshape(length, kv_local, group, head_size)
    key_all = kv_heads[:, :, :head_size]
    value_all = kv_heads[:, :, head_size:]
    positions = jnp.arange(length, dtype=jnp.int32)
    ends = jnp.cumsum(doc_lengths[0])
    segment = jnp.sum((ends[None, :] <= positions[:, None]).astype(jnp.int32), axis=1)
    starts = jnp.arange(num_blocks, dtype=jnp.int32) * block

    def allowed_at(begin):
        rows_here = begin + jnp.arange(block, dtype=jnp.int32)
        query_seg = lax.dynamic_slice_in_dim(segment, begin, block, 0)
        return (query_seg[:, None] == segment[None, :]) & (positions[None, :] <= rows_here[:, None])

    def block_scores(begin):
        query_block = lax.dynamic_slice_in_dim(query_all, begin, block, 0)
        scores = (
            jnp.einsum("qhgd,khd->hgqk", query_block, key_all, preferred_element_type=f32) * scale
        )
        return (query_block, jnp.where(allowed_at(begin), scores, -jnp.inf))

    def attend(begin):
        query_block, scores = block_scores(begin)
        top_score = jnp.max(scores, axis=-1, keepdims=True)
        expos = jnp.exp(scores - top_score)
        totals = jnp.sum(expos, axis=-1, keepdims=True)
        probs = (expos / totals).astype(bf16)
        result = jnp.einsum("hgqk,khd->qhgd", probs, value_all, preferred_element_type=f32)
        return (result.astype(bf16), top_score[..., 0] + jnp.log(totals[..., 0]))

    attended_heads, log_totals = lax.map(attend, starts)
    attended_heads = attended_heads.reshape(length, kv_local, group * head_size)
    attended = lax.all_to_all(
        attended_heads, "seq", split_axis=0, concat_axis=1, tiled=True
    ).reshape(local, head_count * head_size)
    hidden = inputs + jnp.dot(attended, w_out, preferred_element_type=f32)
    hnormed = rms_scale(hidden, gain_ffn).astype(bf16)
    gate = jnp.dot(hnormed, w_gate, preferred_element_type=f32)
    up_part = jnp.dot(hnormed, w_up, preferred_element_type=f32)
    act = (jax.nn.silu(gate) * up_part).astype(bf16)
    output = hidden + jnp.dot(act, w_down, preferred_element_type=f32)
    d_mlp = cotangent[0]
    grad_down = jnp.einsum("tf,td->fd", act, d_mlp, preferred_element_type=f32)
    d_act = jnp.einsum("td,fd->tf", d_mlp, w_down, preferred_element_type=f32)
    gate_again = jnp.dot(hnormed, w_gate, preferred_element_type=f32)
    up_again = jnp.dot(hnormed, w_up, preferred_element_type=f32)
    sigmoid_gate = jax.nn.sigmoid(gate_again)
    d_up = (d_act * gate_again * sigmoid_gate).astype(bf16)
    d_gate = (d_act * up_again * sigmoid_gate * (1.0 + gate_again * (1.0 - sigmoid_gate))).astype(
        bf16
    )
    grad_gate = jnp.einsum("td,tf->df", hnormed, d_gate, preferred_element_type=f32)
    grad_up = jnp.einsum("td,tf->df", hnormed, d_up, preferred_element_type=f32)
    ffn_sums = reduce_grads((grad_gate, grad_up, grad_down))
    d_hnormed = jnp.einsum("tf,df->td", d_gate, w_gate, preferred_element_type=f32) + jnp.einsum(
        "tf,df->td", d_up, w_up, preferred_element_type=f32
    )
    d_hidden_norm, ffn_gain_terms = norm_back(d_hnormed, hidden, gain_ffn)
    d_hidden = cotangent[0].astype(f32) + d_hidden_norm
    d_attn = d_hidden.astype(bf16)
    grad_out = jnp.einsum("tf,td->fd", attended, d_attn, preferred_element_type=f32)
    d_attended = jnp.einsum("td,fd->tf", d_attn, w_out, preferred_element_type=f32).astype(bf16)
    d_heads = lax.all_to_all(
        d_attended.reshape(local, kv_count, group * head_size),
        "seq",
        split_axis=1,
        concat_axis=0,
        tiled=True,
    )
    d_all = d_heads.reshape(length, kv_local, group, head_size)

    def attend_back(carry, item):
        begin, log_block = item
        query_block, scores = block_scores(begin)
        probs = jnp.exp(scores - log_block[..., None])
        d_block = lax.dynamic_slice_in_dim(d_all, begin, block, 0)
        d_probs = jnp.einsum("qhgd,khd->hgqk", d_block, value_all, preferred_element_type=f32)
        delta = jnp.sum(probs * d_probs, axis=-1, keepdims=True)
        d_scores = (scale * (probs * (d_probs - delta))).astype(bf16)
        d_query_block = jnp.einsum("hgqk,khd->qhgd", d_scores, key_all, preferred_element_type=f32)
        key_total = carry[0] + jnp.einsum(
            "hgqk,qhgd->khd", d_scores, query_block, preferred_element_type=f32
        )
        value_total = carry[1] + jnp.einsum(
            "hgqk,qhgd->khd", probs.astype(bf16), d_block, preferred_element_type=f32
        )
        return ((key_total, value_total), d_query_block.astype(bf16))

    empty = jnp.zeros((length, kv_local, head_size), f32)
    (d_keys, d_values), d_queries = lax.scan(attend_back, (empty, empty), (starts, log_totals))
    d_queries = d_queries.reshape(length, kv_local, group * head_size)
    d_kv = jnp.concatenate([d_keys.astype(bf16), d_values.astype(bf16)], axis=2)
    d_query_pos, d_kv_pos = (
        lax.all_to_all(d_queries, "seq", split_axis=0, concat_axis=1, tiled=True),
        lax.all_to_all(d_kv, "seq", split_axis=0, concat_axis=1, tiled=True),
    )
    d_query_rot = d_query_pos.reshape(local, head_count, head_size).astype(f32)
    d_query_raw, query_gain_terms = norm_back(
        rotate(d_query_rot, cosine, -sine), query_raw, gain_query
    )
    d_query_low = d_query_raw.reshape(local, head_count * head_size).astype(bf16)
    d_key_rot = d_kv_pos[:, :, :head_size].astype(f32)
    d_key_raw, key_gain_terms = norm_back(rotate(d_key_rot, cosine, -sine), key_raw, gain_key)
    d_key_low = d_key_raw.reshape(local, kv_count * head_size).astype(bf16)
    d_value_low = d_kv_pos[:, :, head_size:].reshape(local, kv_count * head_size)
    grad_query = jnp.einsum("td,tf->df", normed, d_query_low, preferred_element_type=f32)
    grad_key = jnp.einsum("td,tf->df", normed, d_key_low, preferred_element_type=f32)
    grad_value = jnp.einsum("td,tf->df", normed, d_value_low, preferred_element_type=f32)
    d_normed = jnp.einsum("tf,df->td", d_query_low, w_query, preferred_element_type=f32)
    d_normed = d_normed + jnp.einsum("tf,df->td", d_key_low, w_key, preferred_element_type=f32)
    d_normed = d_normed + jnp.einsum("tf,df->td", d_value_low, w_value, preferred_element_type=f32)
    d_input_norm, attn_gain_terms = norm_back(d_normed, inputs, gain_attn)
    d_inputs = d_hidden + d_input_norm
    attn_sums = reduce_grads((grad_query, grad_key, grad_value, grad_out))
    gain_totals = lax.psum(
        (
            jnp.sum(attn_gain_terms, axis=0),
            jnp.sum(query_gain_terms, axis=(0, 1)),
            jnp.sum(key_gain_terms, axis=(0, 1)),
            jnp.sum(ffn_gain_terms, axis=0),
        ),
        ("dp", "seq"),
    )
    return (
        output[None],
        d_inputs[None],
        gain_totals[0],
        attn_sums[0],
        attn_sums[1],
        attn_sums[2],
        gain_totals[1],
        gain_totals[2],
        attn_sums[3],
        gain_totals[3],
        ffn_sums[0],
        ffn_sums[1],
        ffn_sums[2],
    )


AXES = ("zh", "zl", "y", "c", "x")
QBLOCK = 256
F32 = jnp.float32
BF16 = jnp.bfloat16


def swap(v, axis):
    return lax.ppermute(v, axis, [(0, 1), (1, 0)])


def transpose_pair(v):
    return lax.ppermute(v, ("c", "x"), [(0, 0), (1, 2), (2, 1), (3, 3)])


def pick(bit, low, high):
    return jnp.where(bit == 0, low, high)


def in_order(bit, own, other, axis):
    return jnp.concatenate([pick(bit, own, other), pick(bit, other, own)], axis=axis)


def dot(left, right, left_dim, right_dim):
    return lax.dot_general(
        left, right, (((left_dim,), (right_dim,)), ((), ())), preferred_element_type=F32
    )


def part_columns(w, c):
    width = w.shape[1] // 4
    return [lax.dynamic_slice_in_dim(w, (2 * i + c) * width, width, 1) for i in range(2)]


def part_rows(w, c):
    width = w.shape[0] // 4
    return jnp.concatenate(
        [lax.dynamic_slice_in_dim(w, (2 * i + c) * width, width, 0) for i in range(2)], axis=0
    )


def rope_rows(values, gain, cosine, sine):
    unit = values * lax.rsqrt(jnp.mean(values * values, axis=0, keepdims=True) + EPSILON) * gain
    half = values.shape[0] // 2
    first, second = unit[:half], unit[half:]
    return jnp.concatenate([first * cosine - second * sine, second * cosine + first * sine], axis=0)


def rope_rows_back(incoming, values, gain, cosine, sine):
    half = values.shape[0] // 2
    first, second = incoming[:half], incoming[half:]
    turned = jnp.concatenate([first * cosine + second * sine, second * cosine - first * sine], axis=0)
    inverse = lax.rsqrt(jnp.mean(values * values, axis=0, keepdims=True) + EPSILON)
    unit = values * inverse
    scaled = turned * gain
    d_values = inverse * (scaled - unit * jnp.mean(scaled * unit, axis=0, keepdims=True))
    return d_values, turned * unit


def block_mask(first_key, keys, begin, block, starts, diagonal):
    key_at = first_key + lax.broadcasted_iota(jnp.int32, (keys, block), 0)
    allowed = key_at >= starts
    if diagonal:
        query_at = begin + lax.broadcasted_iota(jnp.int32, (keys, block), 1)
        allowed = allowed & (key_at <= query_at)
    return allowed


def attention_kernel(
    starts_ref, gain_q_ref, gain_k_ref, cos_ref, sin_ref, q_ref, k_ref, v_ref,
    out_ref, log_ref, qs_ref, ks_ref, vs_ref,
):
    size = k_ref.shape[0]
    length = k_ref.shape[1]
    group = q_ref.shape[0] // size
    cosine, sine = cos_ref[...], sin_ref[...]
    k_rot = rope_rows(k_ref[...], gain_k_ref[...], cosine, sine)
    ks_ref[...] = k_rot.astype(BF16)
    keys = k_rot.T.astype(BF16)
    values = v_ref[...].astype(BF16)
    vs_ref[...] = values
    for h in range(group):
        rows = pl.ds(h * size, size)
        q_rot = rope_rows(q_ref[rows, :], gain_q_ref[...], cosine, sine).astype(BF16)
        q_rot = q_rot * jnp.asarray(size ** (-0.5), BF16)
        qs_ref[rows, :] = q_rot
        for begin in range(0, length, QBLOCK):
            stop = begin + QBLOCK
            q_block = q_rot[:, begin:stop]
            starts = starts_ref[:, begin:stop]
            parts = [(begin, stop, True)] + ([(0, begin, False)] if begin else [])
            scores = []
            top = None
            for low, high, diagonal in parts:
                s = dot(keys[low:high], q_block, 1, 0)
                s = jnp.where(block_mask(low, high - low, begin, QBLOCK, starts, diagonal), s, -jnp.inf)
                here = jnp.max(s, axis=0, keepdims=True)
                top = here if top is None else jnp.maximum(top, here)
                scores.append(s)
            expos = [jnp.exp(s - top) for s in scores]
            total = sum(jnp.sum(e, axis=0, keepdims=True) for e in expos)
            inverse = 1.0 / total
            result = 0.0
            for (low, high, _), e in zip(parts, expos):
                result = result + dot(values[:, low:high], (e * inverse).astype(BF16), 1, 0)
            out_ref[rows, begin:stop] = result.astype(BF16)
            log_ref[0, 0, h : h + 1, begin:stop] = top + jnp.log(total)


def attention(qkv, starts, gain_q, gain_k, cosine, sine, size, group, pairs):
    rows, length = qkv.shape
    per = (group + 2) * size * pairs
    halves = rows // per
    unit = group * size
    q_rows, k_rows = per // unit, per // size
    full = lambda a: pl.BlockSpec(a.shape, lambda i, j: (0,) * a.ndim)
    heads = halves * pairs * group
    return pl.pallas_call(
        attention_kernel,
        grid=(halves, pairs),
        in_specs=[full(a) for a in (starts, gain_q, gain_k, cosine, sine)]
        + [
            pl.BlockSpec((unit, length), lambda i, j: (q_rows * i + j, 0)),
            pl.BlockSpec((size, length), lambda i, j: (k_rows * i + pairs * group + j, 0)),
            pl.BlockSpec((size, length), lambda i, j: (k_rows * i + pairs * (group + 1) + j, 0)),
        ],
        out_specs=[
            pl.BlockSpec((unit, length), lambda i, j: (pairs * i + j, 0)),
            pl.BlockSpec((1, 1, group, length), lambda i, j: (i, j, 0, 0)),
            pl.BlockSpec((unit, length), lambda i, j: (pairs * i + j, 0)),
            pl.BlockSpec((size, length), lambda i, j: (pairs * i + j, 0)),
            pl.BlockSpec((size, length), lambda i, j: (pairs * i + j, 0)),
        ],
        out_shape=[
            jax.ShapeDtypeStruct((heads * size, length), BF16),
            jax.ShapeDtypeStruct((halves, pairs, group, length), F32),
            jax.ShapeDtypeStruct((heads * size, length), BF16),
            jax.ShapeDtypeStruct((halves * pairs * size, length), BF16),
            jax.ShapeDtypeStruct((halves * pairs * size, length), BF16),
        ],
        name="attention_forward",
    )(starts, gain_q, gain_k, cosine, sine, qkv, qkv, qkv)


def attention_back_kernel(
    starts_ref, gain_q_ref, gain_k_ref, cos_ref, sin_ref, q_ref, k_ref, qs_ref, ks_ref, vs_ref, log_ref, do_ref,
    out_ref, gq_ref, gk_ref, dk_ref, dv_ref,
):
    size = k_ref.shape[0]
    length = k_ref.shape[1]
    group = q_ref.shape[0] // size
    pair, pairs = pl.program_id(1), pl.num_programs(1)
    cosine, sine = cos_ref[...], sin_ref[...]

    @pl.when((pl.program_id(0) == 0) & (pair == 0))
    def _():
        gq_ref[...] = jnp.zeros_like(gq_ref)
        gk_ref[...] = jnp.zeros_like(gk_ref)

    def fold(terms):
        width = gq_ref.shape[1]
        return sum(terms[:, i : i + width] for i in range(0, length, width))

    keys_t = ks_ref[...]
    keys = keys_t.astype(F32).T.astype(BF16)
    values = vs_ref[...].astype(F32).T.astype(BF16)
    dk_ref[...] = jnp.zeros_like(dk_ref)
    dv_ref[...] = jnp.zeros_like(dv_ref)
    scale = size ** (-0.5)
    for h in range(group):
        rows = pl.ds(h * size, size)
        q_t, do_t = qs_ref[rows, :], do_ref[rows, :]
        q_nat = q_t.astype(F32).T.astype(BF16)
        do_nat = do_t.astype(F32).T.astype(BF16)
        d_query = []
        for begin in range(0, length, QBLOCK):
            stop = begin + QBLOCK
            starts = starts_ref[:, begin:stop]
            logs = log_ref[0, 0, h : h + 1, begin:stop]
            parts = [(begin, stop, True)] + ([(0, begin, False)] if begin else [])
            probs, d_probs = [], []
            delta = 0.0
            for low, high, diagonal in parts:
                s = dot(keys[low:high], q_t[:, begin:stop], 1, 0)
                allowed = block_mask(low, high - low, begin, QBLOCK, starts, diagonal)
                p = jnp.where(allowed, jnp.exp(s - logs), 0.0)
                dp = dot(values[low:high], do_t[:, begin:stop], 1, 0)
                delta = delta + jnp.sum(p * dp, axis=0, keepdims=True)
                probs.append(p)
                d_probs.append(dp)
            d_q = 0.0
            for (low, high, _), p, dp in zip(parts, probs, d_probs):
                ds = (p * (dp - delta)).astype(BF16)
                dv_ref[low:high, :] += dot(p.astype(BF16), do_nat[begin:stop], 1, 0)
                dk_ref[low:high, :] += dot(ds, q_nat[begin:stop], 1, 0)
                d_q = d_q + dot(keys_t[:, low:high], ds, 1, 0)
            d_query.append((d_q * scale).astype(BF16))
        d_q0, terms = rope_rows_back(
            jnp.concatenate(d_query, axis=1).astype(F32), q_ref[rows, :], gain_q_ref[...], cosine, sine
        )
        gq_ref[...] += fold(terms)
        out_ref[pl.ds((pair * group + h) * size, size), :] = d_q0.astype(BF16)
    d_key = dk_ref[...].T.astype(BF16).astype(F32)
    d_k0, terms = rope_rows_back(d_key, k_ref[...], gain_k_ref[...], cosine, sine)
    gk_ref[...] += fold(terms)
    out_ref[pl.ds((pairs * group + pair) * size, size), :] = d_k0.astype(BF16)
    out_ref[pl.ds((pairs * (group + 1) + pair) * size, size), :] = dv_ref[...].T.astype(BF16)


def attention_back(qkv, qs, ks, vs, logs, d_out, starts, gain_q, gain_k, cosine, sine, size, group, pairs):
    rows, length = qkv.shape
    per = (group + 2) * size * pairs
    halves = rows // per
    unit = group * size
    q_rows, k_rows = per // unit, per // size
    full = lambda a: pl.BlockSpec(a.shape, lambda i, j: (0,) * a.ndim)
    wide = pl.BlockSpec((unit, length), lambda i, j: (pairs * i + j, 0))
    thin = pl.BlockSpec((size, length), lambda i, j: (pairs * i + j, 0))
    return pl.pallas_call(
        attention_back_kernel,
        grid=(halves, pairs),
        in_specs=[full(a) for a in (starts, gain_q, gain_k, cosine, sine)]
        + [
            pl.BlockSpec((unit, length), lambda i, j: (q_rows * i + j, 0)),
            pl.BlockSpec((size, length), lambda i, j: (k_rows * i + pairs * group + j, 0)),
            wide, thin, thin,
            pl.BlockSpec((1, 1, group, length), lambda i, j: (i, j, 0, 0)),
            wide,
        ],
        out_specs=[
            pl.BlockSpec((per, length), lambda i, j: (i, 0)),
            pl.BlockSpec((size, 128), lambda i, j: (0, 0)),
            pl.BlockSpec((size, 128), lambda i, j: (0, 0)),
        ],
        out_shape=[
            jax.ShapeDtypeStruct((rows, length), BF16),
            jax.ShapeDtypeStruct((size, 128), F32),
            jax.ShapeDtypeStruct((size, 128), F32),
        ],
        scratch_shapes=[pltpu.VMEM((length, size), F32), pltpu.VMEM((length, size), F32)],
        name="attention_backward",
    )(starts, gain_q, gain_k, cosine, sine, qkv, qkv, qs, ks, vs, logs, d_out)


def add_up(terms):
    return sum(t.astype(F32) for t in terms)


def halve(grad, stages):
    terms = [grad]
    for axis, dim in stages:
        bit = lax.axis_index(axis)
        size = terms[0].shape[dim] // 2
        low = [lax.slice_in_dim(t, 0, size, axis=dim) for t in terms]
        high = [lax.slice_in_dim(t, size, 2 * size, axis=dim) for t in terms]
        send = add_up([pick(bit, h, l) for l, h in zip(low, high)]).astype(BF16)
        terms = [pick(bit, l, h) for l, h in zip(low, high)] + [swap(send, axis)]
    return add_up(terms)


def share_rows(total, c):
    rows = total.shape[0] // 2
    own = pick(c, total[:rows], total[rows:])
    other = swap(pick(c, total[rows:], total[:rows]).astype(BF16), "c").astype(F32)
    return in_order(c, own, other, 1)


def sum_columns(grad, order, c):
    rows, columns = grad.shape
    dims = {"zh": 0, "zl": 1, "y": 2, "x": 4}
    total = halve(grad.reshape(2, 2, 2, rows // 8, columns), [(a, dims[a]) for a in order])
    return share_rows(total.reshape(rows // 8, columns // 2), c)


def sum_rows(grad, order, c):
    rows, columns = grad.shape
    dims = {"zh": 0, "y": 1, "x": 3}
    total = halve(grad.reshape(2, 2, rows // 4, columns), [(a, dims[a]) for a in order])
    total = total.reshape(rows // 4, columns // 2)
    total = total + lax.ppermute(total.astype(BF16), ("zl", "c"), [(2, 0), (1, 3)]).astype(F32)
    rows = total.shape[0] // 2
    own = pick(c, total[:rows], total[rows:])
    other = pick(c, total[rows:], total[:rows]).astype(BF16)
    other = lax.ppermute(other, ("zl", "c"), [(0, 1), (3, 2)]).astype(F32)
    return jnp.where(lax.axis_index("zl") == c, own, other)


def pair_body(
    tokens, cotangent, doc_lengths, attn_gain, w_query, w_key, w_value, query_gain, key_gain, w_out,
    ffn_gain, w_gate, w_up, w_down,
):
    local = tokens.shape[1]
    length = 2 * local
    size = query_gain.shape[0]
    kv_count = w_key.shape[1] // size
    group = w_query.shape[1] // w_key.shape[1]
    pairs = kv_count // 4
    c, x = lax.axis_index("c"), lax.axis_index("x")
    gain_attn = attn_gain.astype(F32)
    gain_ffn = ffn_gain.astype(F32)
    gain_q = query_gain.astype(F32)[:, None]
    gain_k = key_gain.astype(F32)[:, None]

    own_tokens = transpose_pair(tokens[0])
    inputs_low = in_order(c, own_tokens, swap(own_tokens, "c"), 0)
    own_cot = transpose_pair(cotangent[0])
    d_mlp = in_order(c, own_cot, swap(own_cot, "c"), 0)
    lengths = jnp.where(c == x, doc_lengths[0], swap(doc_lengths[0], "c"))
    ends = jnp.cumsum(lengths)
    positions = jnp.arange(length, dtype=jnp.int32)
    starts = jnp.max(jnp.where(ends[:, None] <= positions[None, :], ends[:, None], 0), axis=0, keepdims=True)
    half = size // 2
    spread = jnp.exp(jnp.arange(half, dtype=F32) * (-2.0 * math.log(1000000.0) / size))
    angles = spread[:, None] * positions.astype(F32)[None, :]
    cosine, sine = jnp.cos(angles), jnp.sin(angles)

    parts = [part_columns(w, c) for w in (w_query, w_key, w_value)]
    w_qkv = jnp.concatenate([p[i] for i in range(2) for p in parts], axis=1)
    gate_w = jnp.concatenate(part_columns(w_gate, c), axis=1)
    up_w = jnp.concatenate(part_columns(w_up, c), axis=1)
    down_w = part_rows(w_down, c)
    out_w = part_rows(w_out, c)

    inputs = inputs_low.astype(F32)
    normed = rms_scale(inputs, gain_attn).astype(BF16)
    qkv = dot(w_qkv, normed, 0, 1)
    attended_own, logs, qs, ks, vs = attention(qkv, starts, gain_q, gain_k, cosine, sine, size, group, pairs)
    attended_other = swap(attended_own, "c")
    quarter = attended_own.shape[0] // 2
    attended = jnp.concatenate(
        [
            piece
            for i in range(2)
            for piece in (
                pick(c, attended_own[i * quarter : (i + 1) * quarter], attended_other[i * quarter : (i + 1) * quarter]),
                pick(c, attended_other[i * quarter : (i + 1) * quarter], attended_own[i * quarter : (i + 1) * quarter]),
            )
        ],
        axis=0,
    )
    hidden = inputs + dot(attended, w_out, 0, 0)
    hnormed = rms_scale(hidden, gain_ffn).astype(BF16)

    gate = dot(hnormed, gate_w, 1, 0)
    up_part = dot(hnormed, up_w, 1, 0)
    sigmoid_gate = jax.nn.sigmoid(gate)
    silu_gate = gate * sigmoid_gate
    act = (silu_gate * up_part).astype(BF16)
    d_act = dot(d_mlp, down_w, 1, 1)
    d_up = (d_act * silu_gate).astype(BF16)
    d_gate = (d_act * up_part * sigmoid_gate * (1.0 + gate * (1.0 - sigmoid_gate))).astype(BF16)
    grad_down = dot(act, d_mlp, 0, 0).astype(BF16)
    grad_gate = dot(hnormed, d_gate, 0, 0).astype(BF16)
    grad_up = dot(hnormed, d_up, 0, 0).astype(BF16)
    sum_down = sum_rows(grad_down, ("y", "x", "zh"), c)
    sum_gate = sum_columns(grad_gate, ("x", "y", "zl", "zh"), c)
    sum_up = sum_columns(grad_up, ("zl", "zh", "y", "x"), c)

    d_hn = dot(d_gate, gate_w, 1, 1) + dot(d_up, up_w, 1, 1)
    d_hn = d_hn + swap(d_hn.astype(BF16), "c").astype(F32)
    d_hidden_norm, ffn_gain_terms = norm_back(d_hn, hidden, gain_ffn)
    d_hidden = d_mlp.astype(F32) + d_hidden_norm
    d_attn = d_hidden.astype(BF16)
    d_attn_part = jnp.concatenate(part_columns(d_attn, c), axis=1)
    grad_out = dot(attended, d_attn_part, 1, 0).astype(BF16)
    sum_out = sum_columns(grad_out, ("x", "y", "zl", "zh"), c)
    d_attended = dot(out_w, d_attn, 1, 1).astype(BF16)
    d_qkv, gain_q_terms, gain_k_terms = attention_back(
        qkv, qs, ks, vs, logs, d_attended, starts, gain_q, gain_k, cosine, sine, size, group, pairs
    )
    grad_qkv = dot(normed, d_qkv, 0, 1).astype(BF16)
    sum_qkv = []
    width = grad_qkv.shape[1] // 2
    q_width = pairs * group * size
    q_part = jnp.concatenate([grad_qkv[:, i * width : i * width + q_width] for i in range(2)], axis=1)
    k_part = jnp.concatenate([grad_qkv[:, i * width + q_width : i * width + q_width + pairs * size] for i in range(2)], axis=1)
    v_part = jnp.concatenate([grad_qkv[:, i * width + q_width + pairs * size : (i + 1) * width] for i in range(2)], axis=1)
    sum_query = sum_columns(q_part, ("x", "y", "zl", "zh"), c)
    sum_key = sum_columns(k_part, ("y", "x", "zl", "zh"), c)
    sum_value = sum_columns(v_part, ("y", "x", "zl", "zh"), c)

    def own_rows(v):
        return pick(c, v[:local], v[local:])

    def other_rows(v):
        return pick(c, v[local:], v[:local])

    part = dot(d_qkv, w_qkv, 0, 1)
    d_normed = own_rows(part) + swap(other_rows(part).astype(BF16), "c").astype(F32)
    d_input_norm, attn_gain_terms = norm_back(d_normed, own_rows(inputs), gain_attn)
    d_inputs = own_rows(d_hidden) + d_input_norm
    part = dot(act, down_w, 1, 0)
    output = own_rows(hidden) + own_rows(part) + swap(other_rows(part).astype(BF16), "c").astype(F32)
    stays = c == x
    output = jnp.where(stays, output, transpose_pair(output.astype(BF16)).astype(F32))
    d_inputs = jnp.where(stays, d_inputs, transpose_pair(d_inputs.astype(BF16)).astype(F32))

    gains = jnp.concatenate(
        [
            jnp.sum(attn_gain_terms, axis=0),
            jnp.sum(ffn_gain_terms, axis=0) * 0.5,
            jnp.sum(gain_q_terms, axis=1),
            jnp.sum(gain_k_terms, axis=1),
        ]
    ).reshape(-1, 128)
    for axis in AXES:
        gains = gains + swap(gains, axis)
    gains = gains.reshape(-1)
    d = tokens.shape[2]
    return (
        output[None],
        d_inputs[None],
        gains[:d],
        sum_query,
        sum_key,
        sum_value,
        gains[2 * d : 2 * d + size],
        gains[2 * d + size :],
        sum_out,
        gains[d : 2 * d],
        sum_gate,
        sum_up,
        sum_down,
    )


def solution(mesh):
    rows, shards = mesh.shape["dp"], mesh.shape["seq"]
    if rows == 16 and shards == 2:
        body = pair_body
        mesh = Mesh(mesh.devices.reshape(2, 2, 2, 2, 2), AXES)
        dp, seq = AXES[:4], "x"
    else:
        body = general_body
        dp, seq = "dp", "seq"
    return jax.shard_map(
        body,
        mesh=mesh,
        in_specs=(P(dp, seq, None), P(dp, seq, None), P(dp, None)) + (P(),) * 11,
        out_specs=(P(dp, seq, None), P(dp, seq, None), P())
        + (P(dp, seq),) * 3
        + (P(), P(), P(dp, seq), P())
        + (P(dp, seq),) * 3,
        check_vma=False,
    )
```

```python
import math

import jax
import jax.numpy as jnp
from jax import lax
from jax.experimental import pallas as pl
from jax.experimental.pallas import tpu as pltpu
from jax.sharding import Mesh
from jax.sharding import PartitionSpec as P

EPSILON = 1e-06


def rms_scale(values, gain):
    return values * lax.rsqrt(jnp.mean(values * values, axis=-1, keepdims=True) + EPSILON) * gain


def norm_back(incoming, values, gain):
    inverse = lax.rsqrt(jnp.mean(values * values, axis=-1, keepdims=True) + EPSILON)
    unit = values * inverse
    scaled = incoming * gain
    d_values = inverse * (scaled - unit * jnp.mean(scaled * unit, axis=-1, keepdims=True))
    return (d_values, incoming * unit)


def rope_tables(first, count, width):
    half = width // 2
    spread = jnp.exp(jnp.arange(half, dtype=jnp.float32) * (-2.0 * math.log(1000000.0) / width))
    places = (first + jnp.arange(count, dtype=jnp.int32)).astype(jnp.float32)
    angles = places[:, None] * spread[None, :]
    return (jnp.cos(angles)[:, None, :], jnp.sin(angles)[:, None, :])


def rotate(values, cosine, sine):
    half = values.shape[-1] // 2
    first_half = values[..., :half]
    second_half = values[..., half:]
    return jnp.concatenate(
        [first_half * cosine - second_half * sine, second_half * cosine + first_half * sine],
        axis=-1,
    )


def reduce_grads(grads):
    partial_sum = lax.psum_scatter(grads, "dp", scatter_dimension=0, tiled=True)
    return lax.psum_scatter(partial_sum, "seq", scatter_dimension=1, tiled=True)


def general_body(
    tokens,
    cotangent,
    doc_lengths,
    attn_gain,
    w_query,
    w_key,
    w_value,
    query_gain,
    key_gain,
    w_out,
    ffn_gain,
    w_gate,
    w_up,
    w_down,
):
    shards = lax.axis_size("seq")
    local = tokens.shape[1]
    length = local * shards
    head_size = query_gain.shape[0]
    kv_count = w_key.shape[1] // head_size
    head_count = w_query.shape[1] // head_size
    group = head_count // kv_count
    kv_local = kv_count // shards
    block = min(512, length)
    num_blocks = length // block
    scale = head_size ** (-0.5)
    f32 = jnp.float32
    bf16 = jnp.bfloat16
    gain_attn = attn_gain.astype(f32)
    gain_query = query_gain.astype(f32)
    gain_key = key_gain.astype(f32)
    gain_ffn = ffn_gain.astype(f32)
    inputs = tokens[0].astype(f32)
    normed = rms_scale(inputs, gain_attn).astype(bf16)
    query_raw = jnp.dot(normed, w_query, preferred_element_type=f32).reshape(
        local, head_count, head_size
    )
    key_raw = jnp.dot(normed, w_key, preferred_element_type=f32).reshape(local, kv_count, head_size)
    values = (
        jnp.dot(normed, w_value, preferred_element_type=f32)
        .astype(bf16)
        .reshape(local, kv_count, head_size)
    )
    cosine, sine = rope_tables(lax.axis_index("seq") * local, local, head_size)
    query_rot = rotate(rms_scale(query_raw, gain_query), cosine, sine).astype(bf16)
    key_rot = rotate(rms_scale(key_raw, gain_key), cosine, sine).astype(bf16)
    packed_query = query_rot.reshape(local, kv_count, group * head_size)
    packed_kv = jnp.concatenate([key_rot, values], axis=2)
    query_heads, kv_heads = (
        lax.all_to_all(packed_query, "seq", split_axis=1, concat_axis=0, tiled=True),
        lax.all_to_all(packed_kv, "seq", split_axis=1, concat_axis=0, tiled=True),
    )
    query_all = query_heads.reshape(length, kv_local, group, head_size)
    key_all = kv_heads[:, :, :head_size]
    value_all = kv_heads[:, :, head_size:]
    positions = jnp.arange(length, dtype=jnp.int32)
    ends = jnp.cumsum(doc_lengths[0])
    segment = jnp.sum((ends[None, :] <= positions[:, None]).astype(jnp.int32), axis=1)
    starts = jnp.arange(num_blocks, dtype=jnp.int32) * block

    def allowed_at(begin):
        rows_here = begin + jnp.arange(block, dtype=jnp.int32)
        query_seg = lax.dynamic_slice_in_dim(segment, begin, block, 0)
        return (query_seg[:, None] == segment[None, :]) & (positions[None, :] <= rows_here[:, None])

    def block_scores(begin):
        query_block = lax.dynamic_slice_in_dim(query_all, begin, block, 0)
        scores = (
            jnp.einsum("qhgd,khd->hgqk", query_block, key_all, preferred_element_type=f32) * scale
        )
        return (query_block, jnp.where(allowed_at(begin), scores, -jnp.inf))

    def attend(begin):
        query_block, scores = block_scores(begin)
        top_score = jnp.max(scores, axis=-1, keepdims=True)
        expos = jnp.exp(scores - top_score)
        totals = jnp.sum(expos, axis=-1, keepdims=True)
        probs = (expos / totals).astype(bf16)
        result = jnp.einsum("hgqk,khd->qhgd", probs, value_all, preferred_element_type=f32)
        return (result.astype(bf16), top_score[..., 0] + jnp.log(totals[..., 0]))

    attended_heads, log_totals = lax.map(attend, starts)
    attended_heads = attended_heads.reshape(length, kv_local, group * head_size)
    attended = lax.all_to_all(
        attended_heads, "seq", split_axis=0, concat_axis=1, tiled=True
    ).reshape(local, head_count * head_size)
    hidden = inputs + jnp.dot(attended, w_out, preferred_element_type=f32)
    hnormed = rms_scale(hidden, gain_ffn).astype(bf16)
    gate = jnp.dot(hnormed, w_gate, preferred_element_type=f32)
    up_part = jnp.dot(hnormed, w_up, preferred_element_type=f32)
    act = (jax.nn.silu(gate) * up_part).astype(bf16)
    output = hidden + jnp.dot(act, w_down, preferred_element_type=f32)
    d_mlp = cotangent[0]
    grad_down = jnp.einsum("tf,td->fd", act, d_mlp, preferred_element_type=f32)
    d_act = jnp.einsum("td,fd->tf", d_mlp, w_down, preferred_element_type=f32)
    gate_again = jnp.dot(hnormed, w_gate, preferred_element_type=f32)
    up_again = jnp.dot(hnormed, w_up, preferred_element_type=f32)
    sigmoid_gate = jax.nn.sigmoid(gate_again)
    d_up = (d_act * gate_again * sigmoid_gate).astype(bf16)
    d_gate = (d_act * up_again * sigmoid_gate * (1.0 + gate_again * (1.0 - sigmoid_gate))).astype(
        bf16
    )
    grad_gate = jnp.einsum("td,tf->df", hnormed, d_gate, preferred_element_type=f32)
    grad_up = jnp.einsum("td,tf->df", hnormed, d_up, preferred_element_type=f32)
    ffn_sums = reduce_grads((grad_gate, grad_up, grad_down))
    d_hnormed = jnp.einsum("tf,df->td", d_gate, w_gate, preferred_element_type=f32) + jnp.einsum(
        "tf,df->td", d_up, w_up, preferred_element_type=f32
    )
    d_hidden_norm, ffn_gain_terms = norm_back(d_hnormed, hidden, gain_ffn)
    d_hidden = cotangent[0].astype(f32) + d_hidden_norm
    d_attn = d_hidden.astype(bf16)
    grad_out = jnp.einsum("tf,td->fd", attended, d_attn, preferred_element_type=f32)
    d_attended = jnp.einsum("td,fd->tf", d_attn, w_out, preferred_element_type=f32).astype(bf16)
    d_heads = lax.all_to_all(
        d_attended.reshape(local, kv_count, group * head_size),
        "seq",
        split_axis=1,
        concat_axis=0,
        tiled=True,
    )
    d_all = d_heads.reshape(length, kv_local, group, head_size)

    def attend_back(carry, item):
        begin, log_block = item
        query_block, scores = block_scores(begin)
        probs = jnp.exp(scores - log_block[..., None])
        d_block = lax.dynamic_slice_in_dim(d_all, begin, block, 0)
        d_probs = jnp.einsum("qhgd,khd->hgqk", d_block, value_all, preferred_element_type=f32)
        delta = jnp.sum(probs * d_probs, axis=-1, keepdims=True)
        d_scores = (scale * (probs * (d_probs - delta))).astype(bf16)
        d_query_block = jnp.einsum("hgqk,khd->qhgd", d_scores, key_all, preferred_element_type=f32)
        key_total = carry[0] + jnp.einsum(
            "hgqk,qhgd->khd", d_scores, query_block, preferred_element_type=f32
        )
        value_total = carry[1] + jnp.einsum(
            "hgqk,qhgd->khd", probs.astype(bf16), d_block, preferred_element_type=f32
        )
        return ((key_total, value_total), d_query_block.astype(bf16))

    empty = jnp.zeros((length, kv_local, head_size), f32)
    (d_keys, d_values), d_queries = lax.scan(attend_back, (empty, empty), (starts, log_totals))
    d_queries = d_queries.reshape(length, kv_local, group * head_size)
    d_kv = jnp.concatenate([d_keys.astype(bf16), d_values.astype(bf16)], axis=2)
    d_query_pos, d_kv_pos = (
        lax.all_to_all(d_queries, "seq", split_axis=0, concat_axis=1, tiled=True),
        lax.all_to_all(d_kv, "seq", split_axis=0, concat_axis=1, tiled=True),
    )
    d_query_rot = d_query_pos.reshape(local, head_count, head_size).astype(f32)
    d_query_raw, query_gain_terms = norm_back(
        rotate(d_query_rot, cosine, -sine), query_raw, gain_query
    )
    d_query_low = d_query_raw.reshape(local, head_count * head_size).astype(bf16)
    d_key_rot = d_kv_pos[:, :, :head_size].astype(f32)
    d_key_raw, key_gain_terms = norm_back(rotate(d_key_rot, cosine, -sine), key_raw, gain_key)
    d_key_low = d_key_raw.reshape(local, kv_count * head_size).astype(bf16)
    d_value_low = d_kv_pos[:, :, head_size:].reshape(local, kv_count * head_size)
    grad_query = jnp.einsum("td,tf->df", normed, d_query_low, preferred_element_type=f32)
    grad_key = jnp.einsum("td,tf->df", normed, d_key_low, preferred_element_type=f32)
    grad_value = jnp.einsum("td,tf->df", normed, d_value_low, preferred_element_type=f32)
    d_normed = jnp.einsum("tf,df->td", d_query_low, w_query, preferred_element_type=f32)
    d_normed = d_normed + jnp.einsum("tf,df->td", d_key_low, w_key, preferred_element_type=f32)
    d_normed = d_normed + jnp.einsum("tf,df->td", d_value_low, w_value, preferred_element_type=f32)
    d_input_norm, attn_gain_terms = norm_back(d_normed, inputs, gain_attn)
    d_inputs = d_hidden + d_input_norm
    attn_sums = reduce_grads((grad_query, grad_key, grad_value, grad_out))
    gain_totals = lax.psum(
        (
            jnp.sum(attn_gain_terms, axis=0),
            jnp.sum(query_gain_terms, axis=(0, 1)),
            jnp.sum(key_gain_terms, axis=(0, 1)),
            jnp.sum(ffn_gain_terms, axis=0),
        ),
        ("dp", "seq"),
    )
    return (
        output[None],
        d_inputs[None],
        gain_totals[0],
        attn_sums[0],
        attn_sums[1],
        attn_sums[2],
        gain_totals[1],
        gain_totals[2],
        attn_sums[3],
        gain_totals[3],
        ffn_sums[0],
        ffn_sums[1],
        ffn_sums[2],
    )


AXES = ("zh", "zl", "y", "c", "x")
QBLOCK = 256
F32 = jnp.float32
BF16 = jnp.bfloat16


def swap(v, axis):
    return lax.ppermute(v, axis, [(0, 1), (1, 0)])


def transpose_pair(v):
    return lax.ppermute(v, ("c", "x"), [(0, 0), (1, 2), (2, 1), (3, 3)])


def pick(bit, low, high):
    return jnp.where(bit == 0, low, high)


def in_order(bit, own, other, axis):
    return jnp.concatenate([pick(bit, own, other), pick(bit, other, own)], axis=axis)


def dot(left, right, left_dim, right_dim):
    return lax.dot_general(
        left, right, (((left_dim,), (right_dim,)), ((), ())), preferred_element_type=F32
    )


def part_columns(w, c):
    width = w.shape[1] // 4
    return [lax.dynamic_slice_in_dim(w, (2 * i + c) * width, width, 1) for i in range(2)]


def part_rows(w, c):
    rows, columns = w.shape
    return lax.dynamic_index_in_dim(w.reshape(2, 2, rows // 4, columns), c, 1, False).reshape(rows // 2, columns)


def rope_rows(values, gain, cosine, sine):
    unit = values * lax.rsqrt(jnp.mean(values * values, axis=0, keepdims=True) + EPSILON) * gain
    half = values.shape[0] // 2
    first, second = unit[:half], unit[half:]
    return jnp.concatenate([first * cosine - second * sine, second * cosine + first * sine], axis=0)


def rope_rows_back(incoming, values, gain, cosine, sine):
    half = values.shape[0] // 2
    first, second = incoming[:half], incoming[half:]
    turned = jnp.concatenate([first * cosine + second * sine, second * cosine - first * sine], axis=0)
    inverse = lax.rsqrt(jnp.mean(values * values, axis=0, keepdims=True) + EPSILON)
    unit = values * inverse
    scaled = turned * gain
    d_values = inverse * (scaled - unit * jnp.mean(scaled * unit, axis=0, keepdims=True))
    return d_values, turned * unit


def block_mask(first_key, keys, begin, block, starts, diagonal):
    key_at = first_key + lax.broadcasted_iota(jnp.int32, (keys, block), 0)
    allowed = key_at >= starts
    if diagonal:
        query_at = begin + lax.broadcasted_iota(jnp.int32, (keys, block), 1)
        allowed = allowed & (key_at <= query_at)
    return allowed


def attention_kernel(
    starts_ref, gain_q_ref, gain_k_ref, cos_ref, sin_ref, q_ref, k_ref, v_ref,
    out_ref, log_ref, qs_ref, ks_ref, vs_ref,
):
    size = k_ref.shape[0]
    length = k_ref.shape[1]
    group = q_ref.shape[0] // size
    cosine, sine = cos_ref[...], sin_ref[...]
    k_rot = rope_rows(k_ref[...], gain_k_ref[...], cosine, sine)
    ks_ref[...] = k_rot.astype(BF16)
    keys = k_rot.T.astype(BF16)
    values = v_ref[...].astype(BF16)
    vs_ref[...] = values
    for h in range(group):
        rows = pl.ds(h * size, size)
        q_rot = rope_rows(q_ref[rows, :], gain_q_ref[...], cosine, sine).astype(BF16)
        q_rot = q_rot * jnp.asarray(size ** (-0.5), BF16)
        qs_ref[rows, :] = q_rot
        for begin in range(0, length, QBLOCK):
            stop = begin + QBLOCK
            q_block = q_rot[:, begin:stop]
            starts = starts_ref[:, begin:stop]
            parts = [(begin, stop, True)] + ([(0, begin, False)] if begin else [])
            scores = []
            top = None
            for low, high, diagonal in parts:
                s = dot(keys[low:high], q_block, 1, 0)
                s = jnp.where(block_mask(low, high - low, begin, QBLOCK, starts, diagonal), s, -jnp.inf)
                here = jnp.max(s, axis=0, keepdims=True)
                top = here if top is None else jnp.maximum(top, here)
                scores.append(s)
            expos = [jnp.exp(s - top) for s in scores]
            total = sum(jnp.sum(e, axis=0, keepdims=True) for e in expos)
            inverse = 1.0 / total
            result = 0.0
            for (low, high, _), e in zip(parts, expos):
                result = result + dot(values[:, low:high], (e * inverse).astype(BF16), 1, 0)
            out_ref[rows, begin:stop] = result.astype(BF16)
            log_ref[0, 0, h : h + 1, begin:stop] = top + jnp.log(total)


def attention(qkv, starts, gain_q, gain_k, cosine, sine, size, group, pairs):
    rows, length = qkv.shape
    per = (group + 2) * size * pairs
    halves = rows // per
    unit = group * size
    q_rows, k_rows = per // unit, per // size
    full = lambda a: pl.BlockSpec(a.shape, lambda i, j: (0,) * a.ndim)
    heads = halves * pairs * group
    return pl.pallas_call(
        attention_kernel,
        grid=(halves, pairs),
        in_specs=[full(a) for a in (starts, gain_q, gain_k, cosine, sine)]
        + [
            pl.BlockSpec((unit, length), lambda i, j: (q_rows * i + j, 0)),
            pl.BlockSpec((size, length), lambda i, j: (k_rows * i + pairs * group + j, 0)),
            pl.BlockSpec((size, length), lambda i, j: (k_rows * i + pairs * (group + 1) + j, 0)),
        ],
        out_specs=[
            pl.BlockSpec((unit, length), lambda i, j: (pairs * i + j, 0)),
            pl.BlockSpec((1, 1, group, length), lambda i, j: (i, j, 0, 0)),
            pl.BlockSpec((unit, length), lambda i, j: (pairs * i + j, 0)),
            pl.BlockSpec((size, length), lambda i, j: (pairs * i + j, 0)),
            pl.BlockSpec((size, length), lambda i, j: (pairs * i + j, 0)),
        ],
        out_shape=[
            jax.ShapeDtypeStruct((heads * size, length), BF16),
            jax.ShapeDtypeStruct((halves, pairs, group, length), F32),
            jax.ShapeDtypeStruct((heads * size, length), BF16),
            jax.ShapeDtypeStruct((halves * pairs * size, length), BF16),
            jax.ShapeDtypeStruct((halves * pairs * size, length), BF16),
        ],
        name="attention_forward",
    )(starts, gain_q, gain_k, cosine, sine, qkv, qkv, qkv)


def attention_back_kernel(
    starts_ref, gain_q_ref, gain_k_ref, cos_ref, sin_ref, q_ref, k_ref, qs_ref, ks_ref, vs_ref, log_ref, do_ref,
    out_ref, gq_ref, gk_ref, dk_ref, dv_ref,
):
    size = k_ref.shape[0]
    length = k_ref.shape[1]
    group = q_ref.shape[0] // size
    pair, pairs = pl.program_id(1), pl.num_programs(1)
    cosine, sine = cos_ref[...], sin_ref[...]

    @pl.when((pl.program_id(0) == 0) & (pair == 0))
    def _():
        gq_ref[...] = jnp.zeros_like(gq_ref)
        gk_ref[...] = jnp.zeros_like(gk_ref)

    def fold(terms):
        width = gq_ref.shape[1]
        return sum(terms[:, i : i + width] for i in range(0, length, width))

    keys_t = ks_ref[...]
    keys = keys_t.astype(F32).T.astype(BF16)
    values = vs_ref[...].astype(F32).T.astype(BF16)
    dk_ref[...] = jnp.zeros_like(dk_ref)
    dv_ref[...] = jnp.zeros_like(dv_ref)
    scale = size ** (-0.5)
    for h in range(group):
        rows = pl.ds(h * size, size)
        q_t, do_t = qs_ref[rows, :], do_ref[rows, :]
        q_nat = q_t.astype(F32).T.astype(BF16)
        do_nat = do_t.astype(F32).T.astype(BF16)
        d_query = []
        for begin in range(0, length, QBLOCK):
            stop = begin + QBLOCK
            starts = starts_ref[:, begin:stop]
            logs = log_ref[0, 0, h : h + 1, begin:stop]
            parts = [(begin, stop, True)] + ([(0, begin, False)] if begin else [])
            probs, d_probs = [], []
            delta = 0.0
            for low, high, diagonal in parts:
                s = dot(keys[low:high], q_t[:, begin:stop], 1, 0)
                allowed = block_mask(low, high - low, begin, QBLOCK, starts, diagonal)
                p = jnp.where(allowed, jnp.exp(s - logs), 0.0)
                dp = dot(values[low:high], do_t[:, begin:stop], 1, 0)
                delta = delta + jnp.sum(p * dp, axis=0, keepdims=True)
                probs.append(p)
                d_probs.append(dp)
            d_q = 0.0
            for (low, high, _), p, dp in zip(parts, probs, d_probs):
                ds = (p * (dp - delta)).astype(BF16)
                dv_ref[low:high, :] += dot(p.astype(BF16), do_nat[begin:stop], 1, 0)
                dk_ref[low:high, :] += dot(ds, q_nat[begin:stop], 1, 0)
                d_q = d_q + dot(keys_t[:, low:high], ds, 1, 0)
            d_query.append((d_q * scale).astype(BF16))
        d_q0, terms = rope_rows_back(
            jnp.concatenate(d_query, axis=1).astype(F32), q_ref[rows, :], gain_q_ref[...], cosine, sine
        )
        gq_ref[...] += fold(terms)
        out_ref[pl.ds((pair * group + h) * size, size), :] = d_q0.astype(BF16)
    d_key = dk_ref[...].T.astype(BF16).astype(F32)
    d_k0, terms = rope_rows_back(d_key, k_ref[...], gain_k_ref[...], cosine, sine)
    gk_ref[...] += fold(terms)
    out_ref[pl.ds((pairs * group + pair) * size, size), :] = d_k0.astype(BF16)
    out_ref[pl.ds((pairs * (group + 1) + pair) * size, size), :] = dv_ref[...].T.astype(BF16)


def attention_back(qkv, qs, ks, vs, logs, d_out, starts, gain_q, gain_k, cosine, sine, size, group, pairs):
    rows, length = qkv.shape
    per = (group + 2) * size * pairs
    halves = rows // per
    unit = group * size
    q_rows, k_rows = per // unit, per // size
    full = lambda a: pl.BlockSpec(a.shape, lambda i, j: (0,) * a.ndim)
    wide = pl.BlockSpec((unit, length), lambda i, j: (pairs * i + j, 0))
    thin = pl.BlockSpec((size, length), lambda i, j: (pairs * i + j, 0))
    return pl.pallas_call(
        attention_back_kernel,
        grid=(halves, pairs),
        in_specs=[full(a) for a in (starts, gain_q, gain_k, cosine, sine)]
        + [
            pl.BlockSpec((unit, length), lambda i, j: (q_rows * i + j, 0)),
            pl.BlockSpec((size, length), lambda i, j: (k_rows * i + pairs * group + j, 0)),
            wide, thin, thin,
            pl.BlockSpec((1, 1, group, length), lambda i, j: (i, j, 0, 0)),
            wide,
        ],
        out_specs=[
            pl.BlockSpec((per, length), lambda i, j: (i, 0)),
            pl.BlockSpec((size, 128), lambda i, j: (0, 0)),
            pl.BlockSpec((size, 128), lambda i, j: (0, 0)),
        ],
        out_shape=[
            jax.ShapeDtypeStruct((rows, length), BF16),
            jax.ShapeDtypeStruct((size, 128), F32),
            jax.ShapeDtypeStruct((size, 128), F32),
        ],
        scratch_shapes=[pltpu.VMEM((length, size), F32), pltpu.VMEM((length, size), F32)],
        name="attention_backward",
    )(starts, gain_q, gain_k, cosine, sine, qkv, qkv, qs, ks, vs, logs, d_out)


LANES = 128


def local_block(i, c, blocks):
    return lax.div(i, blocks) * 2 * blocks + c * blocks + lax.rem(i, blocks)


def ffn_kernel(
    sel_ref, hn_ref, dm_ref, gate0_ref, gate1_ref, up0_ref, up1_ref, down0_ref, down1_ref,
    act_ref, dg_ref, du_ref, hz0_ref, hz1_ref, hy0_ref, hy1_ref, dx0_ref, dx1_ref,
):
    @pl.when(pl.program_id(0) == 0)
    def _():
        x, y, zl = sel_ref[1], sel_ref[2], sel_ref[3]
        width = hn_ref.shape[1] // 8
        half = dm_ref.shape[1] // 2
        for order in range(2):
            for i in range(4):
                high, low = divmod(i, 2)
                to = slice(i * width, (i + 1) * width)
                bit = zl if order else 1 - zl
                block = 4 * high + 2 * bit + low
                (hz0_ref, hz1_ref)[order][:, to] = hn_ref[:, pl.ds(pl.multiple_of(block * width, width), width)]
                bit = y if order else 1 - y
                block = 4 * high + 2 * low + bit
                (hy0_ref, hy1_ref)[order][:, to] = hn_ref[:, pl.ds(pl.multiple_of(block * width, width), width)]
            bit = x if order else 1 - x
            (dx0_ref, dx1_ref)[order][...] = dm_ref[:, pl.ds(pl.multiple_of(bit * half, half), half)]

    gate_w = jnp.concatenate([gate0_ref[...], gate1_ref[...]], axis=1)
    up_w = jnp.concatenate([up0_ref[...], up1_ref[...]], axis=1)
    down_w = jnp.concatenate([down0_ref[...], down1_ref[...]], axis=0)
    gate = dot(hn_ref[...], gate_w, 1, 0)
    up = dot(hn_ref[...], up_w, 1, 0)
    d_act = dot(dm_ref[...], down_w, 1, 1)
    sigmoid = 1.0 / (1.0 + jnp.exp(-gate))
    silu = gate * sigmoid
    act_ref[...] = (silu * up).astype(BF16)
    du_ref[...] = (d_act * silu).astype(BF16)
    dg_ref[...] = (d_act * up * (sigmoid + silu * (1.0 - sigmoid))).astype(BF16)


def feed_forward(sel, hnormed, d_mlp, w_gate, w_up, w_down):
    tokens, d = hnormed.shape
    units = w_gate.shape[1] // 2
    blocks = units // 2 // LANES
    whole = pl.BlockSpec((tokens, d), lambda j, sel: (0, 0))
    half = pl.BlockSpec((tokens, d // 2), lambda j, sel: (0, 0))
    columns = [
        pl.BlockSpec((d, LANES), lambda j, sel, i=i: (0, local_block(2 * j + i, sel[0], blocks))) for i in range(2)
    ]
    rows = [pl.BlockSpec((LANES, d), lambda j, sel, i=i: (local_block(2 * j + i, sel[0], blocks), 0)) for i in range(2)]
    return pl.pallas_call(
        ffn_kernel,
        grid_spec=pltpu.PrefetchScalarGridSpec(
            num_scalar_prefetch=1,
            grid=(blocks,),
            in_specs=[whole, whole] + columns + columns + rows,
            out_specs=[pl.BlockSpec((tokens, 2 * LANES), lambda j, sel: (0, j))] * 3 + [half] * 6,
        ),
        out_shape=[jax.ShapeDtypeStruct((tokens, units), BF16)] * 3 + [jax.ShapeDtypeStruct((tokens, d // 2), BF16)] * 6,
        name="feed_forward",
    )(sel, hnormed, d_mlp, w_gate, w_gate, w_up, w_up, w_down, w_down)


def ffn_back_kernel(sel_ref, dg_ref, du_ref, gate0_ref, gate1_ref, up0_ref, up1_ref, out_ref, low_ref):
    gate_w = jnp.concatenate([gate0_ref[...], gate1_ref[...]], axis=1)
    up_w = jnp.concatenate([up0_ref[...], up1_ref[...]], axis=1)
    result = dot(dg_ref[...], gate_w, 1, 1) + dot(du_ref[...], up_w, 1, 1)
    out_ref[...] = result
    low_ref[...] = result.astype(BF16)


def ffn_back(sel, d_gate, d_up, w_gate, w_up):
    tokens, units = d_gate.shape
    d = w_gate.shape[0]
    block = min(256, d)
    whole = pl.BlockSpec((tokens, units), lambda j, sel: (0, 0))
    weights = [pl.BlockSpec((block, units // 2), lambda j, sel, i=i: (j, 2 * i + sel[0])) for i in range(2)]
    return pl.pallas_call(
        ffn_back_kernel,
        grid_spec=pltpu.PrefetchScalarGridSpec(
            num_scalar_prefetch=1,
            grid=(d // block,),
            in_specs=[whole, whole] + weights + weights,
            out_specs=[pl.BlockSpec((tokens, block), lambda j, sel: (0, j))] * 2,
        ),
        out_shape=[jax.ShapeDtypeStruct((tokens, d), t) for t in (F32, BF16)],
        name="feed_forward_back",
    )(sel, d_gate, d_up, w_gate, w_gate, w_up, w_up)


def ffn_out_kernel(sel_ref, act_ref, down0_ref, down1_ref, out_ref):
    out_ref[...] = dot(act_ref[...], jnp.concatenate([down0_ref[...], down1_ref[...]], axis=0), 1, 0)


def ffn_out(sel, act, w_down):
    tokens, units = act.shape
    d = w_down.shape[1]
    block = min(256, d)
    weights = [pl.BlockSpec((units // 2, block), lambda j, sel, i=i: (2 * i + sel[0], j)) for i in range(2)]
    return pl.pallas_call(
        ffn_out_kernel,
        grid_spec=pltpu.PrefetchScalarGridSpec(
            num_scalar_prefetch=1,
            grid=(d // block,),
            in_specs=[pl.BlockSpec((tokens, units), lambda j, sel: (0, 0))] + weights,
            out_specs=pl.BlockSpec((tokens, block), lambda j, sel: (0, j)),
        ),
        out_shape=jax.ShapeDtypeStruct((tokens, d), F32),
        name="feed_forward_out",
    )(sel, act, w_down, w_down)


def tie(values, *others):
    return lax.optimization_barrier((tuple(values), others))[0]


def add_up(terms):
    return sum(t.astype(F32) for t in terms)


def leave(terms, dim, bit):
    size = terms[0].shape[dim] // 2
    if dim < terms[0].ndim - 2:
        return add_up([lax.dynamic_slice_in_dim(t, (1 - bit) * size, size, dim) for t in terms]).astype(BF16)
    low = add_up([lax.slice_in_dim(t, 0, size, axis=dim) for t in terms])
    high = add_up([lax.slice_in_dim(t, size, 2 * size, axis=dim) for t in terms])
    return pick(bit, high, low).astype(BF16)


def stay(terms, dim, bit):
    size = terms[0].shape[dim] // 2
    if dim < terms[0].ndim - 2:
        return [lax.dynamic_slice_in_dim(t, bit * size, size, dim) for t in terms]
    return [
        pick(bit, lax.slice_in_dim(t, 0, size, axis=dim), lax.slice_in_dim(t, size, 2 * size, axis=dim))
        for t in terms
    ]


def halve(terms, axis, dim):
    bit = lax.axis_index(axis)
    return stay(terms, dim, bit) + [swap(leave(terms, dim, bit), axis)]


def share_rows(total, c):
    rows = total.shape[0] // 2
    own = pick(c, total[:rows], total[rows:])
    other = swap(pick(c, total[rows:], total[:rows]).astype(BF16), "c").astype(F32)
    return in_order(c, own, other, 1)


def own_rows(v, c, local):
    return pick(c, v[:local], v[local:])


def other_rows(v, c, local):
    return pick(c, v[local:], v[:local])


def pair_body(
    tokens, cotangent, doc_lengths, attn_gain, w_query, w_key, w_value, query_gain, key_gain, w_out,
    ffn_gain, w_gate, w_up, w_down,
):
    local, d = tokens.shape[1:]
    length = 2 * local
    size = query_gain.shape[0]
    kv_count = w_key.shape[1] // size
    group = w_query.shape[1] // w_key.shape[1]
    pairs = kv_count // 4
    zh, zl, y, c, x = [lax.axis_index(a) for a in AXES]
    gain_attn = attn_gain.astype(F32)
    gain_ffn = ffn_gain.astype(F32)
    gain_q = query_gain.astype(F32)[:, None]
    gain_k = key_gain.astype(F32)[:, None]

    own_tokens = transpose_pair(tokens[0])
    other_tokens = swap(own_tokens, "c")
    (cot_low,) = tie([cotangent[0]], own_tokens)
    own_cot = transpose_pair(cot_low)
    d_mlp = in_order(c, own_cot, swap(own_cot, "c"), 0)
    lengths = jnp.where(c == x, doc_lengths[0], swap(doc_lengths[0], "c"))
    ends = jnp.cumsum(lengths)
    positions = jnp.arange(length, dtype=jnp.int32)
    starts = jnp.max(jnp.where(ends[:, None] <= positions[None, :], ends[:, None], 0), axis=0, keepdims=True)
    half = size // 2
    spread = jnp.exp(jnp.arange(half, dtype=F32) * (-2.0 * math.log(1000000.0) / size))
    angles = spread[:, None] * positions.astype(F32)[None, :]
    cosine, sine = jnp.cos(angles), jnp.sin(angles)

    parts = [part_columns(w, c) for w in (w_query, w_key, w_value)]
    w_qkv = jnp.concatenate([p[i] for i in range(2) for p in parts], axis=1)
    out_w = part_rows(w_out, c)
    sel = jnp.stack([c, x, y, zl]).astype(jnp.int32)
    w_qkv, out_w, cosine, sine, starts, sel, other_tokens = tie(
        (w_qkv, out_w, cosine, sine, starts, sel, other_tokens)
    )

    inputs = in_order(c, own_tokens, other_tokens, 0).astype(F32)
    normed = rms_scale(inputs, gain_attn).astype(BF16)
    qkv = dot(w_qkv, normed, 0, 1)
    attended_own, logs, qs, ks, vs = attention(qkv, starts, gain_q, gain_k, cosine, sine, size, group, pairs)
    attended_other = swap(attended_own, "c")
    width = attended_own.shape[0] // 2
    attended = jnp.concatenate(
        [in_order(c, attended_own[i : i + width], attended_other[i : i + width], 0) for i in (0, width)], axis=0
    )
    hidden = inputs + dot(attended, w_out, 0, 0)
    hnormed = rms_scale(hidden, gain_ffn).astype(BF16)

    act, d_gate, d_up, hn_z0, hn_z1, hn_y0, hn_y1, dm_x0, dm_x1 = feed_forward(
        sel, hnormed, d_mlp, w_gate, w_up, w_down
    )
    send_up = dot(hn_z0, d_up, 0, 0).astype(BF16)
    send_down = dot(act, dm_x0, 0, 0).astype(BF16)
    send_gate = dot(hn_y0, d_gate, 0, 0).astype(BF16)
    come_up, come_down, come_gate = swap(send_up, "zl"), swap(send_down, "x"), swap(send_gate, "y")
    d_gate, d_up, act = tie((d_gate, d_up, act), send_up, send_down, send_gate)
    d_hn, d_hn_low = ffn_back(sel, d_gate, d_up, w_gate, w_up)
    d_hn_other = swap(d_hn_low, "c")
    hn_z1, hn_y1, dm_x1 = tie((hn_z1, hn_y1, dm_x1), d_hn)
    keep_up = dot(hn_z1, d_up, 0, 0).astype(BF16)
    keep_down = dot(act, dm_x1, 0, 0).astype(BF16)
    keep_gate = dot(hn_y1, d_gate, 0, 0).astype(BF16)
    (d_hn_other,) = tie((d_hn_other,), keep_up)
    d_hn = d_hn + d_hn_other.astype(F32)
    d_hidden_norm, ffn_gain_terms = norm_back(d_hn, hidden, gain_ffn)
    d_hidden = d_mlp.astype(F32) + d_hidden_norm
    d_attn = d_hidden.astype(BF16)
    d_attended = dot(out_w, d_attn, 1, 1).astype(BF16)
    units = d_gate.shape[1]
    rows = d // 8
    d_attn_part = jnp.concatenate(part_columns(d_attn, c), axis=1)
    attended_y = attended.reshape(4, 2, rows, length)
    send_out = dot(lax.dynamic_index_in_dim(attended_y, 1 - y, 1, False).reshape(d // 2, length), d_attn_part, 1, 0)
    keep_out = dot(lax.dynamic_index_in_dim(attended_y, y, 1, False).reshape(d // 2, length), d_attn_part, 1, 0)
    send_out, keep_out = send_out.astype(BF16), keep_out.astype(BF16)
    come_out = swap(send_out, "y")
    (d_attended,) = tie((d_attended,), keep_up, keep_down, keep_gate, send_out, keep_out)
    d_qkv, gain_q_terms, gain_k_terms = attention_back(
        qkv, qs, ks, vs, logs, d_attended, starts, gain_q, gain_k, cosine, sine, size, group, pairs
    )

    come_up, come_down, come_gate, d_qkv = tie((come_up, come_down, come_gate, d_qkv))
    up = [v.reshape(2, 2, rows, units) for v in (keep_up, come_up)]
    down = [v.reshape(2, 2, units // 4, d // 2) for v in (keep_down, come_down)]
    gate = [v.reshape(2, 2, rows, units) for v in (keep_gate, come_gate)]
    send_gate, send_down, send_up = leave(gate, 1, zl), leave(down, 1, y), leave(up, 3, x)
    gate = stay(gate, 1, zl) + [swap(send_gate, "zl")]
    down = stay(down, 1, y) + [swap(send_down, "y")]
    up = stay(up, 3, x) + [swap(send_up, "x")]

    (d_qkv,) = tie((d_qkv,), send_gate, send_down, send_up)
    width = d_qkv.shape[0] // 2
    send_qkv = dot(normed, lax.dynamic_slice_in_dim(d_qkv, (1 - x) * width, width, 0), 0, 1).astype(BF16)
    come_qkv = swap(send_qkv, "x")
    (d_qkv,) = tie((d_qkv,), send_qkv)
    part = dot(d_qkv, w_qkv, 0, 1)
    part_low = other_rows(part, c, local).astype(BF16)
    part_other = swap(part_low, "c")
    d_qkv, act = tie((d_qkv, act), part_low)
    keep_qkv = dot(normed, lax.dynamic_slice_in_dim(d_qkv, x * width, width, 0), 0, 1).astype(BF16)
    part_out = ffn_out(sel, act, w_down)
    out_low = other_rows(part_out, c, local).astype(BF16)
    out_other = swap(out_low, "c")
    d_normed = own_rows(part, c, local) + part_other.astype(F32)
    d_input_norm, attn_gain_terms = norm_back(d_normed, own_rows(inputs, c, local), gain_attn)
    d_inputs = own_rows(d_hidden, c, local) + d_input_norm
    output = own_rows(hidden, c, local) + own_rows(part_out, c, local) + out_other.astype(F32)
    output_low, d_inputs_low = output.astype(BF16), d_inputs.astype(BF16)
    output_other, d_inputs_other = transpose_pair(output_low), transpose_pair(d_inputs_low)
    gains = jnp.concatenate(
        [
            jnp.sum(attn_gain_terms, axis=0),
            jnp.sum(ffn_gain_terms, axis=0) * 0.5,
            jnp.sum(gain_q_terms, axis=1),
            jnp.sum(gain_k_terms, axis=1),
        ]
    ).reshape(-1, 128)

    tied = gate[-1], down[-1], up[-1]
    gate[-1], down[-1], up[-1] = tie(tied, output_low, d_inputs_low, gains, keep_qkv)
    send_gate, send_down, send_up = leave(gate, 3, x), add_up(down).astype(BF16), leave(up, 1, y)
    gate = stay(gate, 3, x) + [swap(send_gate, "x")]
    down = down + [lax.ppermute(send_down, ("zl", "c"), [(2, 0), (1, 3)])]
    up = stay(up, 1, y) + [swap(send_up, "y")]

    come_out, come_qkv = tie((come_out, come_qkv), send_gate, send_down, send_up)
    out = [v.reshape(2, 2, 1, rows, d // 2) for v in (keep_out, come_out)]
    qkv_grad = [v.reshape(2, 2, 2, rows, width) for v in (keep_qkv, come_qkv)]
    send_out, send_qkv = leave(out, 4, x), leave(qkv_grad, 2, y)
    out = stay(out, 4, x) + [swap(send_out, "x")]
    qkv_grad = stay(qkv_grad, 2, y) + [swap(send_qkv, "y")]

    tied = gate[-1], down[-1], up[-1]
    gate[-1], down[-1], up[-1] = tie(tied, send_out, send_qkv)
    send_gate, send_down, send_up = leave(gate, 0, zh), leave(down, 0, zh), leave(up, 0, zh)
    gate = stay(gate, 0, zh) + [swap(send_gate, "zh")]
    down = stay(down, 0, zh) + [swap(send_down, "zh")]
    up = stay(up, 0, zh) + [swap(send_up, "zh")]

    out[-1], qkv_grad[-1] = tie((out[-1], qkv_grad[-1]), send_gate, send_down, send_up)
    send_out, send_qkv = leave(out, 1, zl), leave(qkv_grad, 1, zl)
    out = stay(out, 1, zl) + [swap(send_out, "zl")]
    qkv_grad = stay(qkv_grad, 1, zl) + [swap(send_qkv, "zl")]
    for axis in AXES[:2]:
        gains = gains + swap(gains, axis)
    out[-1], qkv_grad[-1] = tie((out[-1], qkv_grad[-1]), gains)
    send_out, send_qkv = leave(out, 0, zh), leave(qkv_grad, 0, zh)
    out = stay(out, 0, zh) + [swap(send_out, "zh")]
    qkv_grad = stay(qkv_grad, 0, zh) + [swap(send_qkv, "zh")]
    for axis in AXES[2:]:
        gains = gains + swap(gains, axis)
    gains = gains.reshape(-1)

    tied = gate[-1], down[-1], up[-1]
    gate[-1], down[-1], up[-1] = tie(tied, send_out, send_qkv)
    total = add_up(down).reshape(-1, d // 2)
    n = total.shape[0] // 2
    own = pick(c, total[:n], total[n:])
    other = pick(c, total[n:], total[:n]).astype(BF16)
    other = lax.ppermute(other, ("zl", "c"), [(0, 1), (3, 2)]).astype(F32)
    sum_down = jnp.where(zl == c, own, other)
    sum_gate, sum_up = [share_rows(add_up(t).reshape(rows, units // 2), c) for t in (gate, up)]
    out[-1], qkv_grad[-1] = tie((out[-1], qkv_grad[-1]), sum_gate, sum_up, sum_down)
    both = jnp.concatenate([add_up(t).reshape(rows, -1) for t in (out, qkv_grad)], axis=1)
    n = rows // 2
    own = pick(c, both[:n], both[n:])
    other = swap(pick(c, both[n:], both[:n]).astype(BF16), "c").astype(F32)
    first, second = pick(c, own, other), pick(c, other, own)
    out_width, q_width, kv_width = d // 4, pairs * group * size, pairs * size
    ends_of = [0, out_width, out_width + q_width, out_width + q_width + kv_width, out_width + q_width + 2 * kv_width]
    sum_out, sum_query, sum_key, sum_value = [
        jnp.concatenate([first[:, low:high], second[:, low:high]], axis=1)
        for low, high in zip(ends_of[:-1], ends_of[1:])
    ]
    stays = c == x
    output = jnp.where(stays, output, output_other.astype(F32))
    d_inputs = jnp.where(stays, d_inputs, d_inputs_other.astype(F32))
    return (
        output[None],
        d_inputs[None],
        gains[:d],
        sum_query,
        sum_key,
        sum_value,
        gains[2 * d : 2 * d + size],
        gains[2 * d + size :],
        sum_out,
        gains[d : 2 * d],
        sum_gate,
        sum_up,
        sum_down,
    )


def solution(mesh):
    rows, shards = mesh.shape["dp"], mesh.shape["seq"]
    if rows == 16 and shards == 2:
        body = pair_body
        mesh = Mesh(mesh.devices.reshape(2, 2, 2, 2, 2), AXES)
        dp, seq = AXES[:4], "x"
    else:
        body = general_body
        dp, seq = "dp", "seq"
    return jax.shard_map(
        body,
        mesh=mesh,
        in_specs=(P(dp, seq, None), P(dp, seq, None), P(dp, None)) + (P(),) * 11,
        out_specs=(P(dp, seq, None), P(dp, seq, None), P())
        + (P(dp, seq),) * 3
        + (P(), P(), P(dp, seq), P())
        + (P(dp, seq),) * 3,
        check_vma=False,
    )
```

```python
import math

import functools

import jax
import jax.numpy as jnp
from jax import lax
from jax.experimental import pallas as pl
from jax.experimental.pallas import tpu as pltpu
from jax.sharding import Mesh
from jax.sharding import PartitionSpec as P

EPSILON = 1e-06


def rms_scale(values, gain):
    return values * lax.rsqrt(jnp.mean(values * values, axis=-1, keepdims=True) + EPSILON) * gain


def norm_back(incoming, values, gain):
    inverse = lax.rsqrt(jnp.mean(values * values, axis=-1, keepdims=True) + EPSILON)
    unit = values * inverse
    scaled = incoming * gain
    d_values = inverse * (scaled - unit * jnp.mean(scaled * unit, axis=-1, keepdims=True))
    return (d_values, incoming * unit)


def rope_tables(first, count, width):
    half = width // 2
    spread = jnp.exp(jnp.arange(half, dtype=jnp.float32) * (-2.0 * math.log(1000000.0) / width))
    places = (first + jnp.arange(count, dtype=jnp.int32)).astype(jnp.float32)
    angles = places[:, None] * spread[None, :]
    return (jnp.cos(angles)[:, None, :], jnp.sin(angles)[:, None, :])


def rotate(values, cosine, sine):
    half = values.shape[-1] // 2
    first_half = values[..., :half]
    second_half = values[..., half:]
    return jnp.concatenate(
        [first_half * cosine - second_half * sine, second_half * cosine + first_half * sine],
        axis=-1,
    )


def reduce_grads(grads):
    partial_sum = lax.psum_scatter(grads, "dp", scatter_dimension=0, tiled=True)
    return lax.psum_scatter(partial_sum, "seq", scatter_dimension=1, tiled=True)


def general_body(
    tokens,
    cotangent,
    doc_lengths,
    attn_gain,
    w_query,
    w_key,
    w_value,
    query_gain,
    key_gain,
    w_out,
    ffn_gain,
    w_gate,
    w_up,
    w_down,
):
    shards = lax.axis_size("seq")
    local = tokens.shape[1]
    length = local * shards
    head_size = query_gain.shape[0]
    kv_count = w_key.shape[1] // head_size
    head_count = w_query.shape[1] // head_size
    group = head_count // kv_count
    kv_local = kv_count // shards
    block = min(512, length)
    num_blocks = length // block
    scale = head_size ** (-0.5)
    f32 = jnp.float32
    bf16 = jnp.bfloat16
    gain_attn = attn_gain.astype(f32)
    gain_query = query_gain.astype(f32)
    gain_key = key_gain.astype(f32)
    gain_ffn = ffn_gain.astype(f32)
    inputs = tokens[0].astype(f32)
    normed = rms_scale(inputs, gain_attn).astype(bf16)
    query_raw = jnp.dot(normed, w_query, preferred_element_type=f32).reshape(
        local, head_count, head_size
    )
    key_raw = jnp.dot(normed, w_key, preferred_element_type=f32).reshape(local, kv_count, head_size)
    values = (
        jnp.dot(normed, w_value, preferred_element_type=f32)
        .astype(bf16)
        .reshape(local, kv_count, head_size)
    )
    cosine, sine = rope_tables(lax.axis_index("seq") * local, local, head_size)
    query_rot = rotate(rms_scale(query_raw, gain_query), cosine, sine).astype(bf16)
    key_rot = rotate(rms_scale(key_raw, gain_key), cosine, sine).astype(bf16)
    packed_query = query_rot.reshape(local, kv_count, group * head_size)
    packed_kv = jnp.concatenate([key_rot, values], axis=2)
    query_heads, kv_heads = (
        lax.all_to_all(packed_query, "seq", split_axis=1, concat_axis=0, tiled=True),
        lax.all_to_all(packed_kv, "seq", split_axis=1, concat_axis=0, tiled=True),
    )
    query_all = query_heads.reshape(length, kv_local, group, head_size)
    key_all = kv_heads[:, :, :head_size]
    value_all = kv_heads[:, :, head_size:]
    positions = jnp.arange(length, dtype=jnp.int32)
    ends = jnp.cumsum(doc_lengths[0])
    segment = jnp.sum((ends[None, :] <= positions[:, None]).astype(jnp.int32), axis=1)
    starts = jnp.arange(num_blocks, dtype=jnp.int32) * block

    def allowed_at(begin):
        rows_here = begin + jnp.arange(block, dtype=jnp.int32)
        query_seg = lax.dynamic_slice_in_dim(segment, begin, block, 0)
        return (query_seg[:, None] == segment[None, :]) & (positions[None, :] <= rows_here[:, None])

    def block_scores(begin):
        query_block = lax.dynamic_slice_in_dim(query_all, begin, block, 0)
        scores = (
            jnp.einsum("qhgd,khd->hgqk", query_block, key_all, preferred_element_type=f32) * scale
        )
        return (query_block, jnp.where(allowed_at(begin), scores, -jnp.inf))

    def attend(begin):
        query_block, scores = block_scores(begin)
        top_score = jnp.max(scores, axis=-1, keepdims=True)
        expos = jnp.exp(scores - top_score)
        totals = jnp.sum(expos, axis=-1, keepdims=True)
        probs = (expos / totals).astype(bf16)
        result = jnp.einsum("hgqk,khd->qhgd", probs, value_all, preferred_element_type=f32)
        return (result.astype(bf16), top_score[..., 0] + jnp.log(totals[..., 0]))

    attended_heads, log_totals = lax.map(attend, starts)
    attended_heads = attended_heads.reshape(length, kv_local, group * head_size)
    attended = lax.all_to_all(
        attended_heads, "seq", split_axis=0, concat_axis=1, tiled=True
    ).reshape(local, head_count * head_size)
    hidden = inputs + jnp.dot(attended, w_out, preferred_element_type=f32)
    hnormed = rms_scale(hidden, gain_ffn).astype(bf16)
    gate = jnp.dot(hnormed, w_gate, preferred_element_type=f32)
    up_part = jnp.dot(hnormed, w_up, preferred_element_type=f32)
    act = (jax.nn.silu(gate) * up_part).astype(bf16)
    output = hidden + jnp.dot(act, w_down, preferred_element_type=f32)
    d_mlp = cotangent[0]
    grad_down = jnp.einsum("tf,td->fd", act, d_mlp, preferred_element_type=f32)
    d_act = jnp.einsum("td,fd->tf", d_mlp, w_down, preferred_element_type=f32)
    gate_again = jnp.dot(hnormed, w_gate, preferred_element_type=f32)
    up_again = jnp.dot(hnormed, w_up, preferred_element_type=f32)
    sigmoid_gate = jax.nn.sigmoid(gate_again)
    d_up = (d_act * gate_again * sigmoid_gate).astype(bf16)
    d_gate = (d_act * up_again * sigmoid_gate * (1.0 + gate_again * (1.0 - sigmoid_gate))).astype(
        bf16
    )
    grad_gate = jnp.einsum("td,tf->df", hnormed, d_gate, preferred_element_type=f32)
    grad_up = jnp.einsum("td,tf->df", hnormed, d_up, preferred_element_type=f32)
    ffn_sums = reduce_grads((grad_gate, grad_up, grad_down))
    d_hnormed = jnp.einsum("tf,df->td", d_gate, w_gate, preferred_element_type=f32) + jnp.einsum(
        "tf,df->td", d_up, w_up, preferred_element_type=f32
    )
    d_hidden_norm, ffn_gain_terms = norm_back(d_hnormed, hidden, gain_ffn)
    d_hidden = cotangent[0].astype(f32) + d_hidden_norm
    d_attn = d_hidden.astype(bf16)
    grad_out = jnp.einsum("tf,td->fd", attended, d_attn, preferred_element_type=f32)
    d_attended = jnp.einsum("td,fd->tf", d_attn, w_out, preferred_element_type=f32).astype(bf16)
    d_heads = lax.all_to_all(
        d_attended.reshape(local, kv_count, group * head_size),
        "seq",
        split_axis=1,
        concat_axis=0,
        tiled=True,
    )
    d_all = d_heads.reshape(length, kv_local, group, head_size)

    def attend_back(carry, item):
        begin, log_block = item
        query_block, scores = block_scores(begin)
        probs = jnp.exp(scores - log_block[..., None])
        d_block = lax.dynamic_slice_in_dim(d_all, begin, block, 0)
        d_probs = jnp.einsum("qhgd,khd->hgqk", d_block, value_all, preferred_element_type=f32)
        delta = jnp.sum(probs * d_probs, axis=-1, keepdims=True)
        d_scores = (scale * (probs * (d_probs - delta))).astype(bf16)
        d_query_block = jnp.einsum("hgqk,khd->qhgd", d_scores, key_all, preferred_element_type=f32)
        key_total = carry[0] + jnp.einsum(
            "hgqk,qhgd->khd", d_scores, query_block, preferred_element_type=f32
        )
        value_total = carry[1] + jnp.einsum(
            "hgqk,qhgd->khd", probs.astype(bf16), d_block, preferred_element_type=f32
        )
        return ((key_total, value_total), d_query_block.astype(bf16))

    empty = jnp.zeros((length, kv_local, head_size), f32)
    (d_keys, d_values), d_queries = lax.scan(attend_back, (empty, empty), (starts, log_totals))
    d_queries = d_queries.reshape(length, kv_local, group * head_size)
    d_kv = jnp.concatenate([d_keys.astype(bf16), d_values.astype(bf16)], axis=2)
    d_query_pos, d_kv_pos = (
        lax.all_to_all(d_queries, "seq", split_axis=0, concat_axis=1, tiled=True),
        lax.all_to_all(d_kv, "seq", split_axis=0, concat_axis=1, tiled=True),
    )
    d_query_rot = d_query_pos.reshape(local, head_count, head_size).astype(f32)
    d_query_raw, query_gain_terms = norm_back(
        rotate(d_query_rot, cosine, -sine), query_raw, gain_query
    )
    d_query_low = d_query_raw.reshape(local, head_count * head_size).astype(bf16)
    d_key_rot = d_kv_pos[:, :, :head_size].astype(f32)
    d_key_raw, key_gain_terms = norm_back(rotate(d_key_rot, cosine, -sine), key_raw, gain_key)
    d_key_low = d_key_raw.reshape(local, kv_count * head_size).astype(bf16)
    d_value_low = d_kv_pos[:, :, head_size:].reshape(local, kv_count * head_size)
    grad_query = jnp.einsum("td,tf->df", normed, d_query_low, preferred_element_type=f32)
    grad_key = jnp.einsum("td,tf->df", normed, d_key_low, preferred_element_type=f32)
    grad_value = jnp.einsum("td,tf->df", normed, d_value_low, preferred_element_type=f32)
    d_normed = jnp.einsum("tf,df->td", d_query_low, w_query, preferred_element_type=f32)
    d_normed = d_normed + jnp.einsum("tf,df->td", d_key_low, w_key, preferred_element_type=f32)
    d_normed = d_normed + jnp.einsum("tf,df->td", d_value_low, w_value, preferred_element_type=f32)
    d_input_norm, attn_gain_terms = norm_back(d_normed, inputs, gain_attn)
    d_inputs = d_hidden + d_input_norm
    attn_sums = reduce_grads((grad_query, grad_key, grad_value, grad_out))
    gain_totals = lax.psum(
        (
            jnp.sum(attn_gain_terms, axis=0),
            jnp.sum(query_gain_terms, axis=(0, 1)),
            jnp.sum(key_gain_terms, axis=(0, 1)),
            jnp.sum(ffn_gain_terms, axis=0),
        ),
        ("dp", "seq"),
    )
    return (
        output[None],
        d_inputs[None],
        gain_totals[0],
        attn_sums[0],
        attn_sums[1],
        attn_sums[2],
        gain_totals[1],
        gain_totals[2],
        attn_sums[3],
        gain_totals[3],
        ffn_sums[0],
        ffn_sums[1],
        ffn_sums[2],
    )


AXES = ("zh", "zl", "y", "c", "x")
QBLOCK = 256
F32 = jnp.float32
BF16 = jnp.bfloat16


def swap(v, axis):
    return lax.ppermute(v, axis, [(0, 1), (1, 0)])


def transpose_pair(v):
    return lax.ppermute(v, ("c", "x"), [(0, 0), (1, 2), (2, 1), (3, 3)])


def pick(bit, low, high):
    return jnp.where(bit == 0, low, high)


def in_order(bit, own, other, axis):
    return jnp.concatenate([pick(bit, own, other), pick(bit, other, own)], axis=axis)


def dot(left, right, left_dim, right_dim):
    return lax.dot_general(
        left, right, (((left_dim,), (right_dim,)), ((), ())), preferred_element_type=F32
    )


def part_columns(w, c):
    width = w.shape[1] // 4
    return [lax.dynamic_slice_in_dim(w, (2 * i + c) * width, width, 1) for i in range(2)]


def part_rows(w, c):
    rows, columns = w.shape
    return lax.dynamic_index_in_dim(w.reshape(2, 2, rows // 4, columns), c, 1, False).reshape(rows // 2, columns)


def rope_rows(values, gain, cosine, sine):
    unit = values * lax.rsqrt(jnp.mean(values * values, axis=0, keepdims=True) + EPSILON) * gain
    half = values.shape[0] // 2
    first, second = unit[:half], unit[half:]
    return jnp.concatenate([first * cosine - second * sine, second * cosine + first * sine], axis=0)


def rope_rows_back(incoming, values, gain, cosine, sine):
    half = values.shape[0] // 2
    first, second = incoming[:half], incoming[half:]
    turned = jnp.concatenate([first * cosine + second * sine, second * cosine - first * sine], axis=0)
    inverse = lax.rsqrt(jnp.mean(values * values, axis=0, keepdims=True) + EPSILON)
    unit = values * inverse
    scaled = turned * gain
    d_values = inverse * (scaled - unit * jnp.mean(scaled * unit, axis=0, keepdims=True))
    return d_values, turned * unit


BLOCKED = 256.0


def split_low(v):
    high = v.astype(BF16)
    rest = v - high.astype(F32)
    middle = rest.astype(BF16)
    return [high, middle, (rest - middle.astype(F32)).astype(BF16)]


def documents(segment, rows, length):
    return (segment == lax.broadcasted_iota(jnp.int32, (rows, length), 0)).astype(F32)


def key_parts(begin, window):
    low = max(0, begin - (window - 1)) // QBLOCK * QBLOCK
    return ([(low, begin, False)] if begin > low else []) + [(begin, begin + QBLOCK, True)]


def causal(block):
    key_at = lax.broadcasted_iota(jnp.int32, (block, block), 0)
    return key_at <= lax.broadcasted_iota(jnp.int32, (block, block), 1)


def attention_kernel(
    segment_ref, gain_q_ref, gain_k_ref, cos_ref, sin_ref, q_ref, k_ref, v_ref,
    out_ref, exact_ref, log_ref, qs_ref, ks_ref, vs_ref, *, docs, window,
):
    size, length = k_ref.shape
    group = q_ref.shape[0] // size
    cosine, sine = cos_ref[...], sin_ref[...]
    same = documents(segment_ref[...], docs, length)
    k_rot = rope_rows(k_ref[...], gain_k_ref[...], cosine, sine)
    ks_ref[...] = k_rot.astype(BF16)
    keys = jnp.concatenate([k_rot, (same - 1.0) * BLOCKED], axis=0).T.astype(BF16)
    values = v_ref[...].astype(BF16)
    vs_ref[...] = values
    ones = (lax.broadcasted_iota(jnp.int32, (16, length), 0) == 0).astype(BF16)
    values = jnp.concatenate([values, ones], axis=0)
    allowed = causal(QBLOCK)
    for h in range(group):
        rows = pl.ds(h * size, size)
        q_rot = rope_rows(q_ref[rows, :], gain_q_ref[...], cosine, sine).astype(BF16)
        q_rot = q_rot * jnp.asarray(size ** (-0.5), BF16)
        qs_ref[rows, :] = q_rot
        query = jnp.concatenate([q_rot, same.astype(BF16)], axis=0)
        for begin in range(0, length, QBLOCK):
            stop = begin + QBLOCK
            result = 0.0
            for low, high, diagonal in key_parts(begin, window):
                e = jnp.exp(dot(keys[low:high], query[:, begin:stop], 1, 0))
                if diagonal:
                    e = jnp.where(allowed, e, 0.0)
                result = result + dot(values[:, low:high], e.astype(BF16), 1, 0)
            total = result[size : size + 1]
            result = result[:size] / total
            exact_ref[rows, begin:stop] = result
            out_ref[rows, begin:stop] = result.astype(BF16)
            log_ref[0, 0, h : h + 1, begin:stop] = jnp.log(total)


def attention(qkv, segment, gain_q, gain_k, cosine, sine, size, group, pairs, docs):
    rows, length = qkv.shape
    per = (group + 2) * size * pairs
    halves = rows // per
    unit = group * size
    q_rows, k_rows = per // unit, per // size
    full = lambda a: pl.BlockSpec(a.shape, lambda i, j: (0,) * a.ndim)
    wide = pl.BlockSpec((unit, length), lambda i, j: (pairs * i + j, 0))
    thin = pl.BlockSpec((size, length), lambda i, j: (pairs * i + j, 0))
    heads = halves * pairs * group
    return pl.pallas_call(
        functools.partial(attention_kernel, docs=docs, window=length // 2),
        grid=(halves, pairs),
        in_specs=[full(a) for a in (segment, gain_q, gain_k, cosine, sine)]
        + [
            pl.BlockSpec((unit, length), lambda i, j: (q_rows * i + j, 0)),
            pl.BlockSpec((size, length), lambda i, j: (k_rows * i + pairs * group + j, 0)),
            pl.BlockSpec((size, length), lambda i, j: (k_rows * i + pairs * (group + 1) + j, 0)),
        ],
        out_specs=[
            wide, wide, pl.BlockSpec((1, 1, group, length), lambda i, j: (i, j, 0, 0)), wide, thin, thin,
        ],
        out_shape=[
            jax.ShapeDtypeStruct((heads * size, length), BF16),
            jax.ShapeDtypeStruct((heads * size, length), F32),
            jax.ShapeDtypeStruct((halves, pairs, group, length), F32),
            jax.ShapeDtypeStruct((heads * size, length), BF16),
            jax.ShapeDtypeStruct((halves * pairs * size, length), BF16),
            jax.ShapeDtypeStruct((halves * pairs * size, length), BF16),
        ],
        cost_estimate=cost(40 * heads * size * length * length // 2, qkv, qkv),
        name="attention_forward",
    )(segment, gain_q, gain_k, cosine, sine, qkv, qkv, qkv)


def attention_back_kernel(
    segment_ref, gain_q_ref, gain_k_ref, cos_ref, sin_ref, q_ref, k_ref, qs_ref, ks_ref, vs_ref, exact_ref, log_ref,
    do_ref, out_ref, gq_ref, gk_ref, dk_ref, dv_ref, *, docs, window,
):
    size, length = k_ref.shape
    group = q_ref.shape[0] // size
    pair, pairs = pl.program_id(1), pl.num_programs(1)
    cosine, sine = cos_ref[...], sin_ref[...]

    @pl.when((pl.program_id(0) == 0) & (pair == 0))
    def _():
        gq_ref[...] = jnp.zeros_like(gq_ref)
        gk_ref[...] = jnp.zeros_like(gk_ref)

    def fold(terms):
        width = gq_ref.shape[1]
        return sum(terms[:, i : i + width] for i in range(0, length, width))

    same = documents(segment_ref[...], docs, length)
    threes = (lax.broadcasted_iota(jnp.int32, (8, length), 0) < 3).astype(F32)
    keys_t = ks_ref[...]
    keys = jnp.concatenate([keys_t.astype(F32), (same - 1.0) * BLOCKED, threes], axis=0).T.astype(BF16)
    values = jnp.concatenate([vs_ref[...].astype(F32), threes], axis=0).T.astype(BF16)
    allowed = causal(QBLOCK)
    dk_ref[...] = jnp.zeros_like(dk_ref)
    dv_ref[...] = jnp.zeros_like(dv_ref)
    scale = size ** (-0.5)
    for h in range(group):
        rows = pl.ds(h * size, size)
        q_t, do_t = qs_ref[rows, :], do_ref[rows, :]
        do_wide = do_t.astype(F32)
        q_nat = q_t.astype(F32).T.astype(BF16)
        do_nat = do_wide.T.astype(BF16)
        delta = jnp.sum(do_wide * exact_ref[rows, :], axis=0, keepdims=True)
        logs = [-v.astype(F32) for v in split_low(log_ref[0, 0, h : h + 1, :])]
        deltas = [-v.astype(F32) for v in split_low(delta)]
        zeros = jnp.zeros((5, length), F32)
        query = jnp.concatenate(
            [q_t, jnp.concatenate([same] + logs + [zeros], axis=0).astype(BF16)], axis=0
        )
        d_out = jnp.concatenate([do_wide] + deltas + [zeros], axis=0).astype(BF16)
        d_query = []
        for begin in range(0, length, QBLOCK):
            stop = begin + QBLOCK
            d_q = 0.0
            for low, high, diagonal in key_parts(begin, window):
                p = jnp.exp(dot(keys[low:high], query[:, begin:stop], 1, 0))
                if diagonal:
                    p = jnp.where(allowed, p, 0.0)
                ds = (p * dot(values[low:high], d_out[:, begin:stop], 1, 0)).astype(BF16)
                dv_ref[low:high, :] += dot(p.astype(BF16), do_nat[begin:stop], 1, 0)
                dk_ref[low:high, :] += dot(ds, q_nat[begin:stop], 1, 0)
                d_q = d_q + dot(keys_t[:, low:high], ds, 1, 0)
            d_query.append((d_q * scale).astype(BF16).astype(F32))
        d_q0, terms = rope_rows_back(
            jnp.concatenate(d_query, axis=1), q_ref[rows, :], gain_q_ref[...], cosine, sine
        )
        gq_ref[...] += fold(terms)
        out_ref[pl.ds((pair * group + h) * size, size), :] = d_q0.astype(BF16)
    d_key = dk_ref[...].T.astype(BF16).astype(F32)
    d_k0, terms = rope_rows_back(d_key, k_ref[...], gain_k_ref[...], cosine, sine)
    gk_ref[...] += fold(terms)
    out_ref[pl.ds((pairs * group + pair) * size, size), :] = d_k0.astype(BF16)
    out_ref[pl.ds((pairs * (group + 1) + pair) * size, size), :] = dv_ref[...].T.astype(BF16)


def attention_back(qkv, qs, ks, vs, exact, logs, d_out, segment, gain_q, gain_k, cosine, sine, size, group, pairs, docs):
    rows, length = qkv.shape
    per = (group + 2) * size * pairs
    halves = rows // per
    unit = group * size
    q_rows, k_rows = per // unit, per // size
    full = lambda a: pl.BlockSpec(a.shape, lambda i, j: (0,) * a.ndim)
    wide = pl.BlockSpec((unit, length), lambda i, j: (pairs * i + j, 0))
    thin = pl.BlockSpec((size, length), lambda i, j: (pairs * i + j, 0))
    return pl.pallas_call(
        functools.partial(attention_back_kernel, docs=docs, window=length // 2),
        grid=(halves, pairs),
        in_specs=[full(a) for a in (segment, gain_q, gain_k, cosine, sine)]
        + [
            pl.BlockSpec((unit, length), lambda i, j: (q_rows * i + j, 0)),
            pl.BlockSpec((size, length), lambda i, j: (k_rows * i + pairs * group + j, 0)),
            wide, thin, thin, wide,
            pl.BlockSpec((1, 1, group, length), lambda i, j: (i, j, 0, 0)),
            wide,
        ],
        out_specs=[
            pl.BlockSpec((per, length), lambda i, j: (i, 0)),
            pl.BlockSpec((size, 128), lambda i, j: (0, 0)),
            pl.BlockSpec((size, 128), lambda i, j: (0, 0)),
        ],
        out_shape=[
            jax.ShapeDtypeStruct((rows, length), BF16),
            jax.ShapeDtypeStruct((size, 128), F32),
            jax.ShapeDtypeStruct((size, 128), F32),
        ],
        scratch_shapes=[pltpu.VMEM((length, size), F32), pltpu.VMEM((length, size), F32)],
        cost_estimate=cost(80 * rows * length * length // 4, qkv, qkv),
        name="attention_backward",
    )(segment, gain_q, gain_k, cosine, sine, qkv, qkv, qs, ks, vs, exact, logs, d_out)


LANES = 128


def local_block(i, c, blocks):
    return lax.div(i, blocks) * 2 * blocks + c * blocks + lax.rem(i, blocks)


def front_kernel(sel_ref, own_ref, other_ref, gain_ref, query_ref, key_ref, value_ref, normed_ref, out_ref):
    local = own_ref.shape[0]

    @pl.when(pl.program_id(0) == 0)
    def _():
        for i, ref in enumerate((own_ref, other_ref)):
            place = pl.multiple_of((sel_ref[0] if i == 0 else 1 - sel_ref[0]) * local, local)
            v = ref[...].astype(F32)
            v = v * lax.rsqrt(jnp.mean(v * v, axis=-1, keepdims=True) + EPSILON) * gain_ref[...]
            normed_ref[pl.ds(place, local), :] = v.astype(BF16)

    at = 0
    for ref in (query_ref, key_ref, value_ref):
        out_ref[at : at + ref.shape[1], :] = dot(ref[...], normed_ref[...], 0, 1)
        at += ref.shape[1]


def front(sel, own, other, gain, w_query, w_key, w_value):
    local, d = own.shape
    widths = [w.shape[1] // 4 for w in (w_query, w_key, w_value)]
    part = pl.BlockSpec((local, d), lambda j, sel: (0, 0))
    return pl.pallas_call(
        front_kernel,
        grid_spec=pltpu.PrefetchScalarGridSpec(
            num_scalar_prefetch=1,
            grid=(2,),
            in_specs=[part, part, pl.BlockSpec((1, d), lambda j, sel: (0, 0))]
            + [pl.BlockSpec((d, w), lambda j, sel: (0, 2 * j + sel[0])) for w in widths],
            out_specs=[
                pl.BlockSpec((2 * local, d), lambda j, sel: (0, 0)),
                pl.BlockSpec((sum(widths), 2 * local), lambda j, sel: (j, 0)),
            ],
        ),
        out_shape=[
            jax.ShapeDtypeStruct((2 * local, d), BF16),
            jax.ShapeDtypeStruct((2 * sum(widths), 2 * local), F32),
        ],
        cost_estimate=cost(4 * local * d * 2 * sum(widths), own, own, w_query, w_query, w_query),
        name="norm_and_projections",
    )(sel, own, other, gain, w_query, w_key, w_value)


def ffn_kernel(
    sel_ref, hn_ref, own_ref, other_ref, gate0_ref, gate1_ref, up0_ref, up1_ref, down0_ref, down1_ref,
    act_ref, dg_ref, du_ref, gate_leave_ref, up_leave_ref, down_leave_ref, hy1_ref, hz1_ref, dx1_ref,
    turned_ref, hz0_ref, hy0_ref, dm_ref, dx0_ref,
):
    tokens, d = hn_ref.shape

    @pl.when(pl.program_id(0) == 0)
    def _():
        c, x, y, zl = [sel_ref[i] for i in range(4)]
        local, half, rows = tokens // 2, d // 2, d // 8
        for i, ref in enumerate((own_ref, other_ref)):
            place = pl.multiple_of((c if i == 0 else 1 - c) * local, local)
            dm_ref[pl.ds(place, local), :] = ref[...]
        turned_ref[...] = hn_ref[...].T
        for order in range(2):
            for i in range(4):
                high, low = divmod(i, 2)
                to = slice(i * rows, (i + 1) * rows)
                block = 4 * high + 2 * (zl if order else 1 - zl) + low
                (hz0_ref, hz1_ref)[order][to, :] = turned_ref[pl.ds(pl.multiple_of(block * rows, rows), rows), :]
                block = 4 * high + 2 * low + (y if order else 1 - y)
                (hy0_ref, hy1_ref)[order][to, :] = turned_ref[pl.ds(pl.multiple_of(block * rows, rows), rows), :]
            place = pl.multiple_of((x if order else 1 - x) * half, half)
            (dx0_ref, dx1_ref)[order][...] = dm_ref[:, pl.ds(place, half)]

    gate_w = jnp.concatenate([gate0_ref[...], gate1_ref[...]], axis=1)
    up_w = jnp.concatenate([up0_ref[...], up1_ref[...]], axis=1)
    down_w = jnp.concatenate([down0_ref[...], down1_ref[...]], axis=0)
    step = min(256, tokens)
    for begin in range(0, tokens, step):
        at = slice(begin, begin + step)
        gate = dot(hn_ref[at, :], gate_w, 1, 0)
        up = dot(hn_ref[at, :], up_w, 1, 0)
        d_act = dot(dm_ref[at, :], down_w, 1, 1)
        sigmoid = 1.0 / (1.0 + jnp.exp(-gate))
        silu = gate * sigmoid
        act_ref[at, :] = (silu * up).astype(BF16)
        du_ref[at, :] = (d_act * silu).astype(BF16)
        dg_ref[at, :] = (d_act * up * (sigmoid + silu * (1.0 - sigmoid))).astype(BF16)
    act_turned = act_ref[...].T
    up_leave_ref[...] = dot(hz0_ref[...], du_ref[...], 1, 0).astype(BF16)
    gate_leave_ref[...] = dot(hy0_ref[...], dg_ref[...], 1, 0).astype(BF16)
    down_leave_ref[...] = dot(act_turned, dx0_ref[...], 1, 0).astype(BF16)


def feed_forward(sel, hnormed, d_own, d_other, w_gate, w_up, w_down):
    tokens, d = hnormed.shape
    units = w_gate.shape[1] // 2
    blocks = units // 2 // LANES
    block = 2 * LANES
    whole = pl.BlockSpec((tokens, d), lambda j, sel: (0, 0))
    part = pl.BlockSpec((tokens // 2, d), lambda j, sel: (0, 0))
    columns = [
        pl.BlockSpec((d, LANES), lambda j, sel, i=i: (0, local_block(2 * j + i, sel[0], blocks))) for i in range(2)
    ]
    rows = [pl.BlockSpec((LANES, d), lambda j, sel, i=i: (local_block(2 * j + i, sel[0], blocks), 0)) for i in range(2)]
    return pl.pallas_call(
        ffn_kernel,
        grid_spec=pltpu.PrefetchScalarGridSpec(
            num_scalar_prefetch=1,
            grid=(units // block,),
            in_specs=[whole, part, part] + columns + columns + rows,
            out_specs=[pl.BlockSpec((tokens, block), lambda j, sel: (0, j))] * 3
            + [pl.BlockSpec((d // 2, block), lambda j, sel: (0, j))] * 2
            + [pl.BlockSpec((block, d // 2), lambda j, sel: (j, 0))]
            + [pl.BlockSpec((d // 2, tokens), lambda j, sel: (0, 0))] * 2
            + [pl.BlockSpec((tokens, d // 2), lambda j, sel: (0, 0))],
            scratch_shapes=[pltpu.VMEM((d, tokens), BF16)]
            + [pltpu.VMEM((d // 2, tokens), BF16)] * 2
            + [pltpu.VMEM((tokens, d), BF16), pltpu.VMEM((tokens, d // 2), BF16)],
        ),
        out_shape=[jax.ShapeDtypeStruct((tokens, units), BF16)] * 3
        + [jax.ShapeDtypeStruct((d // 2, units), BF16)] * 2
        + [jax.ShapeDtypeStruct((units, d // 2), BF16)]
        + [jax.ShapeDtypeStruct((d // 2, tokens), BF16)] * 2
        + [jax.ShapeDtypeStruct((tokens, d // 2), BF16)],
        cost_estimate=cost(12 * tokens * d * units, w_gate, w_gate, w_gate, w_gate),
        name="feed_forward",
    )(sel, hnormed, d_own, d_other, w_gate, w_gate, w_up, w_up, w_down, w_down)


def ffn_back_kernel(sel_ref, dg_ref, du_ref, gate0_ref, gate1_ref, up0_ref, up1_ref, out_ref, low_ref):
    gate_w = jnp.concatenate([gate0_ref[...], gate1_ref[...]], axis=1)
    up_w = jnp.concatenate([up0_ref[...], up1_ref[...]], axis=1)
    result = dot(dg_ref[...], gate_w, 1, 1) + dot(du_ref[...], up_w, 1, 1)
    out_ref[...] = result
    low_ref[...] = result.astype(BF16)


def ffn_back(sel, d_gate, d_up, w_gate, w_up):
    tokens, units = d_gate.shape
    d = w_gate.shape[0]
    block = min(256, d)
    whole = pl.BlockSpec((tokens, units), lambda j, sel: (0, 0))
    weights = [pl.BlockSpec((block, units // 2), lambda j, sel, i=i: (j, 2 * i + sel[0])) for i in range(2)]
    return pl.pallas_call(
        ffn_back_kernel,
        grid_spec=pltpu.PrefetchScalarGridSpec(
            num_scalar_prefetch=1,
            grid=(d // block,),
            in_specs=[whole, whole] + weights + weights,
            out_specs=[pl.BlockSpec((tokens, block), lambda j, sel: (0, j))] * 2,
        ),
        out_shape=[jax.ShapeDtypeStruct((tokens, d), t) for t in (F32, BF16)],
        cost_estimate=cost(4 * tokens * d * units, d_gate, d_up, w_gate),
        name="feed_forward_back",
    )(sel, d_gate, d_up, w_gate, w_gate, w_up, w_up)


def ffn_out_kernel(sel_ref, act_ref, down0_ref, down1_ref, own_ref, low_ref):
    local = own_ref.shape[0]
    down_w = jnp.concatenate([down0_ref[...], down1_ref[...]], axis=0)
    own_ref[...] = dot(act_ref[pl.ds(pl.multiple_of(sel_ref[0] * local, local), local), :], down_w, 1, 0)
    other = act_ref[pl.ds(pl.multiple_of((1 - sel_ref[0]) * local, local), local), :]
    low_ref[...] = dot(other, down_w, 1, 0).astype(BF16)


def ffn_out(sel, act, w_down):
    tokens, units = act.shape
    d = w_down.shape[1]
    block = min(256, d)
    weights = [pl.BlockSpec((units // 2, block), lambda j, sel, i=i: (2 * i + sel[0], j)) for i in range(2)]
    return pl.pallas_call(
        ffn_out_kernel,
        grid_spec=pltpu.PrefetchScalarGridSpec(
            num_scalar_prefetch=1,
            grid=(d // block,),
            in_specs=[pl.BlockSpec((tokens, units), lambda j, sel: (0, 0))] + weights,
            out_specs=[pl.BlockSpec((tokens // 2, block), lambda j, sel: (0, j))] * 2,
        ),
        out_shape=[jax.ShapeDtypeStruct((tokens // 2, d), t) for t in (F32, BF16)],
        cost_estimate=cost(2 * tokens * d * units, act),
        name="feed_forward_out",
    )(sel, act, w_down, w_down)


def tie(values, *others):
    return lax.optimization_barrier((tuple(values), others))[0]


def cost(flops, *arrays):
    return pl.CostEstimate(flops=flops, transcendentals=0, bytes_accessed=sum(a.size * a.dtype.itemsize for a in arrays))


def add_up(terms):
    return sum(t.astype(F32) for t in terms)


def leave(terms, dim, bit):
    size = terms[0].shape[dim] // 2
    if dim < terms[0].ndim - 2:
        return add_up([lax.dynamic_slice_in_dim(t, (1 - bit) * size, size, dim) for t in terms]).astype(BF16)
    low = add_up([lax.slice_in_dim(t, 0, size, axis=dim) for t in terms])
    high = add_up([lax.slice_in_dim(t, size, 2 * size, axis=dim) for t in terms])
    return pick(bit, high, low).astype(BF16)


def stay(terms, dim, bit):
    size = terms[0].shape[dim] // 2
    if dim < terms[0].ndim - 2:
        return [lax.dynamic_slice_in_dim(t, bit * size, size, dim) for t in terms]
    return [
        pick(bit, lax.slice_in_dim(t, 0, size, axis=dim), lax.slice_in_dim(t, size, 2 * size, axis=dim))
        for t in terms
    ]


def halve(terms, axis, dim):
    bit = lax.axis_index(axis)
    return stay(terms, dim, bit) + [swap(leave(terms, dim, bit), axis)]


def share_rows(total, c):
    rows = total.shape[0] // 2
    own = pick(c, total[:rows], total[rows:])
    other = swap(pick(c, total[rows:], total[:rows]).astype(BF16), "c").astype(F32)
    return in_order(c, own, other, 1)


def own_rows(v, c, local):
    return pick(c, v[:local], v[local:])


def pair_body(
    tokens, cotangent, doc_lengths, attn_gain, w_query, w_key, w_value, query_gain, key_gain, w_out,
    ffn_gain, w_gate, w_up, w_down,
):
    local, d = tokens.shape[1:]
    length = 2 * local
    size = query_gain.shape[0]
    kv_count = w_key.shape[1] // size
    group = w_query.shape[1] // w_key.shape[1]
    pairs = kv_count // 4
    zh, zl, y, c, x = [lax.axis_index(a) for a in AXES]
    gain_attn = attn_gain.astype(F32)
    gain_ffn = ffn_gain.astype(F32)
    gain_q = query_gain.astype(F32)[:, None]
    gain_k = key_gain.astype(F32)[:, None]

    own_tokens = transpose_pair(tokens[0])
    lengths = jnp.where(c == x, doc_lengths[0], swap(doc_lengths[0], "c"))
    ends = jnp.cumsum(lengths)
    positions = jnp.arange(length, dtype=jnp.int32)
    segment = jnp.sum((ends[:, None] <= positions[None, :]).astype(jnp.int32), axis=0, keepdims=True)
    half = size // 2
    spread = jnp.exp(jnp.arange(half, dtype=F32) * (-2.0 * math.log(1000000.0) / size))
    angles = spread[:, None] * positions.astype(F32)[None, :]
    cosine, sine = jnp.cos(angles), jnp.sin(angles)
    parts = [part_columns(w, c) for w in (w_query, w_key, w_value)]
    w_qkv = jnp.concatenate([p[i] for i in range(2) for p in parts], axis=1)
    out_w = part_rows(w_out, c)
    sel = jnp.stack([c, x, y, zl]).astype(jnp.int32)
    w_qkv, out_w, cosine, sine, sel, own_tokens = tie((w_qkv, out_w, cosine, sine, sel, own_tokens))
    other_tokens = swap(own_tokens, "c")
    cot_low, other_tokens = tie((cotangent[0], other_tokens))
    own_cot = transpose_pair(cot_low)
    normed, qkv = front(sel, own_tokens, other_tokens, gain_attn[None], w_query, w_key, w_value)
    docs = doc_lengths.shape[1]
    attended_own, exact, logs, qs, ks, vs = attention(
        qkv, segment, gain_q, gain_k, cosine, sine, size, group, pairs, docs
    )
    attended_own, own_cot = tie((attended_own, own_cot))
    attended_other = swap(attended_own, "c")
    other_cot = swap(own_cot, "c")
    width = attended_own.shape[0] // 2
    attended = jnp.concatenate(
        [in_order(c, attended_own[i : i + width], attended_other[i : i + width], 0) for i in (0, width)], axis=0
    )
    inputs = in_order(c, own_tokens, other_tokens, 0).astype(F32)
    hidden = inputs + dot(attended, w_out, 0, 0)
    hnormed = rms_scale(hidden, gain_ffn).astype(BF16)

    act, d_gate, d_up, send_gate, send_up, send_down, hn_y, hn_z, dm_x = feed_forward(
        sel, hnormed, own_cot, other_cot, w_gate, w_up, w_down
    )
    come_up, come_down, come_gate = swap(send_up, "zl"), swap(send_down, "x"), swap(send_gate, "y")
    d_hn, d_hn_low = ffn_back(sel, d_gate, d_up, w_gate, w_up)
    d_hn_other = swap(d_hn_low, "c")
    hn_y, hn_z, dm_x = tie((hn_y, hn_z, dm_x), d_hn)
    keep_up = dot(hn_z, d_up, 1, 0).astype(BF16)
    keep_gate = dot(hn_y, d_gate, 1, 0).astype(BF16)
    keep_down = dot(act, dm_x, 0, 0).astype(BF16)
    (d_hn_other,) = tie((d_hn_other,), keep_up, keep_gate, keep_down)
    d_hn = d_hn + d_hn_other.astype(F32)
    d_hidden_norm, ffn_gain_terms = norm_back(d_hn, hidden, gain_ffn)
    d_hidden = in_order(c, own_cot, other_cot, 0).astype(F32) + d_hidden_norm
    d_attn = d_hidden.astype(BF16)
    d_attended = dot(out_w, d_attn, 1, 1).astype(BF16)
    units = d_gate.shape[1]
    rows = d // 8
    quarter = d // 4
    send_out, keep_out = [
        dot(attended, lax.dynamic_slice_in_dim(d_attn, (2 * i + c) * quarter, quarter, 1), 1, 0).astype(BF16)
        for i in (1 - x, x)
    ]
    come_out = swap(send_out, "x")
    (d_attended,) = tie((d_attended,), send_out, keep_out)
    d_qkv, gain_q_terms, gain_k_terms = attention_back(
        qkv, qs, ks, vs, exact, logs, d_attended, segment, gain_q, gain_k, cosine, sine, size, group, pairs, docs
    )

    come_up, come_down, come_gate, come_out, d_qkv = tie((come_up, come_down, come_gate, come_out, d_qkv))
    up = [v.reshape(2, 2, rows, units) for v in (keep_up, come_up)]
    down = [v.reshape(2, 2, units // 4, d // 2) for v in (keep_down, come_down)]
    gate = [v.reshape(2, 2, rows, units) for v in (keep_gate, come_gate)]
    send_gate, send_down, send_up = leave(gate, 1, zl), leave(down, 1, y), leave(up, 3, x)
    gate = stay(gate, 1, zl) + [swap(send_gate, "zl")]
    down = stay(down, 1, y) + [swap(send_down, "y")]
    up = stay(up, 3, x) + [swap(send_up, "x")]

    (d_qkv,) = tie((d_qkv,), send_gate, send_down, send_up)
    width = d_qkv.shape[0] // 2
    send_qkv = dot(normed, lax.dynamic_slice_in_dim(d_qkv, (1 - x) * width, width, 0), 0, 1).astype(BF16)
    come_qkv = swap(send_qkv, "x")
    (d_qkv,) = tie((d_qkv,), send_qkv)
    part_low = dot(pick(c, d_qkv[:, local:], d_qkv[:, :local]), w_qkv, 0, 1).astype(BF16)
    part_other = swap(part_low, "c")
    (d_qkv,) = tie((d_qkv,), part_low)
    part = dot(pick(c, d_qkv[:, :local], d_qkv[:, local:]), w_qkv, 0, 1)
    keep_qkv = dot(normed, lax.dynamic_slice_in_dim(d_qkv, x * width, width, 0), 0, 1).astype(BF16)
    (part_other,) = tie((part_other,), keep_qkv, part)
    d_normed = part + part_other.astype(F32)
    d_input_norm, attn_gain_terms = norm_back(d_normed, own_tokens.astype(F32), gain_attn)
    d_inputs = own_rows(d_hidden, c, local) + d_input_norm
    gains = jnp.concatenate(
        [
            jnp.sum(attn_gain_terms, axis=0),
            jnp.sum(ffn_gain_terms, axis=0) * 0.5,
            jnp.sum(gain_q_terms, axis=1),
            jnp.sum(gain_k_terms, axis=1),
        ]
    ).reshape(-1, 128)

    gate[-1], down[-1] = tie((gate[-1], down[-1]), d_inputs, gains)
    send_gate, send_down = leave(gate, 3, x), add_up(down).astype(BF16)
    gate = stay(gate, 3, x) + [swap(send_gate, "x")]
    down = down + [lax.ppermute(send_down, ("zl", "c"), [(2, 0), (1, 3)])]
    (act,) = tie((act,), send_gate, send_down)
    reached = swap(gains, AXES[0])
    part_out, out_low = ffn_out(sel, act, w_down)
    out_other = swap(out_low, "c")
    come_out, up[-1], come_qkv, reached = tie((come_out, up[-1], come_qkv, reached), part_out)
    gains = gains + reached
    reached = swap(gains, AXES[1])
    send_up = leave(up, 1, y)
    up = stay(up, 1, y) + [swap(send_up, "y")]
    out = [v.reshape(2, 2, 2, rows, quarter) for v in (keep_out, come_out)]
    qkv_grad = [v.reshape(2, 2, 2, rows, width) for v in (keep_qkv, come_qkv)]
    both = [out, qkv_grad]

    def next_stage(both, axis, dim):
        bit = lax.axis_index(axis)
        send = jnp.concatenate([leave(t, dim, bit) for t in both], axis=-1)
        come = swap(send, axis)
        return [stay(t, dim, bit) + [v] for t, v in zip(both, (come[..., :quarter], come[..., quarter:]))]

    both = next_stage(both, "y", 2)
    out_other, reached = tie((out_other, reached), send_up)
    gains = gains + reached
    output = own_rows(hidden, c, local) + part_out + out_other.astype(F32)
    results = jnp.concatenate([output.astype(BF16), d_inputs.astype(BF16)], axis=0)

    gate[-1], down[-1], results, gains = tie((gate[-1], down[-1], results, gains))
    reached = swap(gains, AXES[2])
    send_gate, send_down = leave(gate, 0, zh), leave(down, 0, zh)
    gate = stay(gate, 0, zh) + [swap(send_gate, "zh")]
    down = stay(down, 0, zh) + [swap(send_down, "zh")]
    up[-1], both[0][-1], both[1][-1], reached = tie((up[-1], both[0][-1], both[1][-1], reached), send_gate, send_down)
    gains = gains + reached
    reached = swap(gains, AXES[3])
    send_up = leave(up, 0, zh)
    up = stay(up, 0, zh) + [swap(send_up, "zh")]
    both = next_stage(both, "zl", 1)
    results, reached = tie((results, reached), send_up)
    results_other = transpose_pair(results)
    gains = gains + reached
    reached = swap(gains, AXES[4])
    out, qkv_grad = next_stage(both, "zh", 0)

    total = add_up(down).reshape(-1, d // 2)
    n = total.shape[0] // 2
    own = pick(c, total[:n], total[n:])
    other = pick(c, total[n:], total[:n]).astype(BF16)
    other = lax.ppermute(other, ("zl", "c"), [(0, 1), (3, 2)]).astype(F32)
    sum_down = jnp.where(zl == c, own, other)
    sum_gate, sum_up = [share_rows(add_up(t).reshape(rows, units // 2), c) for t in (gate, up)]
    out[-1], qkv_grad[-1], reached = tie((out[-1], qkv_grad[-1], reached), sum_gate, sum_up, sum_down)
    gains = (gains + reached).reshape(-1)
    both = jnp.concatenate([add_up(t).reshape(rows, -1) for t in (out, qkv_grad)], axis=1)
    n = rows // 2
    own = pick(c, both[:n], both[n:])
    other = swap(pick(c, both[n:], both[:n]).astype(BF16), "c").astype(F32)
    first, second = pick(c, own, other), pick(c, other, own)
    q_width, kv_width = pairs * group * size, pairs * size
    ends_of = [0, quarter, quarter + q_width, quarter + q_width + kv_width, quarter + q_width + 2 * kv_width]
    sum_out, sum_query, sum_key, sum_value = [
        jnp.concatenate([first[:, low:high], second[:, low:high]], axis=1)
        for low, high in zip(ends_of[:-1], ends_of[1:])
    ]
    stays = c == x
    output = jnp.where(stays, output, results_other[:local].astype(F32))
    d_inputs = jnp.where(stays, d_inputs, results_other[local:].astype(F32))
    return (
        output[None],
        d_inputs[None],
        gains[:d],
        sum_query,
        sum_key,
        sum_value,
        gains[2 * d : 2 * d + size],
        gains[2 * d + size :],
        sum_out,
        gains[d : 2 * d],
        sum_gate,
        sum_up,
        sum_down,
    )


def solution(mesh):
    rows, shards = mesh.shape["dp"], mesh.shape["seq"]
    if rows == 16 and shards == 2:
        body = pair_body
        mesh = Mesh(mesh.devices.reshape(2, 2, 2, 2, 2), AXES)
        dp, seq = AXES[:4], "x"
    else:
        body = general_body
        dp, seq = "dp", "seq"
    return jax.shard_map(
        body,
        mesh=mesh,
        in_specs=(P(dp, seq, None), P(dp, seq, None), P(dp, None)) + (P(),) * 11,
        out_specs=(P(dp, seq, None), P(dp, seq, None), P())
        + (P(dp, seq),) * 3
        + (P(), P(), P(dp, seq), P())
        + (P(dp, seq),) * 3,
        check_vma=False,
    )
```

```python
import math

import functools

import jax
import jax.numpy as jnp
from jax import lax
from jax.experimental import pallas as pl
from jax.experimental.pallas import tpu as pltpu
from jax.sharding import Mesh
from jax.sharding import PartitionSpec as P

EPSILON = 1e-06


def rms_scale(values, gain):
    return values * lax.rsqrt(jnp.mean(values * values, axis=-1, keepdims=True) + EPSILON) * gain


def norm_back(incoming, values, gain):
    inverse = lax.rsqrt(jnp.mean(values * values, axis=-1, keepdims=True) + EPSILON)
    unit = values * inverse
    scaled = incoming * gain
    d_values = inverse * (scaled - unit * jnp.mean(scaled * unit, axis=-1, keepdims=True))
    return (d_values, incoming * unit)


def rope_tables(first, count, width):
    half = width // 2
    spread = jnp.exp(jnp.arange(half, dtype=jnp.float32) * (-2.0 * math.log(1000000.0) / width))
    places = (first + jnp.arange(count, dtype=jnp.int32)).astype(jnp.float32)
    angles = places[:, None] * spread[None, :]
    return (jnp.cos(angles)[:, None, :], jnp.sin(angles)[:, None, :])


def rotate(values, cosine, sine):
    half = values.shape[-1] // 2
    first_half = values[..., :half]
    second_half = values[..., half:]
    return jnp.concatenate(
        [first_half * cosine - second_half * sine, second_half * cosine + first_half * sine],
        axis=-1,
    )


def reduce_grads(grads):
    partial_sum = lax.psum_scatter(grads, "dp", scatter_dimension=0, tiled=True)
    return lax.psum_scatter(partial_sum, "seq", scatter_dimension=1, tiled=True)


def general_body(
    tokens,
    cotangent,
    doc_lengths,
    attn_gain,
    w_query,
    w_key,
    w_value,
    query_gain,
    key_gain,
    w_out,
    ffn_gain,
    w_gate,
    w_up,
    w_down,
):
    shards = lax.axis_size("seq")
    local = tokens.shape[1]
    length = local * shards
    head_size = query_gain.shape[0]
    kv_count = w_key.shape[1] // head_size
    head_count = w_query.shape[1] // head_size
    group = head_count // kv_count
    kv_local = kv_count // shards
    block = min(512, length)
    num_blocks = length // block
    scale = head_size ** (-0.5)
    f32 = jnp.float32
    bf16 = jnp.bfloat16
    gain_attn = attn_gain.astype(f32)
    gain_query = query_gain.astype(f32)
    gain_key = key_gain.astype(f32)
    gain_ffn = ffn_gain.astype(f32)
    inputs = tokens[0].astype(f32)
    normed = rms_scale(inputs, gain_attn).astype(bf16)
    query_raw = jnp.dot(normed, w_query, preferred_element_type=f32).reshape(
        local, head_count, head_size
    )
    key_raw = jnp.dot(normed, w_key, preferred_element_type=f32).reshape(local, kv_count, head_size)
    values = (
        jnp.dot(normed, w_value, preferred_element_type=f32)
        .astype(bf16)
        .reshape(local, kv_count, head_size)
    )
    cosine, sine = rope_tables(lax.axis_index("seq") * local, local, head_size)
    query_rot = rotate(rms_scale(query_raw, gain_query), cosine, sine).astype(bf16)
    key_rot = rotate(rms_scale(key_raw, gain_key), cosine, sine).astype(bf16)
    packed_query = query_rot.reshape(local, kv_count, group * head_size)
    packed_kv = jnp.concatenate([key_rot, values], axis=2)
    query_heads, kv_heads = (
        lax.all_to_all(packed_query, "seq", split_axis=1, concat_axis=0, tiled=True),
        lax.all_to_all(packed_kv, "seq", split_axis=1, concat_axis=0, tiled=True),
    )
    query_all = query_heads.reshape(length, kv_local, group, head_size)
    key_all = kv_heads[:, :, :head_size]
    value_all = kv_heads[:, :, head_size:]
    positions = jnp.arange(length, dtype=jnp.int32)
    ends = jnp.cumsum(doc_lengths[0])
    segment = jnp.sum((ends[None, :] <= positions[:, None]).astype(jnp.int32), axis=1)
    starts = jnp.arange(num_blocks, dtype=jnp.int32) * block

    def allowed_at(begin):
        rows_here = begin + jnp.arange(block, dtype=jnp.int32)
        query_seg = lax.dynamic_slice_in_dim(segment, begin, block, 0)
        return (query_seg[:, None] == segment[None, :]) & (positions[None, :] <= rows_here[:, None])

    def block_scores(begin):
        query_block = lax.dynamic_slice_in_dim(query_all, begin, block, 0)
        scores = (
            jnp.einsum("qhgd,khd->hgqk", query_block, key_all, preferred_element_type=f32) * scale
        )
        return (query_block, jnp.where(allowed_at(begin), scores, -jnp.inf))

    def attend(begin):
        query_block, scores = block_scores(begin)
        top_score = jnp.max(scores, axis=-1, keepdims=True)
        expos = jnp.exp(scores - top_score)
        totals = jnp.sum(expos, axis=-1, keepdims=True)
        probs = (expos / totals).astype(bf16)
        result = jnp.einsum("hgqk,khd->qhgd", probs, value_all, preferred_element_type=f32)
        return (result.astype(bf16), top_score[..., 0] + jnp.log(totals[..., 0]))

    attended_heads, log_totals = lax.map(attend, starts)
    attended_heads = attended_heads.reshape(length, kv_local, group * head_size)
    attended = lax.all_to_all(
        attended_heads, "seq", split_axis=0, concat_axis=1, tiled=True
    ).reshape(local, head_count * head_size)
    hidden = inputs + jnp.dot(attended, w_out, preferred_element_type=f32)
    hnormed = rms_scale(hidden, gain_ffn).astype(bf16)
    gate = jnp.dot(hnormed, w_gate, preferred_element_type=f32)
    up_part = jnp.dot(hnormed, w_up, preferred_element_type=f32)
    act = (jax.nn.silu(gate) * up_part).astype(bf16)
    output = hidden + jnp.dot(act, w_down, preferred_element_type=f32)
    d_mlp = cotangent[0]
    grad_down = jnp.einsum("tf,td->fd", act, d_mlp, preferred_element_type=f32)
    d_act = jnp.einsum("td,fd->tf", d_mlp, w_down, preferred_element_type=f32)
    gate_again = jnp.dot(hnormed, w_gate, preferred_element_type=f32)
    up_again = jnp.dot(hnormed, w_up, preferred_element_type=f32)
    sigmoid_gate = jax.nn.sigmoid(gate_again)
    d_up = (d_act * gate_again * sigmoid_gate).astype(bf16)
    d_gate = (d_act * up_again * sigmoid_gate * (1.0 + gate_again * (1.0 - sigmoid_gate))).astype(
        bf16
    )
    grad_gate = jnp.einsum("td,tf->df", hnormed, d_gate, preferred_element_type=f32)
    grad_up = jnp.einsum("td,tf->df", hnormed, d_up, preferred_element_type=f32)
    ffn_sums = reduce_grads((grad_gate, grad_up, grad_down))
    d_hnormed = jnp.einsum("tf,df->td", d_gate, w_gate, preferred_element_type=f32) + jnp.einsum(
        "tf,df->td", d_up, w_up, preferred_element_type=f32
    )
    d_hidden_norm, ffn_gain_terms = norm_back(d_hnormed, hidden, gain_ffn)
    d_hidden = cotangent[0].astype(f32) + d_hidden_norm
    d_attn = d_hidden.astype(bf16)
    grad_out = jnp.einsum("tf,td->fd", attended, d_attn, preferred_element_type=f32)
    d_attended = jnp.einsum("td,fd->tf", d_attn, w_out, preferred_element_type=f32).astype(bf16)
    d_heads = lax.all_to_all(
        d_attended.reshape(local, kv_count, group * head_size),
        "seq",
        split_axis=1,
        concat_axis=0,
        tiled=True,
    )
    d_all = d_heads.reshape(length, kv_local, group, head_size)

    def attend_back(carry, item):
        begin, log_block = item
        query_block, scores = block_scores(begin)
        probs = jnp.exp(scores - log_block[..., None])
        d_block = lax.dynamic_slice_in_dim(d_all, begin, block, 0)
        d_probs = jnp.einsum("qhgd,khd->hgqk", d_block, value_all, preferred_element_type=f32)
        delta = jnp.sum(probs * d_probs, axis=-1, keepdims=True)
        d_scores = (scale * (probs * (d_probs - delta))).astype(bf16)
        d_query_block = jnp.einsum("hgqk,khd->qhgd", d_scores, key_all, preferred_element_type=f32)
        key_total = carry[0] + jnp.einsum(
            "hgqk,qhgd->khd", d_scores, query_block, preferred_element_type=f32
        )
        value_total = carry[1] + jnp.einsum(
            "hgqk,qhgd->khd", probs.astype(bf16), d_block, preferred_element_type=f32
        )
        return ((key_total, value_total), d_query_block.astype(bf16))

    empty = jnp.zeros((length, kv_local, head_size), f32)
    (d_keys, d_values), d_queries = lax.scan(attend_back, (empty, empty), (starts, log_totals))
    d_queries = d_queries.reshape(length, kv_local, group * head_size)
    d_kv = jnp.concatenate([d_keys.astype(bf16), d_values.astype(bf16)], axis=2)
    d_query_pos, d_kv_pos = (
        lax.all_to_all(d_queries, "seq", split_axis=0, concat_axis=1, tiled=True),
        lax.all_to_all(d_kv, "seq", split_axis=0, concat_axis=1, tiled=True),
    )
    d_query_rot = d_query_pos.reshape(local, head_count, head_size).astype(f32)
    d_query_raw, query_gain_terms = norm_back(
        rotate(d_query_rot, cosine, -sine), query_raw, gain_query
    )
    d_query_low = d_query_raw.reshape(local, head_count * head_size).astype(bf16)
    d_key_rot = d_kv_pos[:, :, :head_size].astype(f32)
    d_key_raw, key_gain_terms = norm_back(rotate(d_key_rot, cosine, -sine), key_raw, gain_key)
    d_key_low = d_key_raw.reshape(local, kv_count * head_size).astype(bf16)
    d_value_low = d_kv_pos[:, :, head_size:].reshape(local, kv_count * head_size)
    grad_query = jnp.einsum("td,tf->df", normed, d_query_low, preferred_element_type=f32)
    grad_key = jnp.einsum("td,tf->df", normed, d_key_low, preferred_element_type=f32)
    grad_value = jnp.einsum("td,tf->df", normed, d_value_low, preferred_element_type=f32)
    d_normed = jnp.einsum("tf,df->td", d_query_low, w_query, preferred_element_type=f32)
    d_normed = d_normed + jnp.einsum("tf,df->td", d_key_low, w_key, preferred_element_type=f32)
    d_normed = d_normed + jnp.einsum("tf,df->td", d_value_low, w_value, preferred_element_type=f32)
    d_input_norm, attn_gain_terms = norm_back(d_normed, inputs, gain_attn)
    d_inputs = d_hidden + d_input_norm
    attn_sums = reduce_grads((grad_query, grad_key, grad_value, grad_out))
    gain_totals = lax.psum(
        (
            jnp.sum(attn_gain_terms, axis=0),
            jnp.sum(query_gain_terms, axis=(0, 1)),
            jnp.sum(key_gain_terms, axis=(0, 1)),
            jnp.sum(ffn_gain_terms, axis=0),
        ),
        ("dp", "seq"),
    )
    return (
        output[None],
        d_inputs[None],
        gain_totals[0],
        attn_sums[0],
        attn_sums[1],
        attn_sums[2],
        gain_totals[1],
        gain_totals[2],
        attn_sums[3],
        gain_totals[3],
        ffn_sums[0],
        ffn_sums[1],
        ffn_sums[2],
    )


AXES = ("zh", "zl", "y", "c", "x")
QBLOCK = 256
F32 = jnp.float32
BF16 = jnp.bfloat16


def swap(v, axis):
    return lax.ppermute(v, axis, [(0, 1), (1, 0)])


def transpose_pair(v):
    return lax.ppermute(v, ("c", "x"), [(0, 0), (1, 2), (2, 1), (3, 3)])


def pick(bit, low, high):
    return jnp.where(bit == 0, low, high)


def in_order(bit, own, other, axis):
    return jnp.concatenate([pick(bit, own, other), pick(bit, other, own)], axis=axis)


def dot(left, right, left_dim, right_dim):
    return lax.dot_general(
        left, right, (((left_dim,), (right_dim,)), ((), ())), preferred_element_type=F32
    )


def part_columns(w, c):
    width = w.shape[1] // 4
    return [lax.dynamic_slice_in_dim(w, (2 * i + c) * width, width, 1) for i in range(2)]


def part_rows(w, c):
    rows, columns = w.shape
    return lax.dynamic_index_in_dim(w.reshape(2, 2, rows // 4, columns), c, 1, False).reshape(rows // 2, columns)


def rope_rows(values, gain, cosine, sine):
    unit = values * lax.rsqrt(jnp.mean(values * values, axis=0, keepdims=True) + EPSILON) * gain
    half = values.shape[0] // 2
    first, second = unit[:half], unit[half:]
    return jnp.concatenate([first * cosine - second * sine, second * cosine + first * sine], axis=0)


def rope_rows_back(incoming, values, gain, cosine, sine):
    half = values.shape[0] // 2
    first, second = incoming[:half], incoming[half:]
    turned = jnp.concatenate([first * cosine + second * sine, second * cosine - first * sine], axis=0)
    inverse = lax.rsqrt(jnp.mean(values * values, axis=0, keepdims=True) + EPSILON)
    unit = values * inverse
    scaled = turned * gain
    d_values = inverse * (scaled - unit * jnp.mean(scaled * unit, axis=0, keepdims=True))
    return d_values, turned * unit


BLOCKED = 256.0


def split_low(v):
    high = v.astype(BF16)
    rest = v - high.astype(F32)
    middle = rest.astype(BF16)
    return [high, middle, (rest - middle.astype(F32)).astype(BF16)]


def documents(segment, rows, length):
    return (segment == lax.broadcasted_iota(jnp.int32, (rows, length), 0)).astype(F32)


def key_parts(begin, window):
    low = max(0, begin - (window - 1)) // QBLOCK * QBLOCK
    return ([(low, begin, False)] if begin > low else []) + [(begin, begin + QBLOCK, True)]


def causal(block):
    key_at = lax.broadcasted_iota(jnp.int32, (block, block), 0)
    return key_at <= lax.broadcasted_iota(jnp.int32, (block, block), 1)


def attention_kernel(
    segment_ref, gain_q_ref, gain_k_ref, cos_ref, sin_ref, q_ref, k_ref, v_ref,
    out_ref, exact_ref, log_ref, qs_ref, ks_ref, vs_ref, *, docs, window,
):
    size, length = k_ref.shape
    group = q_ref.shape[0] // size
    cosine, sine = cos_ref[...], sin_ref[...]
    same = documents(segment_ref[...], docs, length)
    k_rot = rope_rows(k_ref[...], gain_k_ref[...], cosine, sine)
    ks_ref[...] = k_rot.astype(BF16)
    keys = jnp.concatenate([k_rot, (same - 1.0) * BLOCKED], axis=0).T.astype(BF16)
    values = v_ref[...].astype(BF16)
    vs_ref[...] = values
    ones = (lax.broadcasted_iota(jnp.int32, (16, length), 0) == 0).astype(BF16)
    values = jnp.concatenate([values, ones], axis=0)
    allowed = causal(QBLOCK)
    for h in range(group):
        rows = pl.ds(h * size, size)
        q_rot = rope_rows(q_ref[rows, :], gain_q_ref[...], cosine, sine).astype(BF16)
        q_rot = q_rot * jnp.asarray(size ** (-0.5), BF16)
        qs_ref[rows, :] = q_rot
        query = jnp.concatenate([q_rot, same.astype(BF16)], axis=0)
        for begin in range(0, length, QBLOCK):
            stop = begin + QBLOCK
            result = 0.0
            for low, high, diagonal in key_parts(begin, window):
                e = jnp.exp(dot(keys[low:high], query[:, begin:stop], 1, 0))
                if diagonal:
                    e = jnp.where(allowed, e, 0.0)
                result = result + dot(values[:, low:high], e.astype(BF16), 1, 0)
            total = result[size : size + 1]
            result = result[:size] / total
            exact_ref[rows, begin:stop] = result
            out_ref[rows, begin:stop] = result.astype(BF16)
            log_ref[0, 0, h : h + 1, begin:stop] = jnp.log(total)


def attention(qkv, segment, gain_q, gain_k, cosine, sine, size, group, pairs, docs):
    rows, length = qkv.shape
    per = (group + 2) * size * pairs
    halves = rows // per
    unit = group * size
    q_rows, k_rows = per // unit, per // size
    full = lambda a: pl.BlockSpec(a.shape, lambda i, j: (0,) * a.ndim)
    wide = pl.BlockSpec((unit, length), lambda i, j: (pairs * i + j, 0))
    thin = pl.BlockSpec((size, length), lambda i, j: (pairs * i + j, 0))
    heads = halves * pairs * group
    return pl.pallas_call(
        functools.partial(attention_kernel, docs=docs, window=length // 2),
        grid=(halves, pairs),
        in_specs=[full(a) for a in (segment, gain_q, gain_k, cosine, sine)]
        + [
            pl.BlockSpec((unit, length), lambda i, j: (q_rows * i + j, 0)),
            pl.BlockSpec((size, length), lambda i, j: (k_rows * i + pairs * group + j, 0)),
            pl.BlockSpec((size, length), lambda i, j: (k_rows * i + pairs * (group + 1) + j, 0)),
        ],
        out_specs=[
            wide, wide, pl.BlockSpec((1, 1, group, length), lambda i, j: (i, j, 0, 0)), wide, thin, thin,
        ],
        out_shape=[
            jax.ShapeDtypeStruct((heads * size, length), BF16),
            jax.ShapeDtypeStruct((heads * size, length), F32),
            jax.ShapeDtypeStruct((halves, pairs, group, length), F32),
            jax.ShapeDtypeStruct((heads * size, length), BF16),
            jax.ShapeDtypeStruct((halves * pairs * size, length), BF16),
            jax.ShapeDtypeStruct((halves * pairs * size, length), BF16),
        ],
        cost_estimate=cost(40 * heads * size * length * length // 2, qkv, qkv),
        name="attention_forward",
    )(segment, gain_q, gain_k, cosine, sine, qkv, qkv, qkv)


def attention_back_kernel(
    segment_ref, gain_q_ref, gain_k_ref, cos_ref, sin_ref, q_ref, k_ref, qs_ref, ks_ref, vs_ref, exact_ref, log_ref,
    do_ref, out_ref, gq_ref, gk_ref, dk_ref, dv_ref, *, docs, window,
):
    size, length = k_ref.shape
    group = q_ref.shape[0] // size
    pair, pairs = pl.program_id(1), pl.num_programs(1)
    cosine, sine = cos_ref[...], sin_ref[...]

    @pl.when((pl.program_id(0) == 0) & (pair == 0))
    def _():
        gq_ref[...] = jnp.zeros_like(gq_ref)
        gk_ref[...] = jnp.zeros_like(gk_ref)

    def fold(terms):
        width = gq_ref.shape[1]
        return sum(terms[:, i : i + width] for i in range(0, length, width))

    same = documents(segment_ref[...], docs, length)
    threes = (lax.broadcasted_iota(jnp.int32, (8, length), 0) < 3).astype(F32)
    keys_t = ks_ref[...]
    keys = jnp.concatenate([keys_t.astype(F32), (same - 1.0) * BLOCKED, threes], axis=0).T.astype(BF16)
    values = jnp.concatenate([vs_ref[...].astype(F32), threes], axis=0).T.astype(BF16)
    allowed = causal(QBLOCK)
    dk_ref[...] = jnp.zeros_like(dk_ref)
    dv_ref[...] = jnp.zeros_like(dv_ref)
    scale = size ** (-0.5)
    for h in range(group):
        rows = pl.ds(h * size, size)
        q_t, do_t = qs_ref[rows, :], do_ref[rows, :]
        do_wide = do_t.astype(F32)
        q_nat = q_t.astype(F32).T.astype(BF16)
        do_nat = do_wide.T.astype(BF16)
        delta = jnp.sum(do_wide * exact_ref[rows, :], axis=0, keepdims=True)
        logs = [-v.astype(F32) for v in split_low(log_ref[0, 0, h : h + 1, :])]
        deltas = [-v.astype(F32) for v in split_low(delta)]
        zeros = jnp.zeros((5, length), F32)
        query = jnp.concatenate(
            [q_t, jnp.concatenate([same] + logs + [zeros], axis=0).astype(BF16)], axis=0
        )
        d_out = jnp.concatenate([do_wide] + deltas + [zeros], axis=0).astype(BF16)
        d_query = []
        for begin in range(0, length, QBLOCK):
            stop = begin + QBLOCK
            d_q = 0.0
            for low, high, diagonal in key_parts(begin, window):
                p = jnp.exp(dot(keys[low:high], query[:, begin:stop], 1, 0))
                if diagonal:
                    p = jnp.where(allowed, p, 0.0)
                ds = (p * dot(values[low:high], d_out[:, begin:stop], 1, 0)).astype(BF16)
                dv_ref[low:high, :] += dot(p.astype(BF16), do_nat[begin:stop], 1, 0)
                dk_ref[low:high, :] += dot(ds, q_nat[begin:stop], 1, 0)
                d_q = d_q + dot(keys_t[:, low:high], ds, 1, 0)
            d_query.append((d_q * scale).astype(BF16).astype(F32))
        d_q0, terms = rope_rows_back(
            jnp.concatenate(d_query, axis=1), q_ref[rows, :], gain_q_ref[...], cosine, sine
        )
        gq_ref[...] += fold(terms)
        out_ref[pl.ds((pair * group + h) * size, size), :] = d_q0.astype(BF16)
    d_key = dk_ref[...].T.astype(BF16).astype(F32)
    d_k0, terms = rope_rows_back(d_key, k_ref[...], gain_k_ref[...], cosine, sine)
    gk_ref[...] += fold(terms)
    out_ref[pl.ds((pairs * group + pair) * size, size), :] = d_k0.astype(BF16)
    out_ref[pl.ds((pairs * (group + 1) + pair) * size, size), :] = dv_ref[...].T.astype(BF16)


def attention_back(qkv, qs, ks, vs, exact, logs, d_out, segment, gain_q, gain_k, cosine, sine, size, group, pairs, docs):
    rows, length = qkv.shape
    per = (group + 2) * size * pairs
    halves = rows // per
    unit = group * size
    q_rows, k_rows = per // unit, per // size
    full = lambda a: pl.BlockSpec(a.shape, lambda i, j: (0,) * a.ndim)
    wide = pl.BlockSpec((unit, length), lambda i, j: (pairs * i + j, 0))
    thin = pl.BlockSpec((size, length), lambda i, j: (pairs * i + j, 0))
    return pl.pallas_call(
        functools.partial(attention_back_kernel, docs=docs, window=length // 2),
        grid=(halves, pairs),
        in_specs=[full(a) for a in (segment, gain_q, gain_k, cosine, sine)]
        + [
            pl.BlockSpec((unit, length), lambda i, j: (q_rows * i + j, 0)),
            pl.BlockSpec((size, length), lambda i, j: (k_rows * i + pairs * group + j, 0)),
            wide, thin, thin, wide,
            pl.BlockSpec((1, 1, group, length), lambda i, j: (i, j, 0, 0)),
            wide,
        ],
        out_specs=[
            pl.BlockSpec((per, length), lambda i, j: (i, 0)),
            pl.BlockSpec((size, 128), lambda i, j: (0, 0)),
            pl.BlockSpec((size, 128), lambda i, j: (0, 0)),
        ],
        out_shape=[
            jax.ShapeDtypeStruct((rows, length), BF16),
            jax.ShapeDtypeStruct((size, 128), F32),
            jax.ShapeDtypeStruct((size, 128), F32),
        ],
        scratch_shapes=[pltpu.VMEM((length, size), F32), pltpu.VMEM((length, size), F32)],
        cost_estimate=cost(80 * rows * length * length // 4, qkv, qkv),
        name="attention_backward",
    )(segment, gain_q, gain_k, cosine, sine, qkv, qkv, qs, ks, vs, exact, logs, d_out)


LANES = 128


def local_block(i, c, blocks):
    return lax.div(i, blocks) * 2 * blocks + c * blocks + lax.rem(i, blocks)


def front_kernel(sel_ref, own_ref, other_ref, gain_ref, query_ref, key_ref, value_ref, normed_ref, out_ref):
    local = own_ref.shape[0]

    @pl.when(pl.program_id(0) == 0)
    def _():
        for i, ref in enumerate((own_ref, other_ref)):
            place = pl.multiple_of((sel_ref[0] if i == 0 else 1 - sel_ref[0]) * local, local)
            v = ref[...].astype(F32)
            v = v * lax.rsqrt(jnp.mean(v * v, axis=-1, keepdims=True) + EPSILON) * gain_ref[...]
            normed_ref[pl.ds(place, local), :] = v.astype(BF16)

    at = 0
    for ref in (query_ref, key_ref, value_ref):
        out_ref[at : at + ref.shape[1], :] = dot(ref[...], normed_ref[...], 0, 1)
        at += ref.shape[1]


def front(sel, own, other, gain, w_query, w_key, w_value):
    local, d = own.shape
    widths = [w.shape[1] // 4 for w in (w_query, w_key, w_value)]
    part = pl.BlockSpec((local, d), lambda j, sel: (0, 0))
    return pl.pallas_call(
        front_kernel,
        grid_spec=pltpu.PrefetchScalarGridSpec(
            num_scalar_prefetch=1,
            grid=(2,),
            in_specs=[part, part, pl.BlockSpec((1, d), lambda j, sel: (0, 0))]
            + [pl.BlockSpec((d, w), lambda j, sel: (0, 2 * j + sel[0])) for w in widths],
            out_specs=[
                pl.BlockSpec((2 * local, d), lambda j, sel: (0, 0)),
                pl.BlockSpec((sum(widths), 2 * local), lambda j, sel: (j, 0)),
            ],
        ),
        out_shape=[
            jax.ShapeDtypeStruct((2 * local, d), BF16),
            jax.ShapeDtypeStruct((2 * sum(widths), 2 * local), F32),
        ],
        cost_estimate=cost(4 * local * d * 2 * sum(widths), own, own, w_query, w_query, w_query),
        name="norm_and_projections",
    )(sel, own, other, gain, w_query, w_key, w_value)


def ffn_kernel(
    sel_ref, hn_ref, own_ref, other_ref, gate0_ref, gate1_ref, up0_ref, up1_ref, down0_ref, down1_ref,
    act_ref, dg_ref, du_ref, gate_leave_ref, up_leave_ref, down_leave_ref, hy1_ref, hz1_ref, dx1_ref, back_ref, low_ref,
    turned_ref, hz0_ref, hy0_ref, dm_ref, dx0_ref,
):
    tokens, d = hn_ref.shape

    @pl.when(pl.program_id(0) == 0)
    def _():
        c, x, y, zl = [sel_ref[i] for i in range(4)]
        local, half, rows = tokens // 2, d // 2, d // 8
        back_ref[...] = jnp.zeros_like(back_ref)
        for i, ref in enumerate((own_ref, other_ref)):
            place = pl.multiple_of((c if i == 0 else 1 - c) * local, local)
            dm_ref[pl.ds(place, local), :] = ref[...]
        turned_ref[...] = hn_ref[...].T
        for order in range(2):
            for i in range(4):
                high, low = divmod(i, 2)
                to = slice(i * rows, (i + 1) * rows)
                block = 4 * high + 2 * (zl if order else 1 - zl) + low
                (hz0_ref, hz1_ref)[order][to, :] = turned_ref[pl.ds(pl.multiple_of(block * rows, rows), rows), :]
                block = 4 * high + 2 * low + (y if order else 1 - y)
                (hy0_ref, hy1_ref)[order][to, :] = turned_ref[pl.ds(pl.multiple_of(block * rows, rows), rows), :]
            place = pl.multiple_of((x if order else 1 - x) * half, half)
            (dx0_ref, dx1_ref)[order][...] = dm_ref[:, pl.ds(place, half)]

    gate_w = jnp.concatenate([gate0_ref[...], gate1_ref[...]], axis=1)
    up_w = jnp.concatenate([up0_ref[...], up1_ref[...]], axis=1)
    down_w = jnp.concatenate([down0_ref[...], down1_ref[...]], axis=0)
    step = min(256, tokens)
    for begin in range(0, tokens, step):
        at = slice(begin, begin + step)
        gate = dot(hn_ref[at, :], gate_w, 1, 0)
        up = dot(hn_ref[at, :], up_w, 1, 0)
        d_act = dot(dm_ref[at, :], down_w, 1, 1)
        sigmoid = 1.0 / (1.0 + jnp.exp(-gate))
        silu = gate * sigmoid
        act_ref[at, :] = (silu * up).astype(BF16)
        du_ref[at, :] = (d_act * silu).astype(BF16)
        dg_ref[at, :] = (d_act * up * (sigmoid + silu * (1.0 - sigmoid))).astype(BF16)
    up_leave_ref[...] = dot(hz0_ref[...], du_ref[...], 1, 0).astype(BF16)
    gate_leave_ref[...] = dot(hy0_ref[...], dg_ref[...], 1, 0).astype(BF16)
    both_w = jnp.concatenate([gate_w, up_w], axis=1)
    for begin in range(0, tokens, step):
        at = slice(begin, begin + step)
        back_ref[at, :] += dot(jnp.concatenate([dg_ref[at, :], du_ref[at, :]], axis=1), both_w, 1, 1)
    down_leave_ref[...] = dot(act_ref[...].T, dx0_ref[...], 1, 0).astype(BF16)

    @pl.when(pl.program_id(0) == pl.num_programs(0) - 1)
    def _():
        low_ref[...] = back_ref[...].astype(BF16)


def feed_forward(sel, hnormed, d_own, d_other, w_gate, w_up, w_down):
    tokens, d = hnormed.shape
    units = w_gate.shape[1] // 2
    blocks = units // 2 // LANES
    block = 2 * LANES
    whole = pl.BlockSpec((tokens, d), lambda j, sel: (0, 0))
    part = pl.BlockSpec((tokens // 2, d), lambda j, sel: (0, 0))
    columns = [
        pl.BlockSpec((d, LANES), lambda j, sel, i=i: (0, local_block(2 * j + i, sel[0], blocks))) for i in range(2)
    ]
    rows = [pl.BlockSpec((LANES, d), lambda j, sel, i=i: (local_block(2 * j + i, sel[0], blocks), 0)) for i in range(2)]
    return pl.pallas_call(
        ffn_kernel,
        grid_spec=pltpu.PrefetchScalarGridSpec(
            num_scalar_prefetch=1,
            grid=(units // block,),
            in_specs=[whole, part, part] + columns + columns + rows,
            out_specs=[pl.BlockSpec((tokens, block), lambda j, sel: (0, j))] * 3
            + [pl.BlockSpec((d // 2, block), lambda j, sel: (0, j))] * 2
            + [pl.BlockSpec((block, d // 2), lambda j, sel: (j, 0))]
            + [pl.BlockSpec((d // 2, tokens), lambda j, sel: (0, 0))] * 2
            + [pl.BlockSpec((tokens, d // 2), lambda j, sel: (0, 0))]
            + [whole, whole],
            scratch_shapes=[pltpu.VMEM((d, tokens), BF16)]
            + [pltpu.VMEM((d // 2, tokens), BF16)] * 2
            + [pltpu.VMEM((tokens, d), BF16), pltpu.VMEM((tokens, d // 2), BF16)],
        ),
        out_shape=[jax.ShapeDtypeStruct((tokens, units), BF16)] * 3
        + [jax.ShapeDtypeStruct((d // 2, units), BF16)] * 2
        + [jax.ShapeDtypeStruct((units, d // 2), BF16)]
        + [jax.ShapeDtypeStruct((d // 2, tokens), BF16)] * 2
        + [jax.ShapeDtypeStruct((tokens, d // 2), BF16)]
        + [jax.ShapeDtypeStruct((tokens, d), t) for t in (F32, BF16)],
        name="feed_forward",
    )(sel, hnormed, d_own, d_other, w_gate, w_gate, w_up, w_up, w_down, w_down)


def ffn_grads_kernel(act_ref, dg_ref, du_ref, hn_y_ref, hn_z_ref, dm_ref, gate_ref, up_ref, down_ref):
    up_ref[...] = dot(hn_z_ref[...], du_ref[...], 1, 0).astype(BF16)
    gate_ref[...] = dot(hn_y_ref[...], dg_ref[...], 1, 0).astype(BF16)
    down_ref[...] = dot(act_ref[...].T, dm_ref[...], 1, 0).astype(BF16)


def ffn_grads(act, d_gate, d_up, hn_y, hn_z, dm_x):
    tokens, units = act.shape
    half = hn_y.shape[0]
    block = 2 * LANES
    columns = pl.BlockSpec((tokens, block), lambda j: (0, j))
    turned = pl.BlockSpec((half, tokens), lambda j: (0, 0))
    out = pl.BlockSpec((half, block), lambda j: (0, j))
    return pl.pallas_call(
        ffn_grads_kernel,
        grid=(units // block,),
        in_specs=[columns] * 3 + [turned] * 2 + [pl.BlockSpec((tokens, half), lambda j: (0, 0))],
        out_specs=[out, out, pl.BlockSpec((block, half), lambda j: (j, 0))],
        out_shape=[jax.ShapeDtypeStruct((half, units), BF16)] * 2 + [jax.ShapeDtypeStruct((units, half), BF16)],
        cost_estimate=cost(2 * tokens * half * units, act),
        name="feed_forward_gradients",
    )(act, d_gate, d_up, hn_y, hn_z, dm_x)


def ffn_out_kernel(sel_ref, act_ref, down0_ref, down1_ref, own_ref, low_ref):
    local = own_ref.shape[0]
    down_w = jnp.concatenate([down0_ref[...], down1_ref[...]], axis=0)
    own_ref[...] = dot(act_ref[pl.ds(pl.multiple_of(sel_ref[0] * local, local), local), :], down_w, 1, 0)
    other = act_ref[pl.ds(pl.multiple_of((1 - sel_ref[0]) * local, local), local), :]
    low_ref[...] = dot(other, down_w, 1, 0).astype(BF16)


def ffn_out(sel, act, w_down):
    tokens, units = act.shape
    d = w_down.shape[1]
    block = min(256, d)
    weights = [pl.BlockSpec((units // 2, block), lambda j, sel, i=i: (2 * i + sel[0], j)) for i in range(2)]
    return pl.pallas_call(
        ffn_out_kernel,
        grid_spec=pltpu.PrefetchScalarGridSpec(
            num_scalar_prefetch=1,
            grid=(d // block,),
            in_specs=[pl.BlockSpec((tokens, units), lambda j, sel: (0, 0))] + weights,
            out_specs=[pl.BlockSpec((tokens // 2, block), lambda j, sel: (0, j))] * 2,
        ),
        out_shape=[jax.ShapeDtypeStruct((tokens // 2, d), t) for t in (F32, BF16)],
        cost_estimate=pl.CostEstimate(flops=10**9, transcendentals=0, bytes_accessed=1),
        name="feed_forward_out",
    )(sel, act, w_down, w_down)


def tie(values, *others):
    return lax.optimization_barrier((tuple(values), others))[0]


def cost(flops, *arrays):
    return pl.CostEstimate(flops=flops, transcendentals=0, bytes_accessed=sum(a.size * a.dtype.itemsize for a in arrays))


def add_up(terms):
    return sum(t.astype(F32) for t in terms)


def leave(terms, dim, bit):
    size = terms[0].shape[dim] // 2
    if dim < terms[0].ndim - 2:
        return add_up([lax.dynamic_slice_in_dim(t, (1 - bit) * size, size, dim) for t in terms]).astype(BF16)
    low = add_up([lax.slice_in_dim(t, 0, size, axis=dim) for t in terms])
    high = add_up([lax.slice_in_dim(t, size, 2 * size, axis=dim) for t in terms])
    return pick(bit, high, low).astype(BF16)


def stay(terms, dim, bit):
    size = terms[0].shape[dim] // 2 if terms else 0
    if terms and dim < terms[0].ndim - 2:
        return [lax.dynamic_slice_in_dim(t, bit * size, size, dim) for t in terms]
    return [
        pick(bit, lax.slice_in_dim(t, 0, size, axis=dim), lax.slice_in_dim(t, size, 2 * size, axis=dim))
        for t in terms
    ]


def halve(terms, axis, dim):
    bit = lax.axis_index(axis)
    return stay(terms, dim, bit) + [swap(leave(terms, dim, bit), axis)]


def share_rows(total, c):
    rows = total.shape[0] // 2
    own = pick(c, total[:rows], total[rows:])
    other = swap(pick(c, total[rows:], total[:rows]).astype(BF16), "c").astype(F32)
    return in_order(c, own, other, 1)


def own_rows(v, c, local):
    return pick(c, v[:local], v[local:])


def pair_body(
    tokens, cotangent, doc_lengths, attn_gain, w_query, w_key, w_value, query_gain, key_gain, w_out,
    ffn_gain, w_gate, w_up, w_down,
):
    local, d = tokens.shape[1:]
    length = 2 * local
    size = query_gain.shape[0]
    kv_count = w_key.shape[1] // size
    group = w_query.shape[1] // w_key.shape[1]
    pairs = kv_count // 4
    zh, zl, y, c, x = [lax.axis_index(a) for a in AXES]
    gain_attn = attn_gain.astype(F32)
    gain_ffn = ffn_gain.astype(F32)
    gain_q = query_gain.astype(F32)[:, None]
    gain_k = key_gain.astype(F32)[:, None]

    own_tokens = transpose_pair(tokens[0])
    lengths = jnp.where(c == x, doc_lengths[0], swap(doc_lengths[0], "c"))
    ends = jnp.cumsum(lengths)
    positions = jnp.arange(length, dtype=jnp.int32)
    segment = jnp.sum((ends[:, None] <= positions[None, :]).astype(jnp.int32), axis=0, keepdims=True)
    half = size // 2
    spread = jnp.exp(jnp.arange(half, dtype=F32) * (-2.0 * math.log(1000000.0) / size))
    angles = spread[:, None] * positions.astype(F32)[None, :]
    cosine, sine = jnp.cos(angles), jnp.sin(angles)
    parts = [part_columns(w, c) for w in (w_query, w_key, w_value)]
    w_qkv = jnp.concatenate([p[i] for i in range(2) for p in parts], axis=1)
    out_w = part_rows(w_out, c)
    sel = jnp.stack([c, x, y, zl]).astype(jnp.int32)
    w_qkv, out_w, cosine, sine, sel, own_tokens = tie((w_qkv, out_w, cosine, sine, sel, own_tokens))
    other_tokens = swap(own_tokens, "c")
    cot_low, other_tokens = tie((cotangent[0], other_tokens))
    own_cot = transpose_pair(cot_low)
    normed, qkv = front(sel, own_tokens, other_tokens, gain_attn[None], w_query, w_key, w_value)
    docs = doc_lengths.shape[1]
    attended_own, exact, logs, qs, ks, vs = attention(
        qkv, segment, gain_q, gain_k, cosine, sine, size, group, pairs, docs
    )
    attended_own, own_cot = tie((attended_own, own_cot))
    attended_other = swap(attended_own, "c")
    other_cot = swap(own_cot, "c")
    width = attended_own.shape[0] // 2
    attended = jnp.concatenate(
        [in_order(c, attended_own[i : i + width], attended_other[i : i + width], 0) for i in (0, width)], axis=0
    )
    inputs = in_order(c, own_tokens, other_tokens, 0).astype(F32)
    hidden = inputs + dot(attended, w_out, 0, 0)
    hnormed = rms_scale(hidden, gain_ffn).astype(BF16)

    act, d_gate, d_up, send_gate, send_up, send_down, hn_y, hn_z, dm_x, d_hn, d_hn_low = feed_forward(
        sel, hnormed, own_cot, other_cot, w_gate, w_up, w_down
    )
    come_up, come_down, come_gate = swap(send_up, "zl"), swap(send_down, "x"), swap(send_gate, "y")
    d_hn_other = swap(d_hn_low, "c")
    keep_gate, keep_up, keep_down = ffn_grads(act, d_gate, d_up, hn_y, hn_z, dm_x)
    units = d_gate.shape[1]
    rows = d // 8
    half = d // 2
    (d_hn_other,) = tie((d_hn_other,), keep_up, keep_gate, keep_down)
    d_hn = d_hn + d_hn_other.astype(F32)
    d_hidden_norm, ffn_gain_terms = norm_back(d_hn, hidden, gain_ffn)
    d_hidden = in_order(c, own_cot, other_cot, 0).astype(F32) + d_hidden_norm
    d_attn = d_hidden.astype(BF16)
    d_attended = dot(out_w, d_attn, 1, 1).astype(BF16)

    quarter = d // 4
    send_out, keep_out = [
        dot(attended, lax.dynamic_slice_in_dim(d_attn, (2 * i + c) * quarter, quarter, 1), 1, 0).astype(BF16)
        for i in (1 - x, x)
    ]
    come_out = swap(send_out, "x")
    act, d_attended = tie((act, d_attended), send_out, keep_out)
    part_out, out_low = ffn_out(sel, act, w_down)

    come_up, come_down, come_gate, part_out, out_low, d_attended = tie(
        (come_up, come_down, come_gate, part_out, out_low, d_attended)
    )
    up = [v.reshape(2, 2, rows, units) for v in (come_up, keep_up)]
    down = [v.reshape(2, 2, units // 4, half) for v in (come_down, keep_down)]
    gate = [v.reshape(2, 2, rows, units) for v in (come_gate, keep_gate)]
    send_gate, send_down, send_up = leave(gate, 1, zl), leave(down, 1, y), leave(up, 3, x)
    gate = stay(gate, 1, zl) + [swap(send_gate, "zl")]
    down = stay(down, 1, y) + [swap(send_down, "y")]
    up = stay(up, 3, x) + [swap(send_up, "x")]
    come_out, d_attended, out_low = tie((come_out, d_attended, out_low), send_gate, send_down, send_up)
    out_other = swap(out_low, "c")
    d_qkv, gain_q_terms, gain_k_terms = attention_back(
        qkv, qs, ks, vs, exact, logs, d_attended, segment, gain_q, gain_k, cosine, sine, size, group, pairs, docs
    )
    d_qkv, out_other = tie((d_qkv, out_other))
    width = d_qkv.shape[0] // 2
    send_qkv = dot(normed, lax.dynamic_slice_in_dim(d_qkv, (1 - x) * width, width, 0), 0, 1).astype(BF16)
    come_qkv = swap(send_qkv, "x")
    (d_qkv,) = tie((d_qkv,), send_qkv)
    part_low = dot(pick(c, d_qkv[:, local:], d_qkv[:, :local]), w_qkv, 0, 1).astype(BF16)
    part_other = swap(part_low, "c")
    (d_qkv,) = tie((d_qkv,), part_low)
    part = dot(pick(c, d_qkv[:, :local], d_qkv[:, local:]), w_qkv, 0, 1)
    keep_qkv = dot(normed, lax.dynamic_slice_in_dim(d_qkv, x * width, width, 0), 0, 1).astype(BF16)

    gate[-1], down[-1], up[-1], part_other = tie((gate[-1], down[-1], up[-1], part_other), part, keep_qkv)
    send_gate, send_down, send_up = leave(gate, 3, x), add_up(down).astype(BF16), leave(up, 1, y)
    gate = stay(gate, 3, x) + [swap(send_gate, "x")]
    down = down + [lax.ppermute(send_down, ("zl", "c"), [(2, 0), (1, 3)])]
    up = stay(up, 1, y) + [swap(send_up, "y")]
    (part_other,) = tie((part_other,), send_gate, send_down, send_up)
    d_normed = part + part_other.astype(F32)
    d_input_norm, attn_gain_terms = norm_back(d_normed, own_tokens.astype(F32), gain_attn)
    d_inputs = own_rows(d_hidden, c, local) + d_input_norm
    gains = jnp.concatenate(
        [
            jnp.sum(attn_gain_terms, axis=0),
            jnp.sum(ffn_gain_terms, axis=0) * 0.5,
            jnp.sum(gain_q_terms, axis=1),
            jnp.sum(gain_k_terms, axis=1),
        ]
    ).reshape(-1, 128)
    reached = swap(gains, "zh")
    output = own_rows(hidden, c, local) + part_out + out_other.astype(F32)
    results = jnp.concatenate([output.astype(BF16), d_inputs.astype(BF16)], axis=0)

    def joined(parts):
        first, second, joint = parts
        return add_up([jnp.concatenate([add_up(first), add_up(second)], axis=-1)] + joint)

    def next_stage(parts, axis, dim):
        bit = lax.axis_index(axis)
        come = swap(joined([stay(p, dim, 1 - bit) for p in parts]).astype(BF16), axis)
        first, second, joint = [stay(p, dim, bit) for p in parts]
        return first, second, joint + [come]

    gate[-1], down[-1], up[-1], come_qkv, reached, results = tie(
        (gate[-1], down[-1], up[-1], come_qkv, reached, results)
    )
    send_gate, send_down, send_up = leave(gate, 0, zh), leave(down, 0, zh), leave(up, 0, zh)
    gate = stay(gate, 0, zh) + [swap(send_gate, "zh")]
    down = stay(down, 0, zh) + [swap(send_down, "zh")]
    up = stay(up, 0, zh) + [swap(send_up, "zh")]
    out = [v.reshape(2, 2, 2, rows, quarter) for v in (come_out, keep_out)]
    qkv_grad = [v.reshape(2, 2, 2, rows, width) for v in (come_qkv, keep_qkv)]
    first, second, joint = next_stage((out, qkv_grad, []), "y", 2)
    gains = gains + reached
    gains = gains + swap(gains, "x")
    results, gains = tie((results, gains))
    results_other = transpose_pair(results)
    joint[-1], gains = tie((joint[-1], gains))
    first, second, joint = next_stage((first, second, joint), "zl", 1)
    gains = gains + swap(gains, "c")
    gains = gains + swap(gains, "y")
    joint[-1], gains = tie((joint[-1], gains))
    first, second, joint = next_stage((first, second, joint), "zh", 0)
    gains = gains + swap(gains, "zl")
    gate[-1], down[-1], up[-1], gains = tie((gate[-1], down[-1], up[-1], gains))

    total = add_up(down).reshape(-1, d // 2)
    n = total.shape[0] // 2
    own = pick(c, total[:n], total[n:])
    other = pick(c, total[n:], total[:n]).astype(BF16)
    other = lax.ppermute(other, ("zl", "c"), [(0, 1), (3, 2)]).astype(F32)
    sum_down = jnp.where(zl == c, own, other)
    sum_gate, sum_up = [share_rows(add_up(t).reshape(rows, units // 2), c) for t in (gate, up)]
    (joint[-1],) = tie((joint[-1],), sum_gate, sum_up, sum_down)
    gains = gains.reshape(-1)
    both = joined((first, second, joint)).reshape(rows, 3 * quarter)
    n = rows // 2
    own = pick(c, both[:n], both[n:])
    other = swap(pick(c, both[n:], both[:n]).astype(BF16), "c").astype(F32)
    first, second = pick(c, own, other), pick(c, other, own)
    q_width, kv_width = pairs * group * size, pairs * size
    ends_of = [0, quarter, quarter + q_width, quarter + q_width + kv_width, quarter + q_width + 2 * kv_width]
    sum_out, sum_query, sum_key, sum_value = [
        jnp.concatenate([first[:, low:high], second[:, low:high]], axis=1)
        for low, high in zip(ends_of[:-1], ends_of[1:])
    ]
    stays = c == x
    output = jnp.where(stays, output, results_other[:local].astype(F32))
    d_inputs = jnp.where(stays, d_inputs, results_other[local:].astype(F32))
    return (
        output[None],
        d_inputs[None],
        gains[:d],
        sum_query,
        sum_key,
        sum_value,
        gains[2 * d : 2 * d + size],
        gains[2 * d + size :],
        sum_out,
        gains[d : 2 * d],
        sum_gate,
        sum_up,
        sum_down,
    )


def solution(mesh):
    rows, shards = mesh.shape["dp"], mesh.shape["seq"]
    if rows == 16 and shards == 2:
        body = pair_body
        mesh = Mesh(mesh.devices.reshape(2, 2, 2, 2, 2), AXES)
        dp, seq = AXES[:4], "x"
    else:
        body = general_body
        dp, seq = "dp", "seq"
    return jax.shard_map(
        body,
        mesh=mesh,
        in_specs=(P(dp, seq, None), P(dp, seq, None), P(dp, None)) + (P(),) * 11,
        out_specs=(P(dp, seq, None), P(dp, seq, None), P())
        + (P(dp, seq),) * 3
        + (P(), P(), P(dp, seq), P())
        + (P(dp, seq),) * 3,
        check_vma=False,
    )
```

```python
import math

import functools

import jax
import jax.numpy as jnp
from jax import lax
from jax.experimental import pallas as pl
from jax.experimental.pallas import tpu as pltpu
from jax.sharding import Mesh
from jax.sharding import PartitionSpec as P

EPSILON = 1e-06


def rms_scale(values, gain):
    return values * lax.rsqrt(jnp.mean(values * values, axis=-1, keepdims=True) + EPSILON) * gain


def norm_back(incoming, values, gain):
    inverse = lax.rsqrt(jnp.mean(values * values, axis=-1, keepdims=True) + EPSILON)
    unit = values * inverse
    scaled = incoming * gain
    d_values = inverse * (scaled - unit * jnp.mean(scaled * unit, axis=-1, keepdims=True))
    return (d_values, incoming * unit)


def rope_tables(first, count, width):
    half = width // 2
    spread = jnp.exp(jnp.arange(half, dtype=jnp.float32) * (-2.0 * math.log(1000000.0) / width))
    places = (first + jnp.arange(count, dtype=jnp.int32)).astype(jnp.float32)
    angles = places[:, None] * spread[None, :]
    return (jnp.cos(angles)[:, None, :], jnp.sin(angles)[:, None, :])


def rotate(values, cosine, sine):
    half = values.shape[-1] // 2
    first_half = values[..., :half]
    second_half = values[..., half:]
    return jnp.concatenate(
        [first_half * cosine - second_half * sine, second_half * cosine + first_half * sine],
        axis=-1,
    )


def reduce_grads(grads):
    partial_sum = lax.psum_scatter(grads, "dp", scatter_dimension=0, tiled=True)
    return lax.psum_scatter(partial_sum, "seq", scatter_dimension=1, tiled=True)


def general_body(
    tokens,
    cotangent,
    doc_lengths,
    attn_gain,
    w_query,
    w_key,
    w_value,
    query_gain,
    key_gain,
    w_out,
    ffn_gain,
    w_gate,
    w_up,
    w_down,
):
    shards = lax.axis_size("seq")
    local = tokens.shape[1]
    length = local * shards
    head_size = query_gain.shape[0]
    kv_count = w_key.shape[1] // head_size
    head_count = w_query.shape[1] // head_size
    group = head_count // kv_count
    kv_local = kv_count // shards
    block = min(512, length)
    num_blocks = length // block
    scale = head_size ** (-0.5)
    f32 = jnp.float32
    bf16 = jnp.bfloat16
    gain_attn = attn_gain.astype(f32)
    gain_query = query_gain.astype(f32)
    gain_key = key_gain.astype(f32)
    gain_ffn = ffn_gain.astype(f32)
    inputs = tokens[0].astype(f32)
    normed = rms_scale(inputs, gain_attn).astype(bf16)
    query_raw = jnp.dot(normed, w_query, preferred_element_type=f32).reshape(
        local, head_count, head_size
    )
    key_raw = jnp.dot(normed, w_key, preferred_element_type=f32).reshape(local, kv_count, head_size)
    values = (
        jnp.dot(normed, w_value, preferred_element_type=f32)
        .astype(bf16)
        .reshape(local, kv_count, head_size)
    )
    cosine, sine = rope_tables(lax.axis_index("seq") * local, local, head_size)
    query_rot = rotate(rms_scale(query_raw, gain_query), cosine, sine).astype(bf16)
    key_rot = rotate(rms_scale(key_raw, gain_key), cosine, sine).astype(bf16)
    packed_query = query_rot.reshape(local, kv_count, group * head_size)
    packed_kv = jnp.concatenate([key_rot, values], axis=2)
    query_heads, kv_heads = (
        lax.all_to_all(packed_query, "seq", split_axis=1, concat_axis=0, tiled=True),
        lax.all_to_all(packed_kv, "seq", split_axis=1, concat_axis=0, tiled=True),
    )
    query_all = query_heads.reshape(length, kv_local, group, head_size)
    key_all = kv_heads[:, :, :head_size]
    value_all = kv_heads[:, :, head_size:]
    positions = jnp.arange(length, dtype=jnp.int32)
    ends = jnp.cumsum(doc_lengths[0])
    segment = jnp.sum((ends[None, :] <= positions[:, None]).astype(jnp.int32), axis=1)
    starts = jnp.arange(num_blocks, dtype=jnp.int32) * block

    def allowed_at(begin):
        rows_here = begin + jnp.arange(block, dtype=jnp.int32)
        query_seg = lax.dynamic_slice_in_dim(segment, begin, block, 0)
        return (query_seg[:, None] == segment[None, :]) & (positions[None, :] <= rows_here[:, None])

    def block_scores(begin):
        query_block = lax.dynamic_slice_in_dim(query_all, begin, block, 0)
        scores = (
            jnp.einsum("qhgd,khd->hgqk", query_block, key_all, preferred_element_type=f32) * scale
        )
        return (query_block, jnp.where(allowed_at(begin), scores, -jnp.inf))

    def attend(begin):
        query_block, scores = block_scores(begin)
        top_score = jnp.max(scores, axis=-1, keepdims=True)
        expos = jnp.exp(scores - top_score)
        totals = jnp.sum(expos, axis=-1, keepdims=True)
        probs = (expos / totals).astype(bf16)
        result = jnp.einsum("hgqk,khd->qhgd", probs, value_all, preferred_element_type=f32)
        return (result.astype(bf16), top_score[..., 0] + jnp.log(totals[..., 0]))

    attended_heads, log_totals = lax.map(attend, starts)
    attended_heads = attended_heads.reshape(length, kv_local, group * head_size)
    attended = lax.all_to_all(
        attended_heads, "seq", split_axis=0, concat_axis=1, tiled=True
    ).reshape(local, head_count * head_size)
    hidden = inputs + jnp.dot(attended, w_out, preferred_element_type=f32)
    hnormed = rms_scale(hidden, gain_ffn).astype(bf16)
    gate = jnp.dot(hnormed, w_gate, preferred_element_type=f32)
    up_part = jnp.dot(hnormed, w_up, preferred_element_type=f32)
    act = (jax.nn.silu(gate) * up_part).astype(bf16)
    output = hidden + jnp.dot(act, w_down, preferred_element_type=f32)
    d_mlp = cotangent[0]
    grad_down = jnp.einsum("tf,td->fd", act, d_mlp, preferred_element_type=f32)
    d_act = jnp.einsum("td,fd->tf", d_mlp, w_down, preferred_element_type=f32)
    gate_again = jnp.dot(hnormed, w_gate, preferred_element_type=f32)
    up_again = jnp.dot(hnormed, w_up, preferred_element_type=f32)
    sigmoid_gate = jax.nn.sigmoid(gate_again)
    d_up = (d_act * gate_again * sigmoid_gate).astype(bf16)
    d_gate = (d_act * up_again * sigmoid_gate * (1.0 + gate_again * (1.0 - sigmoid_gate))).astype(
        bf16
    )
    grad_gate = jnp.einsum("td,tf->df", hnormed, d_gate, preferred_element_type=f32)
    grad_up = jnp.einsum("td,tf->df", hnormed, d_up, preferred_element_type=f32)
    ffn_sums = reduce_grads((grad_gate, grad_up, grad_down))
    d_hnormed = jnp.einsum("tf,df->td", d_gate, w_gate, preferred_element_type=f32) + jnp.einsum(
        "tf,df->td", d_up, w_up, preferred_element_type=f32
    )
    d_hidden_norm, ffn_gain_terms = norm_back(d_hnormed, hidden, gain_ffn)
    d_hidden = cotangent[0].astype(f32) + d_hidden_norm
    d_attn = d_hidden.astype(bf16)
    grad_out = jnp.einsum("tf,td->fd", attended, d_attn, preferred_element_type=f32)
    d_attended = jnp.einsum("td,fd->tf", d_attn, w_out, preferred_element_type=f32).astype(bf16)
    d_heads = lax.all_to_all(
        d_attended.reshape(local, kv_count, group * head_size),
        "seq",
        split_axis=1,
        concat_axis=0,
        tiled=True,
    )
    d_all = d_heads.reshape(length, kv_local, group, head_size)

    def attend_back(carry, item):
        begin, log_block = item
        query_block, scores = block_scores(begin)
        probs = jnp.exp(scores - log_block[..., None])
        d_block = lax.dynamic_slice_in_dim(d_all, begin, block, 0)
        d_probs = jnp.einsum("qhgd,khd->hgqk", d_block, value_all, preferred_element_type=f32)
        delta = jnp.sum(probs * d_probs, axis=-1, keepdims=True)
        d_scores = (scale * (probs * (d_probs - delta))).astype(bf16)
        d_query_block = jnp.einsum("hgqk,khd->qhgd", d_scores, key_all, preferred_element_type=f32)
        key_total = carry[0] + jnp.einsum(
            "hgqk,qhgd->khd", d_scores, query_block, preferred_element_type=f32
        )
        value_total = carry[1] + jnp.einsum(
            "hgqk,qhgd->khd", probs.astype(bf16), d_block, preferred_element_type=f32
        )
        return ((key_total, value_total), d_query_block.astype(bf16))

    empty = jnp.zeros((length, kv_local, head_size), f32)
    (d_keys, d_values), d_queries = lax.scan(attend_back, (empty, empty), (starts, log_totals))
    d_queries = d_queries.reshape(length, kv_local, group * head_size)
    d_kv = jnp.concatenate([d_keys.astype(bf16), d_values.astype(bf16)], axis=2)
    d_query_pos, d_kv_pos = (
        lax.all_to_all(d_queries, "seq", split_axis=0, concat_axis=1, tiled=True),
        lax.all_to_all(d_kv, "seq", split_axis=0, concat_axis=1, tiled=True),
    )
    d_query_rot = d_query_pos.reshape(local, head_count, head_size).astype(f32)
    d_query_raw, query_gain_terms = norm_back(
        rotate(d_query_rot, cosine, -sine), query_raw, gain_query
    )
    d_query_low = d_query_raw.reshape(local, head_count * head_size).astype(bf16)
    d_key_rot = d_kv_pos[:, :, :head_size].astype(f32)
    d_key_raw, key_gain_terms = norm_back(rotate(d_key_rot, cosine, -sine), key_raw, gain_key)
    d_key_low = d_key_raw.reshape(local, kv_count * head_size).astype(bf16)
    d_value_low = d_kv_pos[:, :, head_size:].reshape(local, kv_count * head_size)
    grad_query = jnp.einsum("td,tf->df", normed, d_query_low, preferred_element_type=f32)
    grad_key = jnp.einsum("td,tf->df", normed, d_key_low, preferred_element_type=f32)
    grad_value = jnp.einsum("td,tf->df", normed, d_value_low, preferred_element_type=f32)
    d_normed = jnp.einsum("tf,df->td", d_query_low, w_query, preferred_element_type=f32)
    d_normed = d_normed + jnp.einsum("tf,df->td", d_key_low, w_key, preferred_element_type=f32)
    d_normed = d_normed + jnp.einsum("tf,df->td", d_value_low, w_value, preferred_element_type=f32)
    d_input_norm, attn_gain_terms = norm_back(d_normed, inputs, gain_attn)
    d_inputs = d_hidden + d_input_norm
    attn_sums = reduce_grads((grad_query, grad_key, grad_value, grad_out))
    gain_totals = lax.psum(
        (
            jnp.sum(attn_gain_terms, axis=0),
            jnp.sum(query_gain_terms, axis=(0, 1)),
            jnp.sum(key_gain_terms, axis=(0, 1)),
            jnp.sum(ffn_gain_terms, axis=0),
        ),
        ("dp", "seq"),
    )
    return (
        output[None],
        d_inputs[None],
        gain_totals[0],
        attn_sums[0],
        attn_sums[1],
        attn_sums[2],
        gain_totals[1],
        gain_totals[2],
        attn_sums[3],
        gain_totals[3],
        ffn_sums[0],
        ffn_sums[1],
        ffn_sums[2],
    )


AXES = ("zh", "zl", "y", "c", "x")
QBLOCK = 256
F32 = jnp.float32
BF16 = jnp.bfloat16


def swap(v, axis):
    return lax.ppermute(v, axis, [(0, 1), (1, 0)])


def transpose_pair(v):
    return lax.ppermute(v, ("c", "x"), [(1, 2), (2, 1)])


def pick(bit, low, high):
    return jnp.where(bit == 0, low, high)


def in_order(bit, own, other, axis):
    return jnp.concatenate([pick(bit, own, other), pick(bit, other, own)], axis=axis)


def dot(left, right, left_dim, right_dim):
    return lax.dot_general(
        left, right, (((left_dim,), (right_dim,)), ((), ())), preferred_element_type=F32
    )


def part_columns(w, c):
    width = w.shape[1] // 4
    return [lax.dynamic_slice_in_dim(w, (2 * i + c) * width, width, 1) for i in range(2)]


def part_rows(w, c):
    rows, columns = w.shape
    return lax.dynamic_index_in_dim(w.reshape(2, 2, rows // 4, columns), c, 1, False).reshape(rows // 2, columns)


def rope_rows(values, gain, cosine, sine):
    unit = values * lax.rsqrt(jnp.mean(values * values, axis=0, keepdims=True) + EPSILON) * gain
    half = values.shape[0] // 2
    first, second = unit[:half], unit[half:]
    return jnp.concatenate([first * cosine - second * sine, second * cosine + first * sine], axis=0)


def rope_rows_back(incoming, values, gain, cosine, sine):
    half = values.shape[0] // 2
    first, second = incoming[:half], incoming[half:]
    turned = jnp.concatenate([first * cosine + second * sine, second * cosine - first * sine], axis=0)
    inverse = lax.rsqrt(jnp.mean(values * values, axis=0, keepdims=True) + EPSILON)
    unit = values * inverse
    scaled = turned * gain
    d_values = inverse * (scaled - unit * jnp.mean(scaled * unit, axis=0, keepdims=True))
    return d_values, turned * unit


BLOCKED = 256.0


def split_low(v):
    high = v.astype(BF16)
    rest = v - high.astype(F32)
    middle = rest.astype(BF16)
    return [high, middle, (rest - middle.astype(F32)).astype(BF16)]


def documents(segment, rows, length):
    return (segment == lax.broadcasted_iota(jnp.int32, (rows, length), 0)).astype(F32)


def key_parts(begin, window):
    low = max(0, begin - (window - 1)) // QBLOCK * QBLOCK
    return ([(low, begin, False)] if begin > low else []) + [(begin, begin + QBLOCK, True)]


def causal(block):
    key_at = lax.broadcasted_iota(jnp.int32, (block, block), 0)
    return key_at <= lax.broadcasted_iota(jnp.int32, (block, block), 1)


def attention_kernel(
    segment_ref, gain_q_ref, gain_k_ref, cos_ref, sin_ref, q_ref, k_ref, v_ref,
    out_ref, exact_ref, log_ref, qs_ref, ks_ref, vs_ref, *, docs, window,
):
    size, length = k_ref.shape
    group = q_ref.shape[0] // size
    cosine, sine = cos_ref[...], sin_ref[...]
    same = documents(segment_ref[...], docs, length)
    k_rot = rope_rows(k_ref[...], gain_k_ref[...], cosine, sine)
    ks_ref[...] = k_rot.astype(BF16)
    keys = jnp.concatenate([k_rot, (same - 1.0) * BLOCKED], axis=0).T.astype(BF16)
    values = v_ref[...].astype(BF16)
    vs_ref[...] = values
    ones = (lax.broadcasted_iota(jnp.int32, (16, length), 0) == 0).astype(BF16)
    values = jnp.concatenate([values, ones], axis=0)
    allowed = causal(QBLOCK)
    for h in range(group):
        rows = pl.ds(h * size, size)
        q_rot = rope_rows(q_ref[rows, :], gain_q_ref[...], cosine, sine).astype(BF16)
        q_rot = q_rot * jnp.asarray(size ** (-0.5), BF16)
        qs_ref[rows, :] = q_rot
        query = jnp.concatenate([q_rot, same.astype(BF16)], axis=0)
        for begin in range(0, length, QBLOCK):
            stop = begin + QBLOCK
            result = 0.0
            for low, high, diagonal in key_parts(begin, window):
                e = jnp.exp(dot(keys[low:high], query[:, begin:stop], 1, 0))
                if diagonal:
                    e = jnp.where(allowed, e, 0.0)
                result = result + dot(values[:, low:high], e.astype(BF16), 1, 0)
            total = result[size : size + 1]
            result = result[:size] / total
            exact_ref[rows, begin:stop] = result
            out_ref[rows, begin:stop] = result.astype(BF16)
            log_ref[0, 0, h : h + 1, begin:stop] = jnp.log(total)


def attention(qkv, segment, gain_q, gain_k, cosine, sine, size, group, pairs, docs):
    rows, length = qkv.shape
    per = (group + 2) * size * pairs
    halves = rows // per
    unit = group * size
    q_rows, k_rows = per // unit, per // size
    full = lambda a: pl.BlockSpec(a.shape, lambda i, j: (0,) * a.ndim)
    wide = pl.BlockSpec((unit, length), lambda i, j: (pairs * i + j, 0))
    thin = pl.BlockSpec((size, length), lambda i, j: (pairs * i + j, 0))
    heads = halves * pairs * group
    return pl.pallas_call(
        functools.partial(attention_kernel, docs=docs, window=length // 2),
        grid=(halves, pairs),
        in_specs=[full(a) for a in (segment, gain_q, gain_k, cosine, sine)]
        + [
            pl.BlockSpec((unit, length), lambda i, j: (q_rows * i + j, 0)),
            pl.BlockSpec((size, length), lambda i, j: (k_rows * i + pairs * group + j, 0)),
            pl.BlockSpec((size, length), lambda i, j: (k_rows * i + pairs * (group + 1) + j, 0)),
        ],
        out_specs=[
            wide, wide, pl.BlockSpec((1, 1, group, length), lambda i, j: (i, j, 0, 0)), wide, thin, thin,
        ],
        out_shape=[
            jax.ShapeDtypeStruct((heads * size, length), BF16),
            jax.ShapeDtypeStruct((heads * size, length), F32),
            jax.ShapeDtypeStruct((halves, pairs, group, length), F32),
            jax.ShapeDtypeStruct((heads * size, length), BF16),
            jax.ShapeDtypeStruct((halves * pairs * size, length), BF16),
            jax.ShapeDtypeStruct((halves * pairs * size, length), BF16),
        ],
        cost_estimate=cost(40 * heads * size * length * length // 2, qkv, qkv),
        name="attention_forward",
    )(segment, gain_q, gain_k, cosine, sine, qkv, qkv, qkv)


def attention_back_kernel(
    segment_ref, gain_q_ref, gain_k_ref, cos_ref, sin_ref, q_ref, k_ref, qs_ref, ks_ref, vs_ref, exact_ref, log_ref,
    do_ref, out_ref, gq_ref, gk_ref, dk_ref, dv_ref, *, docs, window,
):
    size, length = k_ref.shape
    group = q_ref.shape[0] // size
    pair, pairs = pl.program_id(1), pl.num_programs(1)
    cosine, sine = cos_ref[...], sin_ref[...]

    @pl.when((pl.program_id(0) == 0) & (pair == 0))
    def _():
        gq_ref[...] = jnp.zeros_like(gq_ref)
        gk_ref[...] = jnp.zeros_like(gk_ref)

    def fold(terms):
        width = gq_ref.shape[1]
        return sum(terms[:, i : i + width] for i in range(0, length, width))

    same = documents(segment_ref[...], docs, length)
    threes = (lax.broadcasted_iota(jnp.int32, (8, length), 0) < 3).astype(F32)
    keys_t = ks_ref[...]
    keys = jnp.concatenate([keys_t.astype(F32), (same - 1.0) * BLOCKED, threes], axis=0).T.astype(BF16)
    values = jnp.concatenate([vs_ref[...].astype(F32), threes], axis=0).T.astype(BF16)
    allowed = causal(QBLOCK)
    dk_ref[...] = jnp.zeros_like(dk_ref)
    dv_ref[...] = jnp.zeros_like(dv_ref)
    scale = size ** (-0.5)
    for h in range(group):
        rows = pl.ds(h * size, size)
        q_t, do_t = qs_ref[rows, :], do_ref[rows, :]
        do_wide = do_t.astype(F32)
        q_nat = q_t.astype(F32).T.astype(BF16)
        do_nat = do_wide.T.astype(BF16)
        delta = jnp.sum(do_wide * exact_ref[rows, :], axis=0, keepdims=True)
        logs = [-v.astype(F32) for v in split_low(log_ref[0, 0, h : h + 1, :])]
        deltas = [-v.astype(F32) for v in split_low(delta)]
        zeros = jnp.zeros((5, length), F32)
        query = jnp.concatenate(
            [q_t, jnp.concatenate([same] + logs + [zeros], axis=0).astype(BF16)], axis=0
        )
        d_out = jnp.concatenate([do_wide] + deltas + [zeros], axis=0).astype(BF16)
        d_query = []
        for begin in range(0, length, QBLOCK):
            stop = begin + QBLOCK
            d_q = 0.0
            for low, high, diagonal in key_parts(begin, window):
                p = jnp.exp(dot(keys[low:high], query[:, begin:stop], 1, 0))
                if diagonal:
                    p = jnp.where(allowed, p, 0.0)
                ds = (p * dot(values[low:high], d_out[:, begin:stop], 1, 0)).astype(BF16)
                dv_ref[low:high, :] += dot(p.astype(BF16), do_nat[begin:stop], 1, 0)
                dk_ref[low:high, :] += dot(ds, q_nat[begin:stop], 1, 0)
                d_q = d_q + dot(keys_t[:, low:high], ds, 1, 0)
            d_query.append((d_q * scale).astype(BF16).astype(F32))
        d_q0, terms = rope_rows_back(
            jnp.concatenate(d_query, axis=1), q_ref[rows, :], gain_q_ref[...], cosine, sine
        )
        gq_ref[...] += fold(terms)
        out_ref[pl.ds((pair * group + h) * size, size), :] = d_q0.astype(BF16)
    d_key = dk_ref[...].T.astype(BF16).astype(F32)
    d_k0, terms = rope_rows_back(d_key, k_ref[...], gain_k_ref[...], cosine, sine)
    gk_ref[...] += fold(terms)
    out_ref[pl.ds((pairs * group + pair) * size, size), :] = d_k0.astype(BF16)
    out_ref[pl.ds((pairs * (group + 1) + pair) * size, size), :] = dv_ref[...].T.astype(BF16)


def attention_back(qkv, qs, ks, vs, exact, logs, d_out, segment, gain_q, gain_k, cosine, sine, size, group, pairs, docs):
    rows, length = qkv.shape
    per = (group + 2) * size * pairs
    halves = rows // per
    unit = group * size
    q_rows, k_rows = per // unit, per // size
    full = lambda a: pl.BlockSpec(a.shape, lambda i, j: (0,) * a.ndim)
    wide = pl.BlockSpec((unit, length), lambda i, j: (pairs * i + j, 0))
    thin = pl.BlockSpec((size, length), lambda i, j: (pairs * i + j, 0))
    return pl.pallas_call(
        functools.partial(attention_back_kernel, docs=docs, window=length // 2),
        grid=(halves, pairs),
        in_specs=[full(a) for a in (segment, gain_q, gain_k, cosine, sine)]
        + [
            pl.BlockSpec((unit, length), lambda i, j: (q_rows * i + j, 0)),
            pl.BlockSpec((size, length), lambda i, j: (k_rows * i + pairs * group + j, 0)),
            wide, thin, thin, wide,
            pl.BlockSpec((1, 1, group, length), lambda i, j: (i, j, 0, 0)),
            wide,
        ],
        out_specs=[
            pl.BlockSpec((per, length), lambda i, j: (i, 0)),
            pl.BlockSpec((size, 128), lambda i, j: (0, 0)),
            pl.BlockSpec((size, 128), lambda i, j: (0, 0)),
        ],
        out_shape=[
            jax.ShapeDtypeStruct((rows, length), BF16),
            jax.ShapeDtypeStruct((size, 128), F32),
            jax.ShapeDtypeStruct((size, 128), F32),
        ],
        scratch_shapes=[pltpu.VMEM((length, size), F32), pltpu.VMEM((length, size), F32)],
        cost_estimate=cost(80 * rows * length * length // 4, qkv, qkv),
        name="attention_backward",
    )(segment, gain_q, gain_k, cosine, sine, qkv, qkv, qs, ks, vs, exact, logs, d_out)


LANES = 128


def local_block(i, c, blocks):
    return lax.div(i, blocks) * 2 * blocks + c * blocks + lax.rem(i, blocks)


def front_kernel(sel_ref, own_ref, other_ref, gain_ref, query_ref, key_ref, value_ref, normed_ref, out_ref):
    local = own_ref.shape[0]

    @pl.when(pl.program_id(0) == 0)
    def _():
        for i, ref in enumerate((own_ref, other_ref)):
            place = pl.multiple_of((sel_ref[0] if i == 0 else 1 - sel_ref[0]) * local, local)
            v = ref[...].astype(F32)
            v = v * lax.rsqrt(jnp.mean(v * v, axis=-1, keepdims=True) + EPSILON) * gain_ref[...]
            normed_ref[pl.ds(place, local), :] = v.astype(BF16)

    at = 0
    for ref in (query_ref, key_ref, value_ref):
        out_ref[at : at + ref.shape[1], :] = dot(ref[...], normed_ref[...], 0, 1)
        at += ref.shape[1]


def front(sel, own, other, gain, w_query, w_key, w_value):
    local, d = own.shape
    widths = [w.shape[1] // 4 for w in (w_query, w_key, w_value)]
    part = pl.BlockSpec((local, d), lambda j, sel: (0, 0))
    return pl.pallas_call(
        front_kernel,
        grid_spec=pltpu.PrefetchScalarGridSpec(
            num_scalar_prefetch=1,
            grid=(2,),
            in_specs=[part, part, pl.BlockSpec((1, d), lambda j, sel: (0, 0))]
            + [pl.BlockSpec((d, w), lambda j, sel: (0, 2 * j + sel[0])) for w in widths],
            out_specs=[
                pl.BlockSpec((2 * local, d), lambda j, sel: (0, 0)),
                pl.BlockSpec((sum(widths), 2 * local), lambda j, sel: (j, 0)),
            ],
        ),
        out_shape=[
            jax.ShapeDtypeStruct((2 * local, d), BF16),
            jax.ShapeDtypeStruct((2 * sum(widths), 2 * local), F32),
        ],
        cost_estimate=cost(4 * local * d * 2 * sum(widths), own, own, w_query, w_query, w_query),
        name="norm_and_projections",
    )(sel, own, other, gain, w_query, w_key, w_value)


def ffn_kernel(
    sel_ref, hn_ref, own_ref, other_ref, gate0_ref, gate1_ref, up0_ref, up1_ref, down0_ref, down1_ref,
    act_ref, dg_ref, du_ref, gate_leave_ref, up_leave_ref, down_leave_ref, hy1_ref, hz1_ref, dx1_ref, back_ref, low_ref,
    turned_ref, hz0_ref, hy0_ref, dm_ref, dx0_ref,
):
    tokens, d = hn_ref.shape

    @pl.when(pl.program_id(0) == 0)
    def _():
        c, x, y, zl = [sel_ref[i] for i in range(4)]
        local, half, rows = tokens // 2, d // 2, d // 8
        back_ref[...] = jnp.zeros_like(back_ref)
        for i, ref in enumerate((own_ref, other_ref)):
            place = pl.multiple_of((c if i == 0 else 1 - c) * local, local)
            dm_ref[pl.ds(place, local), :] = ref[...]
        turned_ref[...] = hn_ref[...].T
        for order in range(2):
            for i in range(4):
                high, low = divmod(i, 2)
                to = slice(i * rows, (i + 1) * rows)
                block = 4 * high + 2 * (zl if order else 1 - zl) + low
                (hz0_ref, hz1_ref)[order][to, :] = turned_ref[pl.ds(pl.multiple_of(block * rows, rows), rows), :]
                block = 4 * high + 2 * low + (y if order else 1 - y)
                (hy0_ref, hy1_ref)[order][to, :] = turned_ref[pl.ds(pl.multiple_of(block * rows, rows), rows), :]
            place = pl.multiple_of((x if order else 1 - x) * half, half)
            (dx0_ref, dx1_ref)[order][...] = dm_ref[:, pl.ds(place, half)]

    gate_w = jnp.concatenate([gate0_ref[...], gate1_ref[...]], axis=1)
    up_w = jnp.concatenate([up0_ref[...], up1_ref[...]], axis=1)
    down_w = jnp.concatenate([down0_ref[...], down1_ref[...]], axis=0)
    step = min(256, tokens)
    for begin in range(0, tokens, step):
        at = slice(begin, begin + step)
        gate = dot(hn_ref[at, :], gate_w, 1, 0)
        up = dot(hn_ref[at, :], up_w, 1, 0)
        d_act = dot(dm_ref[at, :], down_w, 1, 1)
        sigmoid = 1.0 / (1.0 + jnp.exp(-gate))
        silu = gate * sigmoid
        act_ref[at, :] = (silu * up).astype(BF16)
        du_ref[at, :] = (d_act * silu).astype(BF16)
        dg_ref[at, :] = (d_act * up * (sigmoid + silu * (1.0 - sigmoid))).astype(BF16)
    up_leave_ref[...] = dot(hz0_ref[...], du_ref[...], 1, 0).astype(BF16)
    gate_leave_ref[...] = dot(hy0_ref[...], dg_ref[...], 1, 0).astype(BF16)
    both_w = jnp.concatenate([gate_w, up_w], axis=1)
    for begin in range(0, tokens, step):
        at = slice(begin, begin + step)
        back_ref[at, :] += dot(jnp.concatenate([dg_ref[at, :], du_ref[at, :]], axis=1), both_w, 1, 1)
    down_leave_ref[...] = dot(act_ref[...].T, dx0_ref[...], 1, 0).astype(BF16)

    @pl.when(pl.program_id(0) == pl.num_programs(0) - 1)
    def _():
        low_ref[...] = back_ref[...].astype(BF16)


def feed_forward(sel, hnormed, d_own, d_other, w_gate, w_up, w_down):
    tokens, d = hnormed.shape
    units = w_gate.shape[1] // 2
    blocks = units // 2 // LANES
    block = 2 * LANES
    whole = pl.BlockSpec((tokens, d), lambda j, sel: (0, 0))
    part = pl.BlockSpec((tokens // 2, d), lambda j, sel: (0, 0))
    columns = [
        pl.BlockSpec((d, LANES), lambda j, sel, i=i: (0, local_block(2 * j + i, sel[0], blocks))) for i in range(2)
    ]
    rows = [pl.BlockSpec((LANES, d), lambda j, sel, i=i: (local_block(2 * j + i, sel[0], blocks), 0)) for i in range(2)]
    return pl.pallas_call(
        ffn_kernel,
        grid_spec=pltpu.PrefetchScalarGridSpec(
            num_scalar_prefetch=1,
            grid=(units // block,),
            in_specs=[whole, part, part] + columns + columns + rows,
            out_specs=[pl.BlockSpec((tokens, block), lambda j, sel: (0, j))] * 3
            + [pl.BlockSpec((d // 2, block), lambda j, sel: (0, j))] * 2
            + [pl.BlockSpec((block, d // 2), lambda j, sel: (j, 0))]
            + [pl.BlockSpec((d // 2, tokens), lambda j, sel: (0, 0))] * 2
            + [pl.BlockSpec((tokens, d // 2), lambda j, sel: (0, 0))]
            + [whole, whole],
            scratch_shapes=[pltpu.VMEM((d, tokens), BF16)]
            + [pltpu.VMEM((d // 2, tokens), BF16)] * 2
            + [pltpu.VMEM((tokens, d), BF16), pltpu.VMEM((tokens, d // 2), BF16)],
        ),
        out_shape=[jax.ShapeDtypeStruct((tokens, units), BF16)] * 3
        + [jax.ShapeDtypeStruct((d // 2, units), BF16)] * 2
        + [jax.ShapeDtypeStruct((units, d // 2), BF16)]
        + [jax.ShapeDtypeStruct((d // 2, tokens), BF16)] * 2
        + [jax.ShapeDtypeStruct((tokens, d // 2), BF16)]
        + [jax.ShapeDtypeStruct((tokens, d), t) for t in (F32, BF16)],
        name="feed_forward",
    )(sel, hnormed, d_own, d_other, w_gate, w_gate, w_up, w_up, w_down, w_down)


def ffn_grads_kernel(act_ref, dg_ref, du_ref, hn_y_ref, hn_z_ref, dm_ref, gate_ref, up_ref, down_ref):
    up_ref[...] = dot(hn_z_ref[...], du_ref[...], 1, 0).astype(BF16)
    gate_ref[...] = dot(hn_y_ref[...], dg_ref[...], 1, 0).astype(BF16)
    down_ref[...] = dot(act_ref[...].T, dm_ref[...], 1, 0).astype(BF16)


def ffn_grads(act, d_gate, d_up, hn_y, hn_z, dm_x):
    tokens, units = act.shape
    half = hn_y.shape[0]
    block = 2 * LANES
    columns = pl.BlockSpec((tokens, block), lambda j: (0, j))
    turned = pl.BlockSpec((half, tokens), lambda j: (0, 0))
    out = pl.BlockSpec((half, block), lambda j: (0, j))
    return pl.pallas_call(
        ffn_grads_kernel,
        grid=(units // block,),
        in_specs=[columns] * 3 + [turned] * 2 + [pl.BlockSpec((tokens, half), lambda j: (0, 0))],
        out_specs=[out, out, pl.BlockSpec((block, half), lambda j: (j, 0))],
        out_shape=[jax.ShapeDtypeStruct((half, units), BF16)] * 2 + [jax.ShapeDtypeStruct((units, half), BF16)],
        cost_estimate=cost(2 * tokens * half * units, act),
        name="feed_forward_gradients",
    )(act, d_gate, d_up, hn_y, hn_z, dm_x)


def ffn_out_kernel(sel_ref, act_ref, down0_ref, down1_ref, own_ref, low_ref):
    local = own_ref.shape[0]
    down_w = jnp.concatenate([down0_ref[...], down1_ref[...]], axis=0)
    own_ref[...] = dot(act_ref[pl.ds(pl.multiple_of(sel_ref[0] * local, local), local), :], down_w, 1, 0)
    other = act_ref[pl.ds(pl.multiple_of((1 - sel_ref[0]) * local, local), local), :]
    low_ref[...] = dot(other, down_w, 1, 0).astype(BF16)


def ffn_out(sel, act, w_down):
    tokens, units = act.shape
    d = w_down.shape[1]
    block = min(256, d)
    weights = [pl.BlockSpec((units // 2, block), lambda j, sel, i=i: (2 * i + sel[0], j)) for i in range(2)]
    return pl.pallas_call(
        ffn_out_kernel,
        grid_spec=pltpu.PrefetchScalarGridSpec(
            num_scalar_prefetch=1,
            grid=(d // block,),
            in_specs=[pl.BlockSpec((tokens, units), lambda j, sel: (0, 0))] + weights,
            out_specs=[pl.BlockSpec((tokens // 2, block), lambda j, sel: (0, j))] * 2,
        ),
        out_shape=[jax.ShapeDtypeStruct((tokens // 2, d), t) for t in (F32, BF16)],
        cost_estimate=pl.CostEstimate(flops=10**9, transcendentals=0, bytes_accessed=1),
        name="feed_forward_out",
    )(sel, act, w_down, w_down)


def tie(values, *others):
    return lax.optimization_barrier((tuple(values), others))[0]


def cost(flops, *arrays):
    return pl.CostEstimate(flops=flops, transcendentals=0, bytes_accessed=sum(a.size * a.dtype.itemsize for a in arrays))


def add_up(terms):
    return sum(t.astype(F32) for t in terms)


def leave(terms, dim, bit):
    size = terms[0].shape[dim] // 2
    if dim < terms[0].ndim - 2:
        return add_up([lax.dynamic_slice_in_dim(t, (1 - bit) * size, size, dim) for t in terms]).astype(BF16)
    low = add_up([lax.slice_in_dim(t, 0, size, axis=dim) for t in terms])
    high = add_up([lax.slice_in_dim(t, size, 2 * size, axis=dim) for t in terms])
    return pick(bit, high, low).astype(BF16)


def stay(terms, dim, bit):
    size = terms[0].shape[dim] // 2 if terms else 0
    if terms and dim < terms[0].ndim - 2:
        return [lax.dynamic_slice_in_dim(t, bit * size, size, dim) for t in terms]
    return [
        pick(bit, lax.slice_in_dim(t, 0, size, axis=dim), lax.slice_in_dim(t, size, 2 * size, axis=dim))
        for t in terms
    ]


def halve(terms, axis, dim):
    bit = lax.axis_index(axis)
    return stay(terms, dim, bit) + [swap(leave(terms, dim, bit), axis)]


def share_rows(total, c):
    rows = total.shape[0] // 2
    own = pick(c, total[:rows], total[rows:])
    other = swap(pick(c, total[rows:], total[:rows]).astype(BF16), "c").astype(F32)
    return in_order(c, own, other, 1)


def own_rows(v, c, local):
    return pick(c, v[:local], v[local:])


def pair_body(
    tokens, cotangent, doc_lengths, attn_gain, w_query, w_key, w_value, query_gain, key_gain, w_out,
    ffn_gain, w_gate, w_up, w_down,
):
    local, d = tokens.shape[1:]
    length = 2 * local
    size = query_gain.shape[0]
    kv_count = w_key.shape[1] // size
    group = w_query.shape[1] // w_key.shape[1]
    pairs = kv_count // 4
    zh, zl, y, c, x = [lax.axis_index(a) for a in AXES]
    gain_attn = attn_gain.astype(F32)
    gain_ffn = ffn_gain.astype(F32)
    gain_q = query_gain.astype(F32)[:, None]
    gain_k = key_gain.astype(F32)[:, None]

    come_tokens = transpose_pair(tokens[0])
    lengths = jnp.where(c == x, doc_lengths[0], swap(doc_lengths[0], "c"))
    ends = jnp.cumsum(lengths)
    positions = jnp.arange(length, dtype=jnp.int32)
    segment = jnp.sum((ends[:, None] <= positions[None, :]).astype(jnp.int32), axis=0, keepdims=True)
    half = size // 2
    spread = jnp.exp(jnp.arange(half, dtype=F32) * (-2.0 * math.log(1000000.0) / size))
    angles = spread[:, None] * positions.astype(F32)[None, :]
    cosine, sine = jnp.cos(angles), jnp.sin(angles)
    parts = [part_columns(w, c) for w in (w_query, w_key, w_value)]
    w_qkv = jnp.concatenate([p[i] for i in range(2) for p in parts], axis=1)
    out_w = part_rows(w_out, c)
    sel = jnp.stack([c, x, y, zl]).astype(jnp.int32)
    w_qkv, out_w, cosine, sine, sel, come_tokens = tie((w_qkv, out_w, cosine, sine, sel, come_tokens))
    own_tokens = jnp.where(c == x, tokens[0], come_tokens)
    other_tokens = swap(own_tokens, "c")
    cot_low, other_tokens = tie((cotangent[0], other_tokens))
    come_cot = transpose_pair(cot_low)
    normed, qkv = front(sel, own_tokens, other_tokens, gain_attn[None], w_query, w_key, w_value)
    docs = doc_lengths.shape[1]
    attended_own, exact, logs, qs, ks, vs = attention(
        qkv, segment, gain_q, gain_k, cosine, sine, size, group, pairs, docs
    )
    attended_own, come_cot = tie((attended_own, come_cot))
    attended_other = swap(attended_own, "c")
    own_cot = jnp.where(c == x, cot_low, come_cot)
    other_cot = swap(own_cot, "c")
    width = attended_own.shape[0] // 2
    attended = jnp.concatenate(
        [in_order(c, attended_own[i : i + width], attended_other[i : i + width], 0) for i in (0, width)], axis=0
    )
    inputs = in_order(c, own_tokens, other_tokens, 0).astype(F32)
    hidden = inputs + dot(attended, w_out, 0, 0)
    hnormed = rms_scale(hidden, gain_ffn).astype(BF16)

    act, d_gate, d_up, send_gate, send_up, send_down, hn_y, hn_z, dm_x, d_hn, d_hn_low = feed_forward(
        sel, hnormed, own_cot, other_cot, w_gate, w_up, w_down
    )
    come_up, come_down, come_gate = swap(send_up, "zl"), swap(send_down, "x"), swap(send_gate, "y")
    d_hn_other = swap(d_hn_low, "c")
    keep_gate, keep_up, keep_down = ffn_grads(act, d_gate, d_up, hn_y, hn_z, dm_x)
    units = d_gate.shape[1]
    rows = d // 8
    half = d // 2
    (d_hn_other,) = tie((d_hn_other,), keep_up, keep_gate, keep_down)
    d_hn = d_hn + d_hn_other.astype(F32)
    d_hidden_norm, ffn_gain_terms = norm_back(d_hn, hidden, gain_ffn)
    d_hidden = in_order(c, own_cot, other_cot, 0).astype(F32) + d_hidden_norm
    d_attn = d_hidden.astype(BF16)
    d_attended = dot(out_w, d_attn, 1, 1).astype(BF16)

    quarter = d // 4
    send_out, keep_out = [
        dot(attended, lax.dynamic_slice_in_dim(d_attn, (2 * i + c) * quarter, quarter, 1), 1, 0).astype(BF16)
        for i in (1 - x, x)
    ]
    come_out = swap(send_out, "x")
    act, d_attended = tie((act, d_attended), send_out, keep_out)
    part_out, out_low = ffn_out(sel, act, w_down)

    come_up, come_down, come_gate, part_out, out_low, d_attended = tie(
        (come_up, come_down, come_gate, part_out, out_low, d_attended)
    )
    up = [v.reshape(2, 2, rows, units) for v in (come_up, keep_up)]
    down = [v.reshape(2, 2, units // 4, half) for v in (come_down, keep_down)]
    gate = [v.reshape(2, 2, rows, units) for v in (come_gate, keep_gate)]
    send_gate, send_down, send_up = leave(gate, 1, zl), leave(down, 1, y), leave(up, 3, x)
    gate = stay(gate, 1, zl) + [swap(send_gate, "zl")]
    down = stay(down, 1, y) + [swap(send_down, "y")]
    up = stay(up, 3, x) + [swap(send_up, "x")]
    come_out, d_attended, out_low = tie((come_out, d_attended, out_low), send_gate, send_down, send_up)
    out_other = swap(out_low, "c")
    d_qkv, gain_q_terms, gain_k_terms = attention_back(
        qkv, qs, ks, vs, exact, logs, d_attended, segment, gain_q, gain_k, cosine, sine, size, group, pairs, docs
    )
    d_qkv, out_other = tie((d_qkv, out_other))
    width = d_qkv.shape[0] // 2
    send_qkv = dot(normed, lax.dynamic_slice_in_dim(d_qkv, (1 - x) * width, width, 0), 0, 1).astype(BF16)
    come_qkv = swap(send_qkv, "x")
    (d_qkv,) = tie((d_qkv,), send_qkv)
    part_low = dot(pick(c, d_qkv[:, local:], d_qkv[:, :local]), w_qkv, 0, 1).astype(BF16)
    part_other = swap(part_low, "c")
    (d_qkv,) = tie((d_qkv,), part_low)
    part = dot(pick(c, d_qkv[:, :local], d_qkv[:, local:]), w_qkv, 0, 1)
    keep_qkv = dot(normed, lax.dynamic_slice_in_dim(d_qkv, x * width, width, 0), 0, 1).astype(BF16)

    gate[-1], down[-1], up[-1], part_other = tie((gate[-1], down[-1], up[-1], part_other), part, keep_qkv)
    send_gate, send_down, send_up = leave(gate, 3, x), add_up(down).astype(BF16), leave(up, 1, y)
    gate = stay(gate, 3, x) + [swap(send_gate, "x")]
    down = down + [lax.ppermute(send_down, ("zl", "c"), [(2, 0), (1, 3)])]
    up = stay(up, 1, y) + [swap(send_up, "y")]
    (part_other,) = tie((part_other,), send_gate, send_down, send_up)
    d_normed = part + part_other.astype(F32)
    d_input_norm, attn_gain_terms = norm_back(d_normed, own_tokens.astype(F32), gain_attn)
    d_inputs = own_rows(d_hidden, c, local) + d_input_norm
    gains = jnp.concatenate(
        [
            jnp.sum(attn_gain_terms, axis=0),
            jnp.sum(ffn_gain_terms, axis=0) * 0.5,
            jnp.sum(gain_q_terms, axis=1),
            jnp.sum(gain_k_terms, axis=1),
        ]
    ).reshape(-1, 128)
    reached = swap(gains, "zh")
    output = own_rows(hidden, c, local) + part_out + out_other.astype(F32)
    results = jnp.concatenate([output.astype(BF16), d_inputs.astype(BF16)], axis=0)

    def joined(parts):
        first, second, joint = parts
        return add_up([jnp.concatenate([add_up(first), add_up(second)], axis=-1)] + joint)

    def next_stage(parts, axis, dim):
        bit = lax.axis_index(axis)
        come = swap(joined([stay(p, dim, 1 - bit) for p in parts]).astype(BF16), axis)
        first, second, joint = [stay(p, dim, bit) for p in parts]
        return first, second, joint + [come]

    gate[-1], down[-1], up[-1], come_qkv, reached, results = tie(
        (gate[-1], down[-1], up[-1], come_qkv, reached, results)
    )
    send_gate, send_down, send_up = leave(gate, 0, zh), leave(down, 0, zh), leave(up, 0, zh)
    gate = stay(gate, 0, zh) + [swap(send_gate, "zh")]
    down = stay(down, 0, zh) + [swap(send_down, "zh")]
    up = stay(up, 0, zh) + [swap(send_up, "zh")]
    out = [v.reshape(2, 2, 2, rows, quarter) for v in (come_out, keep_out)]
    qkv_grad = [v.reshape(2, 2, 2, rows, width) for v in (come_qkv, keep_qkv)]
    first, second, joint = next_stage((out, qkv_grad, []), "y", 2)
    gains = gains + reached
    gains = gains + swap(gains, "x")
    results, gains = tie((results, gains))
    results_other = transpose_pair(results)
    joint[-1], gains = tie((joint[-1], gains))
    first, second, joint = next_stage((first, second, joint), "zl", 1)
    gains = gains + swap(gains, "c")
    gains = gains + swap(gains, "y")
    joint[-1], gains = tie((joint[-1], gains))
    first, second, joint = next_stage((first, second, joint), "zh", 0)
    gains = gains + swap(gains, "zl")
    gate[-1], down[-1], up[-1], gains = tie((gate[-1], down[-1], up[-1], gains))

    total = add_up(down).reshape(-1, d // 2)
    n = total.shape[0] // 2
    own = pick(c, total[:n], total[n:])
    other = pick(c, total[n:], total[:n]).astype(BF16)
    other = lax.ppermute(other, ("zl", "c"), [(0, 1), (3, 2)]).astype(F32)
    sum_down = jnp.where(zl == c, own, other)
    sum_gate, sum_up = [share_rows(add_up(t).reshape(rows, units // 2), c) for t in (gate, up)]
    (joint[-1],) = tie((joint[-1],), sum_gate, sum_up, sum_down)
    gains = gains.reshape(-1)
    both = joined((first, second, joint)).reshape(rows, 3 * quarter)
    n = rows // 2
    own = pick(c, both[:n], both[n:])
    other = swap(pick(c, both[n:], both[:n]).astype(BF16), "c").astype(F32)
    first, second = pick(c, own, other), pick(c, other, own)
    q_width, kv_width = pairs * group * size, pairs * size
    ends_of = [0, quarter, quarter + q_width, quarter + q_width + kv_width, quarter + q_width + 2 * kv_width]
    sum_out, sum_query, sum_key, sum_value = [
        jnp.concatenate([first[:, low:high], second[:, low:high]], axis=1)
        for low, high in zip(ends_of[:-1], ends_of[1:])
    ]
    stays = c == x
    output = jnp.where(stays, output, results_other[:local].astype(F32))
    d_inputs = jnp.where(stays, d_inputs, results_other[local:].astype(F32))
    return (
        output[None],
        d_inputs[None],
        gains[:d],
        sum_query,
        sum_key,
        sum_value,
        gains[2 * d : 2 * d + size],
        gains[2 * d + size :],
        sum_out,
        gains[d : 2 * d],
        sum_gate,
        sum_up,
        sum_down,
    )


def solution(mesh):
    rows, shards = mesh.shape["dp"], mesh.shape["seq"]
    if rows == 16 and shards == 2:
        body = pair_body
        mesh = Mesh(mesh.devices.reshape(2, 2, 2, 2, 2), AXES)
        dp, seq = AXES[:4], "x"
    else:
        body = general_body
        dp, seq = "dp", "seq"
    return jax.shard_map(
        body,
        mesh=mesh,
        in_specs=(P(dp, seq, None), P(dp, seq, None), P(dp, None)) + (P(),) * 11,
        out_specs=(P(dp, seq, None), P(dp, seq, None), P())
        + (P(dp, seq),) * 3
        + (P(), P(), P(dp, seq), P())
        + (P(dp, seq),) * 3,
        check_vma=False,
    )
```

```python
import math

import functools

import jax
import jax.numpy as jnp
from jax import lax
from jax.experimental import pallas as pl
from jax.experimental.pallas import tpu as pltpu
from jax.sharding import Mesh
from jax.sharding import PartitionSpec as P

EPSILON = 1e-06


def rms_scale(values, gain):
    return values * lax.rsqrt(jnp.mean(values * values, axis=-1, keepdims=True) + EPSILON) * gain


def norm_back(incoming, values, gain):
    inverse = lax.rsqrt(jnp.mean(values * values, axis=-1, keepdims=True) + EPSILON)
    unit = values * inverse
    scaled = incoming * gain
    d_values = inverse * (scaled - unit * jnp.mean(scaled * unit, axis=-1, keepdims=True))
    return (d_values, incoming * unit)


def rope_tables(first, count, width):
    half = width // 2
    spread = jnp.exp(jnp.arange(half, dtype=jnp.float32) * (-2.0 * math.log(1000000.0) / width))
    places = (first + jnp.arange(count, dtype=jnp.int32)).astype(jnp.float32)
    angles = places[:, None] * spread[None, :]
    return (jnp.cos(angles)[:, None, :], jnp.sin(angles)[:, None, :])


def rotate(values, cosine, sine):
    half = values.shape[-1] // 2
    first_half = values[..., :half]
    second_half = values[..., half:]
    return jnp.concatenate(
        [first_half * cosine - second_half * sine, second_half * cosine + first_half * sine],
        axis=-1,
    )


def reduce_grads(grads):
    partial_sum = lax.psum_scatter(grads, "dp", scatter_dimension=0, tiled=True)
    return lax.psum_scatter(partial_sum, "seq", scatter_dimension=1, tiled=True)


def general_body(
    tokens,
    cotangent,
    doc_lengths,
    attn_gain,
    w_query,
    w_key,
    w_value,
    query_gain,
    key_gain,
    w_out,
    ffn_gain,
    w_gate,
    w_up,
    w_down,
):
    shards = lax.axis_size("seq")
    local = tokens.shape[1]
    length = local * shards
    head_size = query_gain.shape[0]
    kv_count = w_key.shape[1] // head_size
    head_count = w_query.shape[1] // head_size
    group = head_count // kv_count
    kv_local = kv_count // shards
    block = min(512, length)
    num_blocks = length // block
    scale = head_size ** (-0.5)
    f32 = jnp.float32
    bf16 = jnp.bfloat16
    gain_attn = attn_gain.astype(f32)
    gain_query = query_gain.astype(f32)
    gain_key = key_gain.astype(f32)
    gain_ffn = ffn_gain.astype(f32)
    inputs = tokens[0].astype(f32)
    normed = rms_scale(inputs, gain_attn).astype(bf16)
    query_raw = jnp.dot(normed, w_query, preferred_element_type=f32).reshape(
        local, head_count, head_size
    )
    key_raw = jnp.dot(normed, w_key, preferred_element_type=f32).reshape(local, kv_count, head_size)
    values = (
        jnp.dot(normed, w_value, preferred_element_type=f32)
        .astype(bf16)
        .reshape(local, kv_count, head_size)
    )
    cosine, sine = rope_tables(lax.axis_index("seq") * local, local, head_size)
    query_rot = rotate(rms_scale(query_raw, gain_query), cosine, sine).astype(bf16)
    key_rot = rotate(rms_scale(key_raw, gain_key), cosine, sine).astype(bf16)
    packed_query = query_rot.reshape(local, kv_count, group * head_size)
    packed_kv = jnp.concatenate([key_rot, values], axis=2)
    query_heads, kv_heads = (
        lax.all_to_all(packed_query, "seq", split_axis=1, concat_axis=0, tiled=True),
        lax.all_to_all(packed_kv, "seq", split_axis=1, concat_axis=0, tiled=True),
    )
    query_all = query_heads.reshape(length, kv_local, group, head_size)
    key_all = kv_heads[:, :, :head_size]
    value_all = kv_heads[:, :, head_size:]
    positions = jnp.arange(length, dtype=jnp.int32)
    ends = jnp.cumsum(doc_lengths[0])
    segment = jnp.sum((ends[None, :] <= positions[:, None]).astype(jnp.int32), axis=1)
    starts = jnp.arange(num_blocks, dtype=jnp.int32) * block

    def allowed_at(begin):
        rows_here = begin + jnp.arange(block, dtype=jnp.int32)
        query_seg = lax.dynamic_slice_in_dim(segment, begin, block, 0)
        return (query_seg[:, None] == segment[None, :]) & (positions[None, :] <= rows_here[:, None])

    def block_scores(begin):
        query_block = lax.dynamic_slice_in_dim(query_all, begin, block, 0)
        scores = (
            jnp.einsum("qhgd,khd->hgqk", query_block, key_all, preferred_element_type=f32) * scale
        )
        return (query_block, jnp.where(allowed_at(begin), scores, -jnp.inf))

    def attend(begin):
        query_block, scores = block_scores(begin)
        top_score = jnp.max(scores, axis=-1, keepdims=True)
        expos = jnp.exp(scores - top_score)
        totals = jnp.sum(expos, axis=-1, keepdims=True)
        probs = (expos / totals).astype(bf16)
        result = jnp.einsum("hgqk,khd->qhgd", probs, value_all, preferred_element_type=f32)
        return (result.astype(bf16), top_score[..., 0] + jnp.log(totals[..., 0]))

    attended_heads, log_totals = lax.map(attend, starts)
    attended_heads = attended_heads.reshape(length, kv_local, group * head_size)
    attended = lax.all_to_all(
        attended_heads, "seq", split_axis=0, concat_axis=1, tiled=True
    ).reshape(local, head_count * head_size)
    hidden = inputs + jnp.dot(attended, w_out, preferred_element_type=f32)
    hnormed = rms_scale(hidden, gain_ffn).astype(bf16)
    gate = jnp.dot(hnormed, w_gate, preferred_element_type=f32)
    up_part = jnp.dot(hnormed, w_up, preferred_element_type=f32)
    act = (jax.nn.silu(gate) * up_part).astype(bf16)
    output = hidden + jnp.dot(act, w_down, preferred_element_type=f32)
    d_mlp = cotangent[0]
    grad_down = jnp.einsum("tf,td->fd", act, d_mlp, preferred_element_type=f32)
    d_act = jnp.einsum("td,fd->tf", d_mlp, w_down, preferred_element_type=f32)
    gate_again = jnp.dot(hnormed, w_gate, preferred_element_type=f32)
    up_again = jnp.dot(hnormed, w_up, preferred_element_type=f32)
    sigmoid_gate = jax.nn.sigmoid(gate_again)
    d_up = (d_act * gate_again * sigmoid_gate).astype(bf16)
    d_gate = (d_act * up_again * sigmoid_gate * (1.0 + gate_again * (1.0 - sigmoid_gate))).astype(
        bf16
    )
    grad_gate = jnp.einsum("td,tf->df", hnormed, d_gate, preferred_element_type=f32)
    grad_up = jnp.einsum("td,tf->df", hnormed, d_up, preferred_element_type=f32)
    ffn_sums = reduce_grads((grad_gate, grad_up, grad_down))
    d_hnormed = jnp.einsum("tf,df->td", d_gate, w_gate, preferred_element_type=f32) + jnp.einsum(
        "tf,df->td", d_up, w_up, preferred_element_type=f32
    )
    d_hidden_norm, ffn_gain_terms = norm_back(d_hnormed, hidden, gain_ffn)
    d_hidden = cotangent[0].astype(f32) + d_hidden_norm
    d_attn = d_hidden.astype(bf16)
    grad_out = jnp.einsum("tf,td->fd", attended, d_attn, preferred_element_type=f32)
    d_attended = jnp.einsum("td,fd->tf", d_attn, w_out, preferred_element_type=f32).astype(bf16)
    d_heads = lax.all_to_all(
        d_attended.reshape(local, kv_count, group * head_size),
        "seq",
        split_axis=1,
        concat_axis=0,
        tiled=True,
    )
    d_all = d_heads.reshape(length, kv_local, group, head_size)

    def attend_back(carry, item):
        begin, log_block = item
        query_block, scores = block_scores(begin)
        probs = jnp.exp(scores - log_block[..., None])
        d_block = lax.dynamic_slice_in_dim(d_all, begin, block, 0)
        d_probs = jnp.einsum("qhgd,khd->hgqk", d_block, value_all, preferred_element_type=f32)
        delta = jnp.sum(probs * d_probs, axis=-1, keepdims=True)
        d_scores = (scale * (probs * (d_probs - delta))).astype(bf16)
        d_query_block = jnp.einsum("hgqk,khd->qhgd", d_scores, key_all, preferred_element_type=f32)
        key_total = carry[0] + jnp.einsum(
            "hgqk,qhgd->khd", d_scores, query_block, preferred_element_type=f32
        )
        value_total = carry[1] + jnp.einsum(
            "hgqk,qhgd->khd", probs.astype(bf16), d_block, preferred_element_type=f32
        )
        return ((key_total, value_total), d_query_block.astype(bf16))

    empty = jnp.zeros((length, kv_local, head_size), f32)
    (d_keys, d_values), d_queries = lax.scan(attend_back, (empty, empty), (starts, log_totals))
    d_queries = d_queries.reshape(length, kv_local, group * head_size)
    d_kv = jnp.concatenate([d_keys.astype(bf16), d_values.astype(bf16)], axis=2)
    d_query_pos, d_kv_pos = (
        lax.all_to_all(d_queries, "seq", split_axis=0, concat_axis=1, tiled=True),
        lax.all_to_all(d_kv, "seq", split_axis=0, concat_axis=1, tiled=True),
    )
    d_query_rot = d_query_pos.reshape(local, head_count, head_size).astype(f32)
    d_query_raw, query_gain_terms = norm_back(
        rotate(d_query_rot, cosine, -sine), query_raw, gain_query
    )
    d_query_low = d_query_raw.reshape(local, head_count * head_size).astype(bf16)
    d_key_rot = d_kv_pos[:, :, :head_size].astype(f32)
    d_key_raw, key_gain_terms = norm_back(rotate(d_key_rot, cosine, -sine), key_raw, gain_key)
    d_key_low = d_key_raw.reshape(local, kv_count * head_size).astype(bf16)
    d_value_low = d_kv_pos[:, :, head_size:].reshape(local, kv_count * head_size)
    grad_query = jnp.einsum("td,tf->df", normed, d_query_low, preferred_element_type=f32)
    grad_key = jnp.einsum("td,tf->df", normed, d_key_low, preferred_element_type=f32)
    grad_value = jnp.einsum("td,tf->df", normed, d_value_low, preferred_element_type=f32)
    d_normed = jnp.einsum("tf,df->td", d_query_low, w_query, preferred_element_type=f32)
    d_normed = d_normed + jnp.einsum("tf,df->td", d_key_low, w_key, preferred_element_type=f32)
    d_normed = d_normed + jnp.einsum("tf,df->td", d_value_low, w_value, preferred_element_type=f32)
    d_input_norm, attn_gain_terms = norm_back(d_normed, inputs, gain_attn)
    d_inputs = d_hidden + d_input_norm
    attn_sums = reduce_grads((grad_query, grad_key, grad_value, grad_out))
    gain_totals = lax.psum(
        (
            jnp.sum(attn_gain_terms, axis=0),
            jnp.sum(query_gain_terms, axis=(0, 1)),
            jnp.sum(key_gain_terms, axis=(0, 1)),
            jnp.sum(ffn_gain_terms, axis=0),
        ),
        ("dp", "seq"),
    )
    return (
        output[None],
        d_inputs[None],
        gain_totals[0],
        attn_sums[0],
        attn_sums[1],
        attn_sums[2],
        gain_totals[1],
        gain_totals[2],
        attn_sums[3],
        gain_totals[3],
        ffn_sums[0],
        ffn_sums[1],
        ffn_sums[2],
    )


AXES = ("zh", "zl", "y", "c", "x")
QBLOCK = 256
F32 = jnp.float32
BF16 = jnp.bfloat16


def swap(v, axis):
    return lax.ppermute(v, axis, [(0, 1), (1, 0)])


def transpose_pair(v):
    return lax.ppermute(v, ("c", "x"), [(1, 2), (2, 1)])


def pick(bit, low, high):
    return jnp.where(bit == 0, low, high)


def in_order(bit, own, other, axis):
    return jnp.concatenate([pick(bit, own, other), pick(bit, other, own)], axis=axis)


def dot(left, right, left_dim, right_dim):
    return lax.dot_general(
        left, right, (((left_dim,), (right_dim,)), ((), ())), preferred_element_type=F32
    )


def part_columns(w, c):
    width = w.shape[1] // 4
    return [lax.dynamic_slice_in_dim(w, (2 * i + c) * width, width, 1) for i in range(2)]


def part_rows(w, c):
    rows, columns = w.shape
    return lax.dynamic_index_in_dim(w.reshape(2, 2, rows // 4, columns), c, 1, False).reshape(rows // 2, columns)


def rope_rows(values, gain, cosine, sine):
    unit = values * lax.rsqrt(jnp.mean(values * values, axis=0, keepdims=True) + EPSILON) * gain
    half = values.shape[0] // 2
    first, second = unit[:half], unit[half:]
    return jnp.concatenate([first * cosine - second * sine, second * cosine + first * sine], axis=0)


def rope_rows_back(incoming, values, gain, cosine, sine):
    half = values.shape[0] // 2
    first, second = incoming[:half], incoming[half:]
    turned = jnp.concatenate([first * cosine + second * sine, second * cosine - first * sine], axis=0)
    inverse = lax.rsqrt(jnp.mean(values * values, axis=0, keepdims=True) + EPSILON)
    unit = values * inverse
    scaled = turned * gain
    d_values = inverse * (scaled - unit * jnp.mean(scaled * unit, axis=0, keepdims=True))
    return d_values, turned * unit


BLOCKED = 256.0


def split_low(v):
    high = v.astype(BF16)
    rest = v - high.astype(F32)
    middle = rest.astype(BF16)
    return [high, middle, (rest - middle.astype(F32)).astype(BF16)]


def documents(segment, rows, length):
    return (segment == lax.broadcasted_iota(jnp.int32, (rows, length), 0)).astype(F32)


def key_parts(begin, window):
    low = max(0, begin - (window - 1)) // QBLOCK * QBLOCK
    return ([(low, begin, False)] if begin > low else []) + [(begin, begin + QBLOCK, True)]


def causal(block):
    key_at = lax.broadcasted_iota(jnp.int32, (block, block), 0)
    return key_at <= lax.broadcasted_iota(jnp.int32, (block, block), 1)


def attention_kernel(
    segment_ref, gain_q_ref, gain_k_ref, cos_ref, sin_ref, q_ref, k_ref, v_ref,
    out_ref, exact_ref, log_ref, qs_ref, ks_ref, vs_ref, *, docs, window,
):
    size, length = k_ref.shape
    group = q_ref.shape[0] // size
    cosine, sine = cos_ref[...], sin_ref[...]
    same = documents(segment_ref[...], docs, length)
    k_rot = rope_rows(k_ref[...], gain_k_ref[...], cosine, sine)
    ks_ref[...] = k_rot.astype(BF16)
    keys = jnp.concatenate([k_rot, (same - 1.0) * BLOCKED], axis=0).T.astype(BF16)
    values = v_ref[...].astype(BF16)
    vs_ref[...] = values
    ones = (lax.broadcasted_iota(jnp.int32, (16, length), 0) == 0).astype(BF16)
    values = jnp.concatenate([values, ones], axis=0)
    allowed = causal(QBLOCK)
    for h in range(group):
        rows = pl.ds(h * size, size)
        q_rot = rope_rows(q_ref[rows, :], gain_q_ref[...], cosine, sine).astype(BF16)
        q_rot = q_rot * jnp.asarray(size ** (-0.5), BF16)
        qs_ref[rows, :] = q_rot
        query = jnp.concatenate([q_rot, same.astype(BF16)], axis=0)
        for begin in range(0, length, QBLOCK):
            stop = begin + QBLOCK
            result = 0.0
            for low, high, diagonal in key_parts(begin, window):
                e = jnp.exp(dot(keys[low:high], query[:, begin:stop], 1, 0))
                if diagonal:
                    e = jnp.where(allowed, e, 0.0)
                result = result + dot(values[:, low:high], e.astype(BF16), 1, 0)
            total = result[size : size + 1]
            result = result[:size] / total
            exact_ref[rows, begin:stop] = result
            out_ref[rows, begin:stop] = result.astype(BF16)
            log_ref[0, 0, h : h + 1, begin:stop] = jnp.log(total)


def attention(qkv, segment, gain_q, gain_k, cosine, sine, size, group, pairs, docs):
    rows, length = qkv.shape
    per = (group + 2) * size * pairs
    halves = rows // per
    unit = group * size
    q_rows, k_rows = per // unit, per // size
    full = lambda a: pl.BlockSpec(a.shape, lambda i, j: (0,) * a.ndim)
    wide = pl.BlockSpec((unit, length), lambda i, j: (pairs * i + j, 0))
    thin = pl.BlockSpec((size, length), lambda i, j: (pairs * i + j, 0))
    heads = halves * pairs * group
    return pl.pallas_call(
        functools.partial(attention_kernel, docs=docs, window=length // 2),
        grid=(halves, pairs),
        in_specs=[full(a) for a in (segment, gain_q, gain_k, cosine, sine)]
        + [
            pl.BlockSpec((unit, length), lambda i, j: (q_rows * i + j, 0)),
            pl.BlockSpec((size, length), lambda i, j: (k_rows * i + pairs * group + j, 0)),
            pl.BlockSpec((size, length), lambda i, j: (k_rows * i + pairs * (group + 1) + j, 0)),
        ],
        out_specs=[
            wide, wide, pl.BlockSpec((1, 1, group, length), lambda i, j: (i, j, 0, 0)), wide, thin, thin,
        ],
        out_shape=[
            jax.ShapeDtypeStruct((heads * size, length), BF16),
            jax.ShapeDtypeStruct((heads * size, length), F32),
            jax.ShapeDtypeStruct((halves, pairs, group, length), F32),
            jax.ShapeDtypeStruct((heads * size, length), BF16),
            jax.ShapeDtypeStruct((halves * pairs * size, length), BF16),
            jax.ShapeDtypeStruct((halves * pairs * size, length), BF16),
        ],
        cost_estimate=cost(40 * heads * size * length * length // 2, qkv, qkv),
        name="attention_forward",
    )(segment, gain_q, gain_k, cosine, sine, qkv, qkv, qkv)


def attention_back_kernel(
    segment_ref, gain_q_ref, gain_k_ref, cos_ref, sin_ref, q_ref, k_ref, qs_ref, ks_ref, vs_ref, exact_ref, log_ref,
    do_ref, out_ref, gq_ref, gk_ref, dk_ref, dv_ref, *, docs, window,
):
    size, length = k_ref.shape
    group = q_ref.shape[0] // size
    pair, pairs = pl.program_id(1), pl.num_programs(1)
    cosine, sine = cos_ref[...], sin_ref[...]

    @pl.when((pl.program_id(0) == 0) & (pair == 0))
    def _():
        gq_ref[...] = jnp.zeros_like(gq_ref)
        gk_ref[...] = jnp.zeros_like(gk_ref)

    def fold(terms):
        width = gq_ref.shape[1]
        return sum(terms[:, i : i + width] for i in range(0, length, width))

    same = documents(segment_ref[...], docs, length)
    threes = (lax.broadcasted_iota(jnp.int32, (8, length), 0) < 3).astype(F32)
    keys_t = ks_ref[...]
    keys = jnp.concatenate([keys_t.astype(F32), (same - 1.0) * BLOCKED, threes], axis=0).T.astype(BF16)
    values = jnp.concatenate([vs_ref[...].astype(F32), threes], axis=0).T.astype(BF16)
    allowed = causal(QBLOCK)
    dk_ref[...] = jnp.zeros_like(dk_ref)
    dv_ref[...] = jnp.zeros_like(dv_ref)
    scale = size ** (-0.5)
    for h in range(group):
        rows = pl.ds(h * size, size)
        q_t, do_t = qs_ref[rows, :], do_ref[rows, :]
        do_wide = do_t.astype(F32)
        q_nat = q_t.astype(F32).T.astype(BF16)
        do_nat = do_wide.T.astype(BF16)
        delta = jnp.sum(do_wide * exact_ref[rows, :], axis=0, keepdims=True)
        logs = [-v.astype(F32) for v in split_low(log_ref[0, 0, h : h + 1, :])]
        deltas = [-v.astype(F32) for v in split_low(delta)]
        zeros = jnp.zeros((5, length), F32)
        query = jnp.concatenate(
            [q_t, jnp.concatenate([same] + logs + [zeros], axis=0).astype(BF16)], axis=0
        )
        d_out = jnp.concatenate([do_wide] + deltas + [zeros], axis=0).astype(BF16)
        d_query = []
        for begin in range(0, length, QBLOCK):
            stop = begin + QBLOCK
            d_q = 0.0
            for low, high, diagonal in key_parts(begin, window):
                p = jnp.exp(dot(keys[low:high], query[:, begin:stop], 1, 0))
                if diagonal:
                    p = jnp.where(allowed, p, 0.0)
                ds = (p * dot(values[low:high], d_out[:, begin:stop], 1, 0)).astype(BF16)
                dv_ref[low:high, :] += dot(p.astype(BF16), do_nat[begin:stop], 1, 0)
                dk_ref[low:high, :] += dot(ds, q_nat[begin:stop], 1, 0)
                d_q = d_q + dot(keys_t[:, low:high], ds, 1, 0)
            d_query.append((d_q * scale).astype(BF16).astype(F32))
        d_q0, terms = rope_rows_back(
            jnp.concatenate(d_query, axis=1), q_ref[rows, :], gain_q_ref[...], cosine, sine
        )
        gq_ref[...] += fold(terms)
        out_ref[pl.ds((pair * group + h) * size, size), :] = d_q0.astype(BF16)
    d_key = dk_ref[...].T.astype(BF16).astype(F32)
    d_k0, terms = rope_rows_back(d_key, k_ref[...], gain_k_ref[...], cosine, sine)
    gk_ref[...] += fold(terms)
    out_ref[pl.ds((pairs * group + pair) * size, size), :] = d_k0.astype(BF16)
    out_ref[pl.ds((pairs * (group + 1) + pair) * size, size), :] = dv_ref[...].T.astype(BF16)


def attention_back(qkv, qs, ks, vs, exact, logs, d_out, segment, gain_q, gain_k, cosine, sine, size, group, pairs, docs):
    rows, length = qkv.shape
    per = (group + 2) * size * pairs
    halves = rows // per
    unit = group * size
    q_rows, k_rows = per // unit, per // size
    full = lambda a: pl.BlockSpec(a.shape, lambda i, j: (0,) * a.ndim)
    wide = pl.BlockSpec((unit, length), lambda i, j: (pairs * i + j, 0))
    thin = pl.BlockSpec((size, length), lambda i, j: (pairs * i + j, 0))
    return pl.pallas_call(
        functools.partial(attention_back_kernel, docs=docs, window=length // 2),
        grid=(halves, pairs),
        in_specs=[full(a) for a in (segment, gain_q, gain_k, cosine, sine)]
        + [
            pl.BlockSpec((unit, length), lambda i, j: (q_rows * i + j, 0)),
            pl.BlockSpec((size, length), lambda i, j: (k_rows * i + pairs * group + j, 0)),
            wide, thin, thin, wide,
            pl.BlockSpec((1, 1, group, length), lambda i, j: (i, j, 0, 0)),
            wide,
        ],
        out_specs=[
            pl.BlockSpec((per, length), lambda i, j: (i, 0)),
            pl.BlockSpec((size, 128), lambda i, j: (0, 0)),
            pl.BlockSpec((size, 128), lambda i, j: (0, 0)),
        ],
        out_shape=[
            jax.ShapeDtypeStruct((rows, length), BF16),
            jax.ShapeDtypeStruct((size, 128), F32),
            jax.ShapeDtypeStruct((size, 128), F32),
        ],
        scratch_shapes=[pltpu.VMEM((length, size), F32), pltpu.VMEM((length, size), F32)],
        cost_estimate=cost(80 * rows * length * length // 4, qkv, qkv),
        name="attention_backward",
    )(segment, gain_q, gain_k, cosine, sine, qkv, qkv, qs, ks, vs, exact, logs, d_out)


LANES = 128


def local_block(i, c, blocks):
    return lax.div(i, blocks) * 2 * blocks + c * blocks + lax.rem(i, blocks)


def front_kernel(sel_ref, own_ref, other_ref, gain_ref, query_ref, key_ref, value_ref, normed_ref, out_ref):
    local = own_ref.shape[0]

    @pl.when(pl.program_id(0) == 0)
    def _():
        for i, ref in enumerate((own_ref, other_ref)):
            place = pl.multiple_of((sel_ref[0] if i == 0 else 1 - sel_ref[0]) * local, local)
            v = ref[...].astype(F32)
            v = v * lax.rsqrt(jnp.mean(v * v, axis=-1, keepdims=True) + EPSILON) * gain_ref[...]
            normed_ref[pl.ds(place, local), :] = v.astype(BF16)

    at = 0
    for ref in (query_ref, key_ref, value_ref):
        out_ref[at : at + ref.shape[1], :] = dot(ref[...], normed_ref[...], 0, 1)
        at += ref.shape[1]


def front(sel, own, other, gain, w_query, w_key, w_value):
    local, d = own.shape
    widths = [w.shape[1] // 4 for w in (w_query, w_key, w_value)]
    part = pl.BlockSpec((local, d), lambda j, sel: (0, 0))
    return pl.pallas_call(
        front_kernel,
        grid_spec=pltpu.PrefetchScalarGridSpec(
            num_scalar_prefetch=1,
            grid=(2,),
            in_specs=[part, part, pl.BlockSpec((1, d), lambda j, sel: (0, 0))]
            + [pl.BlockSpec((d, w), lambda j, sel: (0, 2 * j + sel[0])) for w in widths],
            out_specs=[
                pl.BlockSpec((2 * local, d), lambda j, sel: (0, 0)),
                pl.BlockSpec((sum(widths), 2 * local), lambda j, sel: (j, 0)),
            ],
        ),
        out_shape=[
            jax.ShapeDtypeStruct((2 * local, d), BF16),
            jax.ShapeDtypeStruct((2 * sum(widths), 2 * local), F32),
        ],
        cost_estimate=cost(4 * local * d * 2 * sum(widths), own, own, w_query, w_query, w_query),
        name="norm_and_projections",
    )(sel, own, other, gain, w_query, w_key, w_value)


def ffn_kernel(
    sel_ref, hn_ref, own_ref, other_ref, gate0_ref, gate1_ref, up0_ref, up1_ref, down0_ref, down1_ref,
    act_ref, dg_ref, du_ref, gate_leave_ref, up_leave_ref, down_leave_ref, hy1_ref, hz1_ref, dx1_ref, back_ref, low_ref,
    turned_ref, hz0_ref, hy0_ref, dm_ref, dx0_ref,
):
    tokens, d = hn_ref.shape

    @pl.when(pl.program_id(0) == 0)
    def _():
        c, x, y, zl = [sel_ref[i] for i in range(4)]
        local, half, rows = tokens // 2, d // 2, d // 8
        back_ref[...] = jnp.zeros_like(back_ref)
        for i, ref in enumerate((own_ref, other_ref)):
            place = pl.multiple_of((c if i == 0 else 1 - c) * local, local)
            dm_ref[pl.ds(place, local), :] = ref[...]
        turned_ref[...] = hn_ref[...].T
        for order in range(2):
            for i in range(4):
                high, low = divmod(i, 2)
                to = slice(i * rows, (i + 1) * rows)
                block = 4 * high + 2 * (zl if order else 1 - zl) + low
                (hz0_ref, hz1_ref)[order][to, :] = turned_ref[pl.ds(pl.multiple_of(block * rows, rows), rows), :]
                block = 4 * high + 2 * low + (y if order else 1 - y)
                (hy0_ref, hy1_ref)[order][to, :] = turned_ref[pl.ds(pl.multiple_of(block * rows, rows), rows), :]
            place = pl.multiple_of((x if order else 1 - x) * half, half)
            (dx0_ref, dx1_ref)[order][...] = dm_ref[:, pl.ds(place, half)]

    gate_w = jnp.concatenate([gate0_ref[...], gate1_ref[...]], axis=1)
    up_w = jnp.concatenate([up0_ref[...], up1_ref[...]], axis=1)
    down_w = jnp.concatenate([down0_ref[...], down1_ref[...]], axis=0)
    step = min(256, tokens)
    for begin in range(0, tokens, step):
        at = slice(begin, begin + step)
        gate = dot(hn_ref[at, :], gate_w, 1, 0)
        up = dot(hn_ref[at, :], up_w, 1, 0)
        d_act = dot(dm_ref[at, :], down_w, 1, 1)
        sigmoid = 1.0 / (1.0 + jnp.exp(-gate))
        silu = gate * sigmoid
        act_ref[at, :] = (silu * up).astype(BF16)
        du_ref[at, :] = (d_act * silu).astype(BF16)
        dg_ref[at, :] = (d_act * up * (sigmoid + silu * (1.0 - sigmoid))).astype(BF16)
    up_leave_ref[...] = dot(hz0_ref[...], du_ref[...], 1, 0).astype(BF16)
    gate_leave_ref[...] = dot(hy0_ref[...], dg_ref[...], 1, 0).astype(BF16)
    both_w = jnp.concatenate([gate_w, up_w], axis=1)
    for begin in range(0, tokens, step):
        at = slice(begin, begin + step)
        back_ref[at, :] += dot(jnp.concatenate([dg_ref[at, :], du_ref[at, :]], axis=1), both_w, 1, 1)
    down_leave_ref[...] = dot(act_ref[...].T, dx0_ref[...], 1, 0).astype(BF16)

    @pl.when(pl.program_id(0) == pl.num_programs(0) - 1)
    def _():
        low_ref[...] = back_ref[...].astype(BF16)


def feed_forward(sel, hnormed, d_own, d_other, w_gate, w_up, w_down):
    tokens, d = hnormed.shape
    units = w_gate.shape[1] // 2
    blocks = units // 2 // LANES
    block = 2 * LANES
    whole = pl.BlockSpec((tokens, d), lambda j, sel: (0, 0))
    part = pl.BlockSpec((tokens // 2, d), lambda j, sel: (0, 0))
    columns = [
        pl.BlockSpec((d, LANES), lambda j, sel, i=i: (0, local_block(2 * j + i, sel[0], blocks))) for i in range(2)
    ]
    rows = [pl.BlockSpec((LANES, d), lambda j, sel, i=i: (local_block(2 * j + i, sel[0], blocks), 0)) for i in range(2)]
    return pl.pallas_call(
        ffn_kernel,
        grid_spec=pltpu.PrefetchScalarGridSpec(
            num_scalar_prefetch=1,
            grid=(units // block,),
            in_specs=[whole, part, part] + columns + columns + rows,
            out_specs=[pl.BlockSpec((tokens, block), lambda j, sel: (0, j))] * 3
            + [pl.BlockSpec((d // 2, block), lambda j, sel: (0, j))] * 2
            + [pl.BlockSpec((block, d // 2), lambda j, sel: (j, 0))]
            + [pl.BlockSpec((d // 2, tokens), lambda j, sel: (0, 0))] * 2
            + [pl.BlockSpec((tokens, d // 2), lambda j, sel: (0, 0))]
            + [whole, whole],
            scratch_shapes=[pltpu.VMEM((d, tokens), BF16)]
            + [pltpu.VMEM((d // 2, tokens), BF16)] * 2
            + [pltpu.VMEM((tokens, d), BF16), pltpu.VMEM((tokens, d // 2), BF16)],
        ),
        out_shape=[jax.ShapeDtypeStruct((tokens, units), BF16)] * 3
        + [jax.ShapeDtypeStruct((d // 2, units), BF16)] * 2
        + [jax.ShapeDtypeStruct((units, d // 2), BF16)]
        + [jax.ShapeDtypeStruct((d // 2, tokens), BF16)] * 2
        + [jax.ShapeDtypeStruct((tokens, d // 2), BF16)]
        + [jax.ShapeDtypeStruct((tokens, d), t) for t in (F32, BF16)],
        name="feed_forward",
    )(sel, hnormed, d_own, d_other, w_gate, w_gate, w_up, w_up, w_down, w_down)


def ffn_grads_kernel(act_ref, dg_ref, du_ref, hn_y_ref, hn_z_ref, dm_ref, gate_ref, up_ref, down_ref):
    up_ref[...] = dot(hn_z_ref[...], du_ref[...], 1, 0).astype(BF16)
    gate_ref[...] = dot(hn_y_ref[...], dg_ref[...], 1, 0).astype(BF16)
    down_ref[...] = dot(act_ref[...].T, dm_ref[...], 1, 0).astype(BF16)


def ffn_grads(act, d_gate, d_up, hn_y, hn_z, dm_x):
    tokens, units = act.shape
    half = hn_y.shape[0]
    block = 2 * LANES
    columns = pl.BlockSpec((tokens, block), lambda j: (0, j))
    turned = pl.BlockSpec((half, tokens), lambda j: (0, 0))
    out = pl.BlockSpec((half, block), lambda j: (0, j))
    return pl.pallas_call(
        ffn_grads_kernel,
        grid=(units // block,),
        in_specs=[columns] * 3 + [turned] * 2 + [pl.BlockSpec((tokens, half), lambda j: (0, 0))],
        out_specs=[out, out, pl.BlockSpec((block, half), lambda j: (j, 0))],
        out_shape=[jax.ShapeDtypeStruct((half, units), BF16)] * 2 + [jax.ShapeDtypeStruct((units, half), BF16)],
        cost_estimate=cost(2 * tokens * half * units, act),
        compiler_params=pltpu.CompilerParams(vmem_limit_bytes=20 << 20),
        name="feed_forward_gradients",
    )(act, d_gate, d_up, hn_y, hn_z, dm_x)


def ffn_out_kernel(sel_ref, act_ref, down0_ref, down1_ref, own_ref, low_ref):
    local = own_ref.shape[0]
    down_w = jnp.concatenate([down0_ref[...], down1_ref[...]], axis=0)
    own_ref[...] = dot(act_ref[pl.ds(pl.multiple_of(sel_ref[0] * local, local), local), :], down_w, 1, 0)
    other = act_ref[pl.ds(pl.multiple_of((1 - sel_ref[0]) * local, local), local), :]
    low_ref[...] = dot(other, down_w, 1, 0).astype(BF16)


def ffn_out(sel, act, w_down):
    tokens, units = act.shape
    d = w_down.shape[1]
    block = min(256, d)
    weights = [pl.BlockSpec((units // 2, block), lambda j, sel, i=i: (2 * i + sel[0], j)) for i in range(2)]
    return pl.pallas_call(
        ffn_out_kernel,
        grid_spec=pltpu.PrefetchScalarGridSpec(
            num_scalar_prefetch=1,
            grid=(d // block,),
            in_specs=[pl.BlockSpec((tokens, units), lambda j, sel: (0, 0))] + weights,
            out_specs=[pl.BlockSpec((tokens // 2, block), lambda j, sel: (0, j))] * 2,
        ),
        out_shape=[jax.ShapeDtypeStruct((tokens // 2, d), t) for t in (F32, BF16)],
        cost_estimate=pl.CostEstimate(flops=10**9, transcendentals=0, bytes_accessed=1),
        compiler_params=pltpu.CompilerParams(vmem_limit_bytes=24 << 20),
        name="feed_forward_out",
    )(sel, act, w_down, w_down)


def tie(values, *others):
    return lax.optimization_barrier((tuple(values), others))[0]


def cost(flops, *arrays):
    return pl.CostEstimate(flops=flops, transcendentals=0, bytes_accessed=sum(a.size * a.dtype.itemsize for a in arrays))


def add_up(terms):
    return sum(t.astype(F32) for t in terms)


def leave(terms, dim, bit):
    size = terms[0].shape[dim] // 2
    if dim < terms[0].ndim - 2:
        return add_up([lax.dynamic_slice_in_dim(t, (1 - bit) * size, size, dim) for t in terms]).astype(BF16)
    low = add_up([lax.slice_in_dim(t, 0, size, axis=dim) for t in terms])
    high = add_up([lax.slice_in_dim(t, size, 2 * size, axis=dim) for t in terms])
    return pick(bit, high, low).astype(BF16)


def stay(terms, dim, bit):
    size = terms[0].shape[dim] // 2 if terms else 0
    if terms and dim < terms[0].ndim - 2:
        return [lax.dynamic_slice_in_dim(t, bit * size, size, dim) for t in terms]
    return [
        pick(bit, lax.slice_in_dim(t, 0, size, axis=dim), lax.slice_in_dim(t, size, 2 * size, axis=dim))
        for t in terms
    ]


def halve(terms, axis, dim):
    bit = lax.axis_index(axis)
    return stay(terms, dim, bit) + [swap(leave(terms, dim, bit), axis)]


def share_rows(total, c):
    rows = total.shape[0] // 2
    own = pick(c, total[:rows], total[rows:])
    other = swap(pick(c, total[rows:], total[:rows]).astype(BF16), "c").astype(F32)
    return in_order(c, own, other, 1)


def own_rows(v, c, local):
    return pick(c, v[:local], v[local:])


def pair_body(
    tokens, cotangent, doc_lengths, attn_gain, w_query, w_key, w_value, query_gain, key_gain, w_out,
    ffn_gain, w_gate, w_up, w_down,
):
    local, d = tokens.shape[1:]
    length = 2 * local
    size = query_gain.shape[0]
    kv_count = w_key.shape[1] // size
    group = w_query.shape[1] // w_key.shape[1]
    pairs = kv_count // 4
    zh, zl, y, c, x = [lax.axis_index(a) for a in AXES]
    gain_attn = attn_gain.astype(F32)
    gain_ffn = ffn_gain.astype(F32)
    gain_q = query_gain.astype(F32)[:, None]
    gain_k = key_gain.astype(F32)[:, None]

    come_tokens = transpose_pair(tokens[0])
    lengths = jnp.where(c == x, doc_lengths[0], swap(doc_lengths[0], "c"))
    ends = jnp.cumsum(lengths)
    positions = jnp.arange(length, dtype=jnp.int32)
    segment = jnp.sum((ends[:, None] <= positions[None, :]).astype(jnp.int32), axis=0, keepdims=True)
    half = size // 2
    spread = jnp.exp(jnp.arange(half, dtype=F32) * (-2.0 * math.log(1000000.0) / size))
    angles = spread[:, None] * positions.astype(F32)[None, :]
    cosine, sine = jnp.cos(angles), jnp.sin(angles)
    parts = [part_columns(w, c) for w in (w_query, w_key, w_value)]
    w_qkv = jnp.concatenate([p[i] for i in range(2) for p in parts], axis=1)
    out_w = part_rows(w_out, c)
    sel = jnp.stack([c, x, y, zl]).astype(jnp.int32)
    w_qkv, out_w, cosine, sine, sel, come_tokens = tie((w_qkv, out_w, cosine, sine, sel, come_tokens))
    own_tokens = jnp.where(c == x, tokens[0], come_tokens)
    other_tokens = swap(own_tokens, "c")
    cot_low, other_tokens = tie((cotangent[0], other_tokens))
    come_cot = transpose_pair(cot_low)
    normed, qkv = front(sel, own_tokens, other_tokens, gain_attn[None], w_query, w_key, w_value)
    docs = doc_lengths.shape[1]
    attended_own, exact, logs, qs, ks, vs = attention(
        qkv, segment, gain_q, gain_k, cosine, sine, size, group, pairs, docs
    )
    attended_own, come_cot = tie((attended_own, come_cot))
    attended_other = swap(attended_own, "c")
    own_cot = jnp.where(c == x, cot_low, come_cot)
    other_cot = swap(own_cot, "c")
    width = attended_own.shape[0] // 2
    attended = jnp.concatenate(
        [in_order(c, attended_own[i : i + width], attended_other[i : i + width], 0) for i in (0, width)], axis=0
    )
    inputs = in_order(c, own_tokens, other_tokens, 0).astype(F32)
    hidden = inputs + dot(attended, w_out, 0, 0)
    hnormed = rms_scale(hidden, gain_ffn).astype(BF16)

    act, d_gate, d_up, send_gate, send_up, send_down, hn_y, hn_z, dm_x, d_hn, d_hn_low = feed_forward(
        sel, hnormed, own_cot, other_cot, w_gate, w_up, w_down
    )
    come_up, come_down, come_gate = swap(send_up, "zl"), swap(send_down, "x"), swap(send_gate, "y")
    d_hn_other = swap(d_hn_low, "c")
    keep_gate, keep_up, keep_down = ffn_grads(act, d_gate, d_up, hn_y, hn_z, dm_x)
    units = d_gate.shape[1]
    rows = d // 8
    half = d // 2
    (d_hn_other,) = tie((d_hn_other,), keep_up, keep_gate, keep_down)
    d_hn = d_hn + d_hn_other.astype(F32)
    d_hidden_norm, ffn_gain_terms = norm_back(d_hn, hidden, gain_ffn)
    d_hidden = in_order(c, own_cot, other_cot, 0).astype(F32) + d_hidden_norm
    d_attn = d_hidden.astype(BF16)
    d_attended = dot(out_w, d_attn, 1, 1).astype(BF16)

    quarter = d // 4
    send_out, keep_out = [
        dot(attended, lax.dynamic_slice_in_dim(d_attn, (2 * i + c) * quarter, quarter, 1), 1, 0).astype(BF16)
        for i in (1 - x, x)
    ]
    come_out = swap(send_out, "x")
    act, d_attended = tie((act, d_attended), send_out, keep_out)
    part_out, out_low = ffn_out(sel, act, w_down)

    come_up, come_down, come_gate, part_out, out_low, d_attended = tie(
        (come_up, come_down, come_gate, part_out, out_low, d_attended)
    )
    up = [v.reshape(2, 2, rows, units) for v in (come_up, keep_up)]
    down = [v.reshape(2, 2, units // 4, half) for v in (come_down, keep_down)]
    gate = [v.reshape(2, 2, rows, units) for v in (come_gate, keep_gate)]
    send_gate, send_down, send_up = leave(gate, 1, zl), leave(down, 1, y), leave(up, 3, x)
    gate = stay(gate, 1, zl) + [swap(send_gate, "zl")]
    down = stay(down, 1, y) + [swap(send_down, "y")]
    up = stay(up, 3, x) + [swap(send_up, "x")]
    come_out, d_attended, out_low = tie((come_out, d_attended, out_low), send_gate, send_down, send_up)
    out_other = swap(out_low, "c")
    d_qkv, gain_q_terms, gain_k_terms = attention_back(
        qkv, qs, ks, vs, exact, logs, d_attended, segment, gain_q, gain_k, cosine, sine, size, group, pairs, docs
    )
    d_qkv, out_other = tie((d_qkv, out_other))
    width = d_qkv.shape[0] // 2
    send_qkv = dot(normed, lax.dynamic_slice_in_dim(d_qkv, (1 - x) * width, width, 0), 0, 1).astype(BF16)
    come_qkv = swap(send_qkv, "x")
    (d_qkv,) = tie((d_qkv,), send_qkv)
    part_low = dot(pick(c, d_qkv[:, local:], d_qkv[:, :local]), w_qkv, 0, 1).astype(BF16)
    part_other = swap(part_low, "c")
    (d_qkv,) = tie((d_qkv,), part_low)
    part = dot(pick(c, d_qkv[:, :local], d_qkv[:, local:]), w_qkv, 0, 1)
    keep_qkv = dot(normed, lax.dynamic_slice_in_dim(d_qkv, x * width, width, 0), 0, 1).astype(BF16)

    gate[-1], down[-1], up[-1], part_other = tie((gate[-1], down[-1], up[-1], part_other), part, keep_qkv)
    send_gate, send_down, send_up = leave(gate, 3, x), add_up(down).astype(BF16), leave(up, 1, y)
    gate = stay(gate, 3, x) + [swap(send_gate, "x")]
    down = down + [lax.ppermute(send_down, ("zl", "c"), [(2, 0), (1, 3)])]
    up = stay(up, 1, y) + [swap(send_up, "y")]
    (part_other,) = tie((part_other,), send_gate, send_down, send_up)
    d_normed = part + part_other.astype(F32)
    d_input_norm, attn_gain_terms = norm_back(d_normed, own_tokens.astype(F32), gain_attn)
    d_inputs = own_rows(d_hidden, c, local) + d_input_norm
    gains = jnp.concatenate(
        [
            jnp.sum(attn_gain_terms, axis=0),
            jnp.sum(ffn_gain_terms, axis=0) * 0.5,
            jnp.sum(gain_q_terms, axis=1),
            jnp.sum(gain_k_terms, axis=1),
        ]
    ).reshape(-1, 128)
    reached = swap(gains, "zh")
    output = own_rows(hidden, c, local) + part_out + out_other.astype(F32)
    results = jnp.concatenate([output.astype(BF16), d_inputs.astype(BF16)], axis=0)

    def joined(parts):
        first, second, joint = parts
        return add_up([jnp.concatenate([add_up(first), add_up(second)], axis=-1)] + joint)

    def next_stage(parts, axis, dim):
        bit = lax.axis_index(axis)
        come = swap(joined([stay(p, dim, 1 - bit) for p in parts]).astype(BF16), axis)
        first, second, joint = [stay(p, dim, bit) for p in parts]
        return first, second, joint + [come]

    gate[-1], down[-1], up[-1], come_qkv, reached, results = tie(
        (gate[-1], down[-1], up[-1], come_qkv, reached, results)
    )
    send_gate, send_down, send_up = leave(gate, 0, zh), leave(down, 0, zh), leave(up, 0, zh)
    gate = stay(gate, 0, zh) + [swap(send_gate, "zh")]
    down = stay(down, 0, zh) + [swap(send_down, "zh")]
    up = stay(up, 0, zh) + [swap(send_up, "zh")]
    out = [v.reshape(2, 2, 2, rows, quarter) for v in (come_out, keep_out)]
    qkv_grad = [v.reshape(2, 2, 2, rows, width) for v in (come_qkv, keep_qkv)]
    first, second, joint = next_stage((out, qkv_grad, []), "y", 2)
    gains = gains + reached
    gains = gains + swap(gains, "x")
    results, gains = tie((results, gains))
    results_other = transpose_pair(results)
    joint[-1], gains = tie((joint[-1], gains))
    first, second, joint = next_stage((first, second, joint), "zl", 1)
    gains = gains + swap(gains, "c")
    gains = gains + swap(gains, "y")
    joint[-1], gains = tie((joint[-1], gains))
    first, second, joint = next_stage((first, second, joint), "zh", 0)
    gains = gains + swap(gains, "zl")
    gate[-1], down[-1], up[-1], gains = tie((gate[-1], down[-1], up[-1], gains))

    total = add_up(down).reshape(-1, d // 2)
    n = total.shape[0] // 2
    own = pick(c, total[:n], total[n:])
    other = pick(c, total[n:], total[:n]).astype(BF16)
    other = lax.ppermute(other, ("zl", "c"), [(0, 1), (3, 2)]).astype(F32)
    sum_down = jnp.where(zl == c, own, other)
    sum_gate, sum_up = [share_rows(add_up(t).reshape(rows, units // 2), c) for t in (gate, up)]
    (joint[-1],) = tie((joint[-1],), sum_gate, sum_up, sum_down)
    gains = gains.reshape(-1)
    both = joined((first, second, joint)).reshape(rows, 3 * quarter)
    n = rows // 2
    own = pick(c, both[:n], both[n:])
    other = swap(pick(c, both[n:], both[:n]).astype(BF16), "c").astype(F32)
    first, second = pick(c, own, other), pick(c, other, own)
    q_width, kv_width = pairs * group * size, pairs * size
    ends_of = [0, quarter, quarter + q_width, quarter + q_width + kv_width, quarter + q_width + 2 * kv_width]
    sum_out, sum_query, sum_key, sum_value = [
        jnp.concatenate([first[:, low:high], second[:, low:high]], axis=1)
        for low, high in zip(ends_of[:-1], ends_of[1:])
    ]
    stays = c == x
    output = jnp.where(stays, output, results_other[:local].astype(F32))
    d_inputs = jnp.where(stays, d_inputs, results_other[local:].astype(F32))
    return (
        output[None],
        d_inputs[None],
        gains[:d],
        sum_query,
        sum_key,
        sum_value,
        gains[2 * d : 2 * d + size],
        gains[2 * d + size :],
        sum_out,
        gains[d : 2 * d],
        sum_gate,
        sum_up,
        sum_down,
    )


def solution(mesh):
    rows, shards = mesh.shape["dp"], mesh.shape["seq"]
    if rows == 16 and shards == 2:
        body = pair_body
        mesh = Mesh(mesh.devices.reshape(2, 2, 2, 2, 2), AXES)
        dp, seq = AXES[:4], "x"
    else:
        body = general_body
        dp, seq = "dp", "seq"
    return jax.shard_map(
        body,
        mesh=mesh,
        in_specs=(P(dp, seq, None), P(dp, seq, None), P(dp, None)) + (P(),) * 11,
        out_specs=(P(dp, seq, None), P(dp, seq, None), P())
        + (P(dp, seq),) * 3
        + (P(), P(), P(dp, seq), P())
        + (P(dp, seq),) * 3,
        check_vma=False,
    )
```

```python
import math

import functools

import jax
import jax.numpy as jnp
from jax import lax
from jax.experimental import pallas as pl
from jax.experimental.pallas import tpu as pltpu
from jax.sharding import Mesh
from jax.sharding import PartitionSpec as P

EPSILON = 1e-06


def rms_scale(values, gain):
    return values * lax.rsqrt(jnp.mean(values * values, axis=-1, keepdims=True) + EPSILON) * gain


def norm_back(incoming, values, gain):
    inverse = lax.rsqrt(jnp.mean(values * values, axis=-1, keepdims=True) + EPSILON)
    unit = values * inverse
    scaled = incoming * gain
    d_values = inverse * (scaled - unit * jnp.mean(scaled * unit, axis=-1, keepdims=True))
    return (d_values, incoming * unit)


def rope_tables(first, count, width):
    half = width // 2
    spread = jnp.exp(jnp.arange(half, dtype=jnp.float32) * (-2.0 * math.log(1000000.0) / width))
    places = (first + jnp.arange(count, dtype=jnp.int32)).astype(jnp.float32)
    angles = places[:, None] * spread[None, :]
    return (jnp.cos(angles)[:, None, :], jnp.sin(angles)[:, None, :])


def rotate(values, cosine, sine):
    half = values.shape[-1] // 2
    first_half = values[..., :half]
    second_half = values[..., half:]
    return jnp.concatenate(
        [first_half * cosine - second_half * sine, second_half * cosine + first_half * sine],
        axis=-1,
    )


def reduce_grads(grads):
    partial_sum = lax.psum_scatter(grads, "dp", scatter_dimension=0, tiled=True)
    return lax.psum_scatter(partial_sum, "seq", scatter_dimension=1, tiled=True)


def general_body(
    tokens,
    cotangent,
    doc_lengths,
    attn_gain,
    w_query,
    w_key,
    w_value,
    query_gain,
    key_gain,
    w_out,
    ffn_gain,
    w_gate,
    w_up,
    w_down,
):
    shards = lax.axis_size("seq")
    local = tokens.shape[1]
    length = local * shards
    head_size = query_gain.shape[0]
    kv_count = w_key.shape[1] // head_size
    head_count = w_query.shape[1] // head_size
    group = head_count // kv_count
    kv_local = kv_count // shards
    block = min(512, length)
    num_blocks = length // block
    scale = head_size ** (-0.5)
    f32 = jnp.float32
    bf16 = jnp.bfloat16
    gain_attn = attn_gain.astype(f32)
    gain_query = query_gain.astype(f32)
    gain_key = key_gain.astype(f32)
    gain_ffn = ffn_gain.astype(f32)
    inputs = tokens[0].astype(f32)
    normed = rms_scale(inputs, gain_attn).astype(bf16)
    query_raw = jnp.dot(normed, w_query, preferred_element_type=f32).reshape(
        local, head_count, head_size
    )
    key_raw = jnp.dot(normed, w_key, preferred_element_type=f32).reshape(local, kv_count, head_size)
    values = (
        jnp.dot(normed, w_value, preferred_element_type=f32)
        .astype(bf16)
        .reshape(local, kv_count, head_size)
    )
    cosine, sine = rope_tables(lax.axis_index("seq") * local, local, head_size)
    query_rot = rotate(rms_scale(query_raw, gain_query), cosine, sine).astype(bf16)
    key_rot = rotate(rms_scale(key_raw, gain_key), cosine, sine).astype(bf16)
    packed_query = query_rot.reshape(local, kv_count, group * head_size)
    packed_kv = jnp.concatenate([key_rot, values], axis=2)
    query_heads, kv_heads = (
        lax.all_to_all(packed_query, "seq", split_axis=1, concat_axis=0, tiled=True),
        lax.all_to_all(packed_kv, "seq", split_axis=1, concat_axis=0, tiled=True),
    )
    query_all = query_heads.reshape(length, kv_local, group, head_size)
    key_all = kv_heads[:, :, :head_size]
    value_all = kv_heads[:, :, head_size:]
    positions = jnp.arange(length, dtype=jnp.int32)
    ends = jnp.cumsum(doc_lengths[0])
    segment = jnp.sum((ends[None, :] <= positions[:, None]).astype(jnp.int32), axis=1)
    starts = jnp.arange(num_blocks, dtype=jnp.int32) * block

    def allowed_at(begin):
        rows_here = begin + jnp.arange(block, dtype=jnp.int32)
        query_seg = lax.dynamic_slice_in_dim(segment, begin, block, 0)
        return (query_seg[:, None] == segment[None, :]) & (positions[None, :] <= rows_here[:, None])

    def block_scores(begin):
        query_block = lax.dynamic_slice_in_dim(query_all, begin, block, 0)
        scores = (
            jnp.einsum("qhgd,khd->hgqk", query_block, key_all, preferred_element_type=f32) * scale
        )
        return (query_block, jnp.where(allowed_at(begin), scores, -jnp.inf))

    def attend(begin):
        query_block, scores = block_scores(begin)
        top_score = jnp.max(scores, axis=-1, keepdims=True)
        expos = jnp.exp(scores - top_score)
        totals = jnp.sum(expos, axis=-1, keepdims=True)
        probs = (expos / totals).astype(bf16)
        result = jnp.einsum("hgqk,khd->qhgd", probs, value_all, preferred_element_type=f32)
        return (result.astype(bf16), top_score[..., 0] + jnp.log(totals[..., 0]))

    attended_heads, log_totals = lax.map(attend, starts)
    attended_heads = attended_heads.reshape(length, kv_local, group * head_size)
    attended = lax.all_to_all(
        attended_heads, "seq", split_axis=0, concat_axis=1, tiled=True
    ).reshape(local, head_count * head_size)
    hidden = inputs + jnp.dot(attended, w_out, preferred_element_type=f32)
    hnormed = rms_scale(hidden, gain_ffn).astype(bf16)
    gate = jnp.dot(hnormed, w_gate, preferred_element_type=f32)
    up_part = jnp.dot(hnormed, w_up, preferred_element_type=f32)
    act = (jax.nn.silu(gate) * up_part).astype(bf16)
    output = hidden + jnp.dot(act, w_down, preferred_element_type=f32)
    d_mlp = cotangent[0]
    grad_down = jnp.einsum("tf,td->fd", act, d_mlp, preferred_element_type=f32)
    d_act = jnp.einsum("td,fd->tf", d_mlp, w_down, preferred_element_type=f32)
    gate_again = jnp.dot(hnormed, w_gate, preferred_element_type=f32)
    up_again = jnp.dot(hnormed, w_up, preferred_element_type=f32)
    sigmoid_gate = jax.nn.sigmoid(gate_again)
    d_up = (d_act * gate_again * sigmoid_gate).astype(bf16)
    d_gate = (d_act * up_again * sigmoid_gate * (1.0 + gate_again * (1.0 - sigmoid_gate))).astype(
        bf16
    )
    grad_gate = jnp.einsum("td,tf->df", hnormed, d_gate, preferred_element_type=f32)
    grad_up = jnp.einsum("td,tf->df", hnormed, d_up, preferred_element_type=f32)
    ffn_sums = reduce_grads((grad_gate, grad_up, grad_down))
    d_hnormed = jnp.einsum("tf,df->td", d_gate, w_gate, preferred_element_type=f32) + jnp.einsum(
        "tf,df->td", d_up, w_up, preferred_element_type=f32
    )
    d_hidden_norm, ffn_gain_terms = norm_back(d_hnormed, hidden, gain_ffn)
    d_hidden = cotangent[0].astype(f32) + d_hidden_norm
    d_attn = d_hidden.astype(bf16)
    grad_out = jnp.einsum("tf,td->fd", attended, d_attn, preferred_element_type=f32)
    d_attended = jnp.einsum("td,fd->tf", d_attn, w_out, preferred_element_type=f32).astype(bf16)
    d_heads = lax.all_to_all(
        d_attended.reshape(local, kv_count, group * head_size),
        "seq",
        split_axis=1,
        concat_axis=0,
        tiled=True,
    )
    d_all = d_heads.reshape(length, kv_local, group, head_size)

    def attend_back(carry, item):
        begin, log_block = item
        query_block, scores = block_scores(begin)
        probs = jnp.exp(scores - log_block[..., None])
        d_block = lax.dynamic_slice_in_dim(d_all, begin, block, 0)
        d_probs = jnp.einsum("qhgd,khd->hgqk", d_block, value_all, preferred_element_type=f32)
        delta = jnp.sum(probs * d_probs, axis=-1, keepdims=True)
        d_scores = (scale * (probs * (d_probs - delta))).astype(bf16)
        d_query_block = jnp.einsum("hgqk,khd->qhgd", d_scores, key_all, preferred_element_type=f32)
        key_total = carry[0] + jnp.einsum(
            "hgqk,qhgd->khd", d_scores, query_block, preferred_element_type=f32
        )
        value_total = carry[1] + jnp.einsum(
            "hgqk,qhgd->khd", probs.astype(bf16), d_block, preferred_element_type=f32
        )
        return ((key_total, value_total), d_query_block.astype(bf16))

    empty = jnp.zeros((length, kv_local, head_size), f32)
    (d_keys, d_values), d_queries = lax.scan(attend_back, (empty, empty), (starts, log_totals))
    d_queries = d_queries.reshape(length, kv_local, group * head_size)
    d_kv = jnp.concatenate([d_keys.astype(bf16), d_values.astype(bf16)], axis=2)
    d_query_pos, d_kv_pos = (
        lax.all_to_all(d_queries, "seq", split_axis=0, concat_axis=1, tiled=True),
        lax.all_to_all(d_kv, "seq", split_axis=0, concat_axis=1, tiled=True),
    )
    d_query_rot = d_query_pos.reshape(local, head_count, head_size).astype(f32)
    d_query_raw, query_gain_terms = norm_back(
        rotate(d_query_rot, cosine, -sine), query_raw, gain_query
    )
    d_query_low = d_query_raw.reshape(local, head_count * head_size).astype(bf16)
    d_key_rot = d_kv_pos[:, :, :head_size].astype(f32)
    d_key_raw, key_gain_terms = norm_back(rotate(d_key_rot, cosine, -sine), key_raw, gain_key)
    d_key_low = d_key_raw.reshape(local, kv_count * head_size).astype(bf16)
    d_value_low = d_kv_pos[:, :, head_size:].reshape(local, kv_count * head_size)
    grad_query = jnp.einsum("td,tf->df", normed, d_query_low, preferred_element_type=f32)
    grad_key = jnp.einsum("td,tf->df", normed, d_key_low, preferred_element_type=f32)
    grad_value = jnp.einsum("td,tf->df", normed, d_value_low, preferred_element_type=f32)
    d_normed = jnp.einsum("tf,df->td", d_query_low, w_query, preferred_element_type=f32)
    d_normed = d_normed + jnp.einsum("tf,df->td", d_key_low, w_key, preferred_element_type=f32)
    d_normed = d_normed + jnp.einsum("tf,df->td", d_value_low, w_value, preferred_element_type=f32)
    d_input_norm, attn_gain_terms = norm_back(d_normed, inputs, gain_attn)
    d_inputs = d_hidden + d_input_norm
    attn_sums = reduce_grads((grad_query, grad_key, grad_value, grad_out))
    gain_totals = lax.psum(
        (
            jnp.sum(attn_gain_terms, axis=0),
            jnp.sum(query_gain_terms, axis=(0, 1)),
            jnp.sum(key_gain_terms, axis=(0, 1)),
            jnp.sum(ffn_gain_terms, axis=0),
        ),
        ("dp", "seq"),
    )
    return (
        output[None],
        d_inputs[None],
        gain_totals[0],
        attn_sums[0],
        attn_sums[1],
        attn_sums[2],
        gain_totals[1],
        gain_totals[2],
        attn_sums[3],
        gain_totals[3],
        ffn_sums[0],
        ffn_sums[1],
        ffn_sums[2],
    )


AXES = ("zh", "zl", "y", "c", "x")
QBLOCK = 256
F32 = jnp.float32
BF16 = jnp.bfloat16


def swap(v, axis):
    return lax.ppermute(v, axis, [(0, 1), (1, 0)])


def transpose_pair(v):
    return lax.ppermute(v, ("c", "x"), [(1, 2), (2, 1)])


def pick(bit, low, high):
    return jnp.where(bit == 0, low, high)


def in_order(bit, own, other, axis):
    return jnp.concatenate([pick(bit, own, other), pick(bit, other, own)], axis=axis)


def dot(left, right, left_dim, right_dim):
    return lax.dot_general(
        left, right, (((left_dim,), (right_dim,)), ((), ())), preferred_element_type=F32
    )


def part_columns(w, c):
    width = w.shape[1] // 4
    return [lax.dynamic_slice_in_dim(w, (2 * i + c) * width, width, 1) for i in range(2)]


def part_rows(w, c):
    rows, columns = w.shape
    return lax.dynamic_index_in_dim(w.reshape(2, 2, rows // 4, columns), c, 1, False).reshape(rows // 2, columns)


def rope_rows(values, gain, cosine, sine):
    unit = values * lax.rsqrt(jnp.mean(values * values, axis=0, keepdims=True) + EPSILON) * gain
    half = values.shape[0] // 2
    first, second = unit[:half], unit[half:]
    return jnp.concatenate([first * cosine - second * sine, second * cosine + first * sine], axis=0)


def rope_rows_back(incoming, values, gain, cosine, sine):
    half = values.shape[0] // 2
    first, second = incoming[:half], incoming[half:]
    turned = jnp.concatenate([first * cosine + second * sine, second * cosine - first * sine], axis=0)
    inverse = lax.rsqrt(jnp.mean(values * values, axis=0, keepdims=True) + EPSILON)
    unit = values * inverse
    scaled = turned * gain
    d_values = inverse * (scaled - unit * jnp.mean(scaled * unit, axis=0, keepdims=True))
    return d_values, turned * unit


BLOCKED = 256.0


def split_low(v):
    high = v.astype(BF16)
    rest = v - high.astype(F32)
    middle = rest.astype(BF16)
    return [high, middle, (rest - middle.astype(F32)).astype(BF16)]


def documents(segment, rows, length):
    return (segment == lax.broadcasted_iota(jnp.int32, (rows, length), 0)).astype(F32)


def key_parts(begin, window):
    low = max(0, begin - (window - 1)) // QBLOCK * QBLOCK
    return ([(low, begin, False)] if begin > low else []) + [(begin, begin + QBLOCK, True)]


def causal(block):
    key_at = lax.broadcasted_iota(jnp.int32, (block, block), 0)
    return key_at <= lax.broadcasted_iota(jnp.int32, (block, block), 1)


def attention_kernel(
    segment_ref, gain_q_ref, gain_k_ref, cos_ref, sin_ref, q_ref, k_ref, v_ref,
    out_ref, exact_ref, log_ref, qs_ref, ks_ref, vs_ref, *, docs, window,
):
    size, length = k_ref.shape
    group = q_ref.shape[0] // size
    cosine, sine = cos_ref[...], sin_ref[...]
    same = documents(segment_ref[...], docs, length)
    k_rot = rope_rows(k_ref[...], gain_k_ref[...], cosine, sine)
    ks_ref[...] = k_rot.astype(BF16)
    keys = jnp.concatenate([k_rot, (same - 1.0) * BLOCKED], axis=0).T.astype(BF16)
    values = v_ref[...].astype(BF16)
    vs_ref[...] = values
    ones = (lax.broadcasted_iota(jnp.int32, (16, length), 0) == 0).astype(BF16)
    values = jnp.concatenate([values, ones], axis=0)
    allowed = causal(QBLOCK)
    for h in range(group):
        rows = pl.ds(h * size, size)
        q_rot = rope_rows(q_ref[rows, :], gain_q_ref[...], cosine, sine).astype(BF16)
        q_rot = q_rot * jnp.asarray(size ** (-0.5), BF16)
        qs_ref[rows, :] = q_rot
        query = jnp.concatenate([q_rot, same.astype(BF16)], axis=0)
        for begin in range(0, length, QBLOCK):
            stop = begin + QBLOCK
            result = 0.0
            for low, high, diagonal in key_parts(begin, window):
                e = jnp.exp(dot(keys[low:high], query[:, begin:stop], 1, 0))
                if diagonal:
                    e = jnp.where(allowed, e, 0.0)
                result = result + dot(values[:, low:high], e.astype(BF16), 1, 0)
            total = result[size : size + 1]
            result = result[:size] / total
            exact_ref[rows, begin:stop] = result
            out_ref[rows, begin:stop] = result.astype(BF16)
            log_ref[0, 0, h : h + 1, begin:stop] = jnp.log(total)


def attention(qkv, segment, gain_q, gain_k, cosine, sine, size, group, pairs, docs):
    rows, length = qkv.shape
    per = (group + 2) * size * pairs
    halves = rows // per
    unit = group * size
    q_rows, k_rows = per // unit, per // size
    full = lambda a: pl.BlockSpec(a.shape, lambda i, j: (0,) * a.ndim)
    wide = pl.BlockSpec((unit, length), lambda i, j: (pairs * i + j, 0))
    thin = pl.BlockSpec((size, length), lambda i, j: (pairs * i + j, 0))
    heads = halves * pairs * group
    return pl.pallas_call(
        functools.partial(attention_kernel, docs=docs, window=length // 2),
        grid=(halves, pairs),
        in_specs=[full(a) for a in (segment, gain_q, gain_k, cosine, sine)]
        + [
            pl.BlockSpec((unit, length), lambda i, j: (q_rows * i + j, 0)),
            pl.BlockSpec((size, length), lambda i, j: (k_rows * i + pairs * group + j, 0)),
            pl.BlockSpec((size, length), lambda i, j: (k_rows * i + pairs * (group + 1) + j, 0)),
        ],
        out_specs=[
            wide, wide, pl.BlockSpec((1, 1, group, length), lambda i, j: (i, j, 0, 0)), wide, thin, thin,
        ],
        out_shape=[
            jax.ShapeDtypeStruct((heads * size, length), BF16),
            jax.ShapeDtypeStruct((heads * size, length), F32),
            jax.ShapeDtypeStruct((halves, pairs, group, length), F32),
            jax.ShapeDtypeStruct((heads * size, length), BF16),
            jax.ShapeDtypeStruct((halves * pairs * size, length), BF16),
            jax.ShapeDtypeStruct((halves * pairs * size, length), BF16),
        ],
        cost_estimate=cost(40 * heads * size * length * length // 2, qkv, qkv),
        name="attention_forward",
    )(segment, gain_q, gain_k, cosine, sine, qkv, qkv, qkv)


def attention_back_kernel(
    segment_ref, gain_q_ref, gain_k_ref, cos_ref, sin_ref, q_ref, k_ref, qs_ref, ks_ref, vs_ref, exact_ref, log_ref,
    do_ref, out_ref, gq_ref, gk_ref, dk_ref, dv_ref, *, docs, window,
):
    size, length = k_ref.shape
    group = q_ref.shape[0] // size
    pair, pairs = pl.program_id(1), pl.num_programs(1)
    cosine, sine = cos_ref[...], sin_ref[...]

    @pl.when((pl.program_id(0) == 0) & (pair == 0))
    def _():
        gq_ref[...] = jnp.zeros_like(gq_ref)
        gk_ref[...] = jnp.zeros_like(gk_ref)

    def fold(terms):
        width = gq_ref.shape[1]
        return sum(terms[:, i : i + width] for i in range(0, length, width))

    same = documents(segment_ref[...], docs, length)
    threes = (lax.broadcasted_iota(jnp.int32, (8, length), 0) < 3).astype(F32)
    keys_t = ks_ref[...]
    keys = jnp.concatenate([keys_t.astype(F32), (same - 1.0) * BLOCKED, threes], axis=0).T.astype(BF16)
    values = jnp.concatenate([vs_ref[...].astype(F32), threes], axis=0).T.astype(BF16)
    allowed = causal(QBLOCK)
    dk_ref[...] = jnp.zeros_like(dk_ref)
    dv_ref[...] = jnp.zeros_like(dv_ref)
    scale = size ** (-0.5)
    for h in range(group):
        rows = pl.ds(h * size, size)
        q_t, do_t = qs_ref[rows, :], do_ref[rows, :]
        do_wide = do_t.astype(F32)
        q_nat = q_t.astype(F32).T.astype(BF16)
        do_nat = do_wide.T.astype(BF16)
        delta = jnp.sum(do_wide * exact_ref[rows, :], axis=0, keepdims=True)
        logs = [-v.astype(F32) for v in split_low(log_ref[0, 0, h : h + 1, :])]
        deltas = [-v.astype(F32) for v in split_low(delta)]
        zeros = jnp.zeros((5, length), F32)
        query = jnp.concatenate(
            [q_t, jnp.concatenate([same] + logs + [zeros], axis=0).astype(BF16)], axis=0
        )
        d_out = jnp.concatenate([do_wide] + deltas + [zeros], axis=0).astype(BF16)
        d_query = []
        for begin in range(0, length, QBLOCK):
            stop = begin + QBLOCK
            d_q = 0.0
            for low, high, diagonal in key_parts(begin, window):
                p = jnp.exp(dot(keys[low:high], query[:, begin:stop], 1, 0))
                if diagonal:
                    p = jnp.where(allowed, p, 0.0)
                ds = (p * dot(values[low:high], d_out[:, begin:stop], 1, 0)).astype(BF16)
                dv_ref[low:high, :] += dot(p.astype(BF16), do_nat[begin:stop], 1, 0)
                dk_ref[low:high, :] += dot(ds, q_nat[begin:stop], 1, 0)
                d_q = d_q + dot(keys_t[:, low:high], ds, 1, 0)
            d_query.append((d_q * scale).astype(BF16).astype(F32))
        d_q0, terms = rope_rows_back(
            jnp.concatenate(d_query, axis=1), q_ref[rows, :], gain_q_ref[...], cosine, sine
        )
        gq_ref[...] += fold(terms)
        out_ref[pl.ds((pair * group + h) * size, size), :] = d_q0.astype(BF16)
    d_key = dk_ref[...].T.astype(BF16).astype(F32)
    d_k0, terms = rope_rows_back(d_key, k_ref[...], gain_k_ref[...], cosine, sine)
    gk_ref[...] += fold(terms)
    out_ref[pl.ds((pairs * group + pair) * size, size), :] = d_k0.astype(BF16)
    out_ref[pl.ds((pairs * (group + 1) + pair) * size, size), :] = dv_ref[...].T.astype(BF16)


def attention_back(qkv, qs, ks, vs, exact, logs, d_out, segment, gain_q, gain_k, cosine, sine, size, group, pairs, docs):
    rows, length = qkv.shape
    per = (group + 2) * size * pairs
    halves = rows // per
    unit = group * size
    q_rows, k_rows = per // unit, per // size
    full = lambda a: pl.BlockSpec(a.shape, lambda i, j: (0,) * a.ndim)
    wide = pl.BlockSpec((unit, length), lambda i, j: (pairs * i + j, 0))
    thin = pl.BlockSpec((size, length), lambda i, j: (pairs * i + j, 0))
    return pl.pallas_call(
        functools.partial(attention_back_kernel, docs=docs, window=length // 2),
        grid=(halves, pairs),
        in_specs=[full(a) for a in (segment, gain_q, gain_k, cosine, sine)]
        + [
            pl.BlockSpec((unit, length), lambda i, j: (q_rows * i + j, 0)),
            pl.BlockSpec((size, length), lambda i, j: (k_rows * i + pairs * group + j, 0)),
            wide, thin, thin, wide,
            pl.BlockSpec((1, 1, group, length), lambda i, j: (i, j, 0, 0)),
            wide,
        ],
        out_specs=[
            pl.BlockSpec((per, length), lambda i, j: (i, 0)),
            pl.BlockSpec((size, 128), lambda i, j: (0, 0)),
            pl.BlockSpec((size, 128), lambda i, j: (0, 0)),
        ],
        out_shape=[
            jax.ShapeDtypeStruct((rows, length), BF16),
            jax.ShapeDtypeStruct((size, 128), F32),
            jax.ShapeDtypeStruct((size, 128), F32),
        ],
        scratch_shapes=[pltpu.VMEM((length, size), F32), pltpu.VMEM((length, size), F32)],
        cost_estimate=cost(80 * rows * length * length // 4, qkv, qkv),
        compiler_params=pltpu.CompilerParams(vmem_limit_bytes=28 << 20),
        name="attention_backward",
    )(segment, gain_q, gain_k, cosine, sine, qkv, qkv, qs, ks, vs, exact, logs, d_out)


LANES = 128


def local_block(i, c, blocks):
    return lax.div(i, blocks) * 2 * blocks + c * blocks + lax.rem(i, blocks)


def front_kernel(sel_ref, own_ref, other_ref, gain_ref, query_ref, key_ref, value_ref, normed_ref, out_ref):
    local = own_ref.shape[0]

    @pl.when(pl.program_id(0) == 0)
    def _():
        for i, ref in enumerate((own_ref, other_ref)):
            place = pl.multiple_of((sel_ref[0] if i == 0 else 1 - sel_ref[0]) * local, local)
            v = ref[...].astype(F32)
            v = v * lax.rsqrt(jnp.mean(v * v, axis=-1, keepdims=True) + EPSILON) * gain_ref[...]
            normed_ref[pl.ds(place, local), :] = v.astype(BF16)

    at = 0
    for ref in (query_ref, key_ref, value_ref):
        out_ref[at : at + ref.shape[1], :] = dot(ref[...], normed_ref[...], 0, 1)
        at += ref.shape[1]


def front(sel, own, other, gain, w_query, w_key, w_value):
    local, d = own.shape
    widths = [w.shape[1] // 4 for w in (w_query, w_key, w_value)]
    part = pl.BlockSpec((local, d), lambda j, sel: (0, 0))
    return pl.pallas_call(
        front_kernel,
        grid_spec=pltpu.PrefetchScalarGridSpec(
            num_scalar_prefetch=1,
            grid=(2,),
            in_specs=[part, part, pl.BlockSpec((1, d), lambda j, sel: (0, 0))]
            + [pl.BlockSpec((d, w), lambda j, sel: (0, 2 * j + sel[0])) for w in widths],
            out_specs=[
                pl.BlockSpec((2 * local, d), lambda j, sel: (0, 0)),
                pl.BlockSpec((sum(widths), 2 * local), lambda j, sel: (j, 0)),
            ],
        ),
        out_shape=[
            jax.ShapeDtypeStruct((2 * local, d), BF16),
            jax.ShapeDtypeStruct((2 * sum(widths), 2 * local), F32),
        ],
        cost_estimate=cost(4 * local * d * 2 * sum(widths), own, own, w_query, w_query, w_query),
        name="norm_and_projections",
    )(sel, own, other, gain, w_query, w_key, w_value)


def ffn_kernel(
    sel_ref, hn_ref, own_ref, other_ref, gate0_ref, gate1_ref, up0_ref, up1_ref, down0_ref, down1_ref,
    act_ref, dg_ref, du_ref, gate_leave_ref, up_leave_ref, down_leave_ref, hy1_ref, hz1_ref, dx1_ref, back_ref, low_ref,
    turned_ref, hz0_ref, hy0_ref, dm_ref, dx0_ref,
):
    tokens, d = hn_ref.shape

    @pl.when(pl.program_id(0) == 0)
    def _():
        c, x, y, zl = [sel_ref[i] for i in range(4)]
        local, half, rows = tokens // 2, d // 2, d // 8
        back_ref[...] = jnp.zeros_like(back_ref)
        for i, ref in enumerate((own_ref, other_ref)):
            place = pl.multiple_of((c if i == 0 else 1 - c) * local, local)
            dm_ref[pl.ds(place, local), :] = ref[...]
        turned_ref[...] = hn_ref[...].T
        for order in range(2):
            for i in range(4):
                high, low = divmod(i, 2)
                to = slice(i * rows, (i + 1) * rows)
                block = 4 * high + 2 * (zl if order else 1 - zl) + low
                (hz0_ref, hz1_ref)[order][to, :] = turned_ref[pl.ds(pl.multiple_of(block * rows, rows), rows), :]
                block = 4 * high + 2 * low + (y if order else 1 - y)
                (hy0_ref, hy1_ref)[order][to, :] = turned_ref[pl.ds(pl.multiple_of(block * rows, rows), rows), :]
            place = pl.multiple_of((x if order else 1 - x) * half, half)
            (dx0_ref, dx1_ref)[order][...] = dm_ref[:, pl.ds(place, half)]

    gate_w = jnp.concatenate([gate0_ref[...], gate1_ref[...]], axis=1)
    up_w = jnp.concatenate([up0_ref[...], up1_ref[...]], axis=1)
    down_w = jnp.concatenate([down0_ref[...], down1_ref[...]], axis=0)
    step = min(256, tokens)
    for begin in range(0, tokens, step):
        at = slice(begin, begin + step)
        gate = dot(hn_ref[at, :], gate_w, 1, 0)
        up = dot(hn_ref[at, :], up_w, 1, 0)
        d_act = dot(dm_ref[at, :], down_w, 1, 1)
        sigmoid = 1.0 / (1.0 + jnp.exp(-gate))
        silu = gate * sigmoid
        act_ref[at, :] = (silu * up).astype(BF16)
        du_ref[at, :] = (d_act * silu).astype(BF16)
        dg_ref[at, :] = (d_act * up * (sigmoid + silu * (1.0 - sigmoid))).astype(BF16)
    up_leave_ref[...] = dot(hz0_ref[...], du_ref[...], 1, 0).astype(BF16)
    gate_leave_ref[...] = dot(hy0_ref[...], dg_ref[...], 1, 0).astype(BF16)
    both_w = jnp.concatenate([gate_w, up_w], axis=1)
    for begin in range(0, tokens, step):
        at = slice(begin, begin + step)
        back_ref[at, :] += dot(jnp.concatenate([dg_ref[at, :], du_ref[at, :]], axis=1), both_w, 1, 1)
    down_leave_ref[...] = dot(act_ref[...].T, dx0_ref[...], 1, 0).astype(BF16)

    @pl.when(pl.program_id(0) == pl.num_programs(0) - 1)
    def _():
        low_ref[...] = back_ref[...].astype(BF16)


def feed_forward(sel, hnormed, d_own, d_other, w_gate, w_up, w_down):
    tokens, d = hnormed.shape
    units = w_gate.shape[1] // 2
    blocks = units // 2 // LANES
    block = 2 * LANES
    whole = pl.BlockSpec((tokens, d), lambda j, sel: (0, 0))
    part = pl.BlockSpec((tokens // 2, d), lambda j, sel: (0, 0))
    columns = [
        pl.BlockSpec((d, LANES), lambda j, sel, i=i: (0, local_block(2 * j + i, sel[0], blocks))) for i in range(2)
    ]
    rows = [pl.BlockSpec((LANES, d), lambda j, sel, i=i: (local_block(2 * j + i, sel[0], blocks), 0)) for i in range(2)]
    return pl.pallas_call(
        ffn_kernel,
        grid_spec=pltpu.PrefetchScalarGridSpec(
            num_scalar_prefetch=1,
            grid=(units // block,),
            in_specs=[whole, part, part] + columns + columns + rows,
            out_specs=[pl.BlockSpec((tokens, block), lambda j, sel: (0, j))] * 3
            + [pl.BlockSpec((d // 2, block), lambda j, sel: (0, j))] * 2
            + [pl.BlockSpec((block, d // 2), lambda j, sel: (j, 0))]
            + [pl.BlockSpec((d // 2, tokens), lambda j, sel: (0, 0))] * 2
            + [pl.BlockSpec((tokens, d // 2), lambda j, sel: (0, 0))]
            + [whole, whole],
            scratch_shapes=[pltpu.VMEM((d, tokens), BF16)]
            + [pltpu.VMEM((d // 2, tokens), BF16)] * 2
            + [pltpu.VMEM((tokens, d), BF16), pltpu.VMEM((tokens, d // 2), BF16)],
        ),
        out_shape=[jax.ShapeDtypeStruct((tokens, units), BF16)] * 3
        + [jax.ShapeDtypeStruct((d // 2, units), BF16)] * 2
        + [jax.ShapeDtypeStruct((units, d // 2), BF16)]
        + [jax.ShapeDtypeStruct((d // 2, tokens), BF16)] * 2
        + [jax.ShapeDtypeStruct((tokens, d // 2), BF16)]
        + [jax.ShapeDtypeStruct((tokens, d), t) for t in (F32, BF16)],
        name="feed_forward",
    )(sel, hnormed, d_own, d_other, w_gate, w_gate, w_up, w_up, w_down, w_down)


def ffn_grads_kernel(act_ref, dg_ref, du_ref, hn_y_ref, hn_z_ref, dm_ref, gate_ref, up_ref, down_ref):
    up_ref[...] = dot(hn_z_ref[...], du_ref[...], 1, 0).astype(BF16)
    gate_ref[...] = dot(hn_y_ref[...], dg_ref[...], 1, 0).astype(BF16)
    down_ref[...] = dot(act_ref[...].T, dm_ref[...], 1, 0).astype(BF16)


def ffn_grads(act, d_gate, d_up, hn_y, hn_z, dm_x):
    tokens, units = act.shape
    half = hn_y.shape[0]
    block = 2 * LANES
    columns = pl.BlockSpec((tokens, block), lambda j: (0, j))
    turned = pl.BlockSpec((half, tokens), lambda j: (0, 0))
    out = pl.BlockSpec((half, block), lambda j: (0, j))
    return pl.pallas_call(
        ffn_grads_kernel,
        grid=(units // block,),
        in_specs=[columns] * 3 + [turned] * 2 + [pl.BlockSpec((tokens, half), lambda j: (0, 0))],
        out_specs=[out, out, pl.BlockSpec((block, half), lambda j: (j, 0))],
        out_shape=[jax.ShapeDtypeStruct((half, units), BF16)] * 2 + [jax.ShapeDtypeStruct((units, half), BF16)],
        cost_estimate=cost(2 * tokens * half * units, act),
        compiler_params=pltpu.CompilerParams(vmem_limit_bytes=20 << 20),
        name="feed_forward_gradients",
    )(act, d_gate, d_up, hn_y, hn_z, dm_x)


def ffn_out_kernel(sel_ref, act_ref, down0_ref, down1_ref, own_ref, low_ref):
    local = own_ref.shape[0]
    down_w = jnp.concatenate([down0_ref[...], down1_ref[...]], axis=0)
    own_ref[...] = dot(act_ref[pl.ds(pl.multiple_of(sel_ref[0] * local, local), local), :], down_w, 1, 0)
    other = act_ref[pl.ds(pl.multiple_of((1 - sel_ref[0]) * local, local), local), :]
    low_ref[...] = dot(other, down_w, 1, 0).astype(BF16)


def ffn_out(sel, act, w_down):
    tokens, units = act.shape
    d = w_down.shape[1]
    block = min(256, d)
    weights = [pl.BlockSpec((units // 2, block), lambda j, sel, i=i: (2 * i + sel[0], j)) for i in range(2)]
    return pl.pallas_call(
        ffn_out_kernel,
        grid_spec=pltpu.PrefetchScalarGridSpec(
            num_scalar_prefetch=1,
            grid=(d // block,),
            in_specs=[pl.BlockSpec((tokens, units), lambda j, sel: (0, 0))] + weights,
            out_specs=[pl.BlockSpec((tokens // 2, block), lambda j, sel: (0, j))] * 2,
        ),
        out_shape=[jax.ShapeDtypeStruct((tokens // 2, d), t) for t in (F32, BF16)],
        cost_estimate=pl.CostEstimate(flops=10**9, transcendentals=0, bytes_accessed=1),
        compiler_params=pltpu.CompilerParams(vmem_limit_bytes=24 << 20),
        name="feed_forward_out",
    )(sel, act, w_down, w_down)


def tie(values, *others):
    return lax.optimization_barrier((tuple(values), others))[0]


def cost(flops, *arrays):
    return pl.CostEstimate(flops=flops, transcendentals=0, bytes_accessed=sum(a.size * a.dtype.itemsize for a in arrays))


def add_up(terms):
    return sum(t.astype(F32) for t in terms)


def leave(terms, dim, bit):
    size = terms[0].shape[dim] // 2
    if dim < terms[0].ndim - 2:
        return add_up([lax.dynamic_slice_in_dim(t, (1 - bit) * size, size, dim) for t in terms]).astype(BF16)
    low = add_up([lax.slice_in_dim(t, 0, size, axis=dim) for t in terms])
    high = add_up([lax.slice_in_dim(t, size, 2 * size, axis=dim) for t in terms])
    return pick(bit, high, low).astype(BF16)


def stay(terms, dim, bit):
    size = terms[0].shape[dim] // 2 if terms else 0
    if terms and dim < terms[0].ndim - 2:
        return [lax.dynamic_slice_in_dim(t, bit * size, size, dim) for t in terms]
    return [
        pick(bit, lax.slice_in_dim(t, 0, size, axis=dim), lax.slice_in_dim(t, size, 2 * size, axis=dim))
        for t in terms
    ]


def halve(terms, axis, dim):
    bit = lax.axis_index(axis)
    return stay(terms, dim, bit) + [swap(leave(terms, dim, bit), axis)]


def share_rows(total, c):
    rows = total.shape[0] // 2
    own = pick(c, total[:rows], total[rows:])
    other = swap(pick(c, total[rows:], total[:rows]).astype(BF16), "c").astype(F32)
    return in_order(c, own, other, 1)


def own_rows(v, c, local):
    return pick(c, v[:local], v[local:])


def pair_body(
    tokens, cotangent, doc_lengths, attn_gain, w_query, w_key, w_value, query_gain, key_gain, w_out,
    ffn_gain, w_gate, w_up, w_down,
):
    local, d = tokens.shape[1:]
    length = 2 * local
    size = query_gain.shape[0]
    kv_count = w_key.shape[1] // size
    group = w_query.shape[1] // w_key.shape[1]
    pairs = kv_count // 4
    zh, zl, y, c, x = [lax.axis_index(a) for a in AXES]
    gain_attn = attn_gain.astype(F32)
    gain_ffn = ffn_gain.astype(F32)
    gain_q = query_gain.astype(F32)[:, None]
    gain_k = key_gain.astype(F32)[:, None]

    come_tokens = transpose_pair(tokens[0])
    lengths = jnp.where(c == x, doc_lengths[0], swap(doc_lengths[0], "c"))
    ends = jnp.cumsum(lengths)
    positions = jnp.arange(length, dtype=jnp.int32)
    segment = jnp.sum((ends[:, None] <= positions[None, :]).astype(jnp.int32), axis=0, keepdims=True)
    half = size // 2
    spread = jnp.exp(jnp.arange(half, dtype=F32) * (-2.0 * math.log(1000000.0) / size))
    angles = spread[:, None] * positions.astype(F32)[None, :]
    cosine, sine = jnp.cos(angles), jnp.sin(angles)
    parts = [part_columns(w, c) for w in (w_query, w_key, w_value)]
    w_qkv = jnp.concatenate([p[i] for i in range(2) for p in parts], axis=1)
    out_w = part_rows(w_out, c)
    sel = jnp.stack([c, x, y, zl]).astype(jnp.int32)
    w_qkv, out_w, cosine, sine, sel, come_tokens = tie((w_qkv, out_w, cosine, sine, sel, come_tokens))
    own_tokens = jnp.where(c == x, tokens[0], come_tokens)
    other_tokens = swap(own_tokens, "c")
    cot_low, other_tokens = tie((cotangent[0], other_tokens))
    come_cot = transpose_pair(cot_low)
    normed, qkv = front(sel, own_tokens, other_tokens, gain_attn[None], w_query, w_key, w_value)
    docs = doc_lengths.shape[1]
    attended_own, exact, logs, qs, ks, vs = attention(
        qkv, segment, gain_q, gain_k, cosine, sine, size, group, pairs, docs
    )
    attended_own, come_cot = tie((attended_own, come_cot))
    attended_other = swap(attended_own, "c")
    own_cot = jnp.where(c == x, cot_low, come_cot)
    other_cot = swap(own_cot, "c")
    width = attended_own.shape[0] // 2
    attended = jnp.concatenate(
        [in_order(c, attended_own[i : i + width], attended_other[i : i + width], 0) for i in (0, width)], axis=0
    )
    inputs = in_order(c, own_tokens, other_tokens, 0).astype(F32)
    hidden = inputs + dot(attended, w_out, 0, 0)
    hnormed = rms_scale(hidden, gain_ffn).astype(BF16)

    act, d_gate, d_up, send_gate, send_up, send_down, hn_y, hn_z, dm_x, d_hn, d_hn_low = feed_forward(
        sel, hnormed, own_cot, other_cot, w_gate, w_up, w_down
    )
    come_up, come_down, come_gate = swap(send_up, "zl"), swap(send_down, "x"), swap(send_gate, "y")
    d_hn_other = swap(d_hn_low, "c")
    keep_gate, keep_up, keep_down = ffn_grads(act, d_gate, d_up, hn_y, hn_z, dm_x)
    units = d_gate.shape[1]
    rows = d // 8
    half = d // 2
    (d_hn_other,) = tie((d_hn_other,), keep_up, keep_gate, keep_down)
    d_hn = d_hn + d_hn_other.astype(F32)
    d_hidden_norm, ffn_gain_terms = norm_back(d_hn, hidden, gain_ffn)
    d_hidden = in_order(c, own_cot, other_cot, 0).astype(F32) + d_hidden_norm
    d_attn = d_hidden.astype(BF16)
    d_attended = dot(out_w, d_attn, 1, 1).astype(BF16)

    quarter = d // 4
    send_out, keep_out = [
        dot(attended, lax.dynamic_slice_in_dim(d_attn, (2 * i + c) * quarter, quarter, 1), 1, 0).astype(BF16)
        for i in (1 - x, x)
    ]
    come_out = swap(send_out, "x")
    act, d_attended = tie((act, d_attended), send_out, keep_out)
    part_out, out_low = ffn_out(sel, act, w_down)

    come_up, come_down, come_gate, part_out, out_low, d_attended = tie(
        (come_up, come_down, come_gate, part_out, out_low, d_attended)
    )
    up = [v.reshape(2, 2, rows, units) for v in (come_up, keep_up)]
    down = [v.reshape(2, 2, units // 4, half) for v in (come_down, keep_down)]
    gate = [v.reshape(2, 2, rows, units) for v in (come_gate, keep_gate)]
    send_gate, send_down, send_up = leave(gate, 1, zl), leave(down, 1, y), leave(up, 3, x)
    gate = stay(gate, 1, zl) + [swap(send_gate, "zl")]
    down = stay(down, 1, y) + [swap(send_down, "y")]
    up = stay(up, 3, x) + [swap(send_up, "x")]
    come_out, d_attended, out_low = tie((come_out, d_attended, out_low), send_gate, send_down, send_up)
    out_other = swap(out_low, "c")
    d_qkv, gain_q_terms, gain_k_terms = attention_back(
        qkv, qs, ks, vs, exact, logs, d_attended, segment, gain_q, gain_k, cosine, sine, size, group, pairs, docs
    )
    d_qkv, out_other = tie((d_qkv, out_other))
    width = d_qkv.shape[0] // 2
    send_qkv = dot(normed, lax.dynamic_slice_in_dim(d_qkv, (1 - x) * width, width, 0), 0, 1).astype(BF16)
    come_qkv = swap(send_qkv, "x")
    (d_qkv,) = tie((d_qkv,), send_qkv)
    part_low = dot(pick(c, d_qkv[:, local:], d_qkv[:, :local]), w_qkv, 0, 1).astype(BF16)
    part_other = swap(part_low, "c")
    (d_qkv,) = tie((d_qkv,), part_low)
    part = dot(pick(c, d_qkv[:, :local], d_qkv[:, local:]), w_qkv, 0, 1)
    keep_qkv = dot(normed, lax.dynamic_slice_in_dim(d_qkv, x * width, width, 0), 0, 1).astype(BF16)

    gate[-1], down[-1], up[-1], part_other = tie((gate[-1], down[-1], up[-1], part_other), part, keep_qkv)
    send_gate, send_down, send_up = leave(gate, 3, x), add_up(down).astype(BF16), leave(up, 1, y)
    gate = stay(gate, 3, x) + [swap(send_gate, "x")]
    down = down + [lax.ppermute(send_down, ("zl", "c"), [(2, 0), (1, 3)])]
    up = stay(up, 1, y) + [swap(send_up, "y")]
    (part_other,) = tie((part_other,), send_gate, send_down, send_up)
    d_normed = part + part_other.astype(F32)
    d_input_norm, attn_gain_terms = norm_back(d_normed, own_tokens.astype(F32), gain_attn)
    d_inputs = own_rows(d_hidden, c, local) + d_input_norm
    gains = jnp.concatenate(
        [
            jnp.sum(attn_gain_terms, axis=0),
            jnp.sum(ffn_gain_terms, axis=0) * 0.5,
            jnp.sum(gain_q_terms, axis=1),
            jnp.sum(gain_k_terms, axis=1),
        ]
    ).reshape(-1, 128)
    reached = swap(gains, "zh")
    output = own_rows(hidden, c, local) + part_out + out_other.astype(F32)
    results = jnp.concatenate([output.astype(BF16), d_inputs.astype(BF16)], axis=0)

    def joined(parts):
        first, second, joint = parts
        return add_up([jnp.concatenate([add_up(first), add_up(second)], axis=-1)] + joint)

    def next_stage(parts, axis, dim):
        bit = lax.axis_index(axis)
        come = swap(joined([stay(p, dim, 1 - bit) for p in parts]).astype(BF16), axis)
        first, second, joint = [stay(p, dim, bit) for p in parts]
        return first, second, joint + [come]

    gate[-1], down[-1], up[-1], come_qkv, reached, results = tie(
        (gate[-1], down[-1], up[-1], come_qkv, reached, results)
    )
    send_gate, send_down, send_up = leave(gate, 0, zh), leave(down, 0, zh), leave(up, 0, zh)
    gate = stay(gate, 0, zh) + [swap(send_gate, "zh")]
    down = stay(down, 0, zh) + [swap(send_down, "zh")]
    up = stay(up, 0, zh) + [swap(send_up, "zh")]
    out = [v.reshape(2, 2, 2, rows, quarter) for v in (come_out, keep_out)]
    qkv_grad = [v.reshape(2, 2, 2, rows, width) for v in (come_qkv, keep_qkv)]
    first, second, joint = next_stage((out, qkv_grad, []), "y", 2)
    gains = gains + reached
    gains = gains + swap(gains, "x")
    results, gains = tie((results, gains))
    results_other = transpose_pair(results)
    joint[-1], gains = tie((joint[-1], gains))
    first, second, joint = next_stage((first, second, joint), "zl", 1)
    gains = gains + swap(gains, "c")
    gains = gains + swap(gains, "y")
    joint[-1], gains = tie((joint[-1], gains))
    first, second, joint = next_stage((first, second, joint), "zh", 0)
    gains = gains + swap(gains, "zl")
    gate[-1], down[-1], up[-1], gains = tie((gate[-1], down[-1], up[-1], gains))

    total = add_up(down).reshape(-1, d // 2)
    n = total.shape[0] // 2
    own = pick(c, total[:n], total[n:])
    other = pick(c, total[n:], total[:n]).astype(BF16)
    other = lax.ppermute(other, ("zl", "c"), [(0, 1), (3, 2)]).astype(F32)
    sum_down = jnp.where(zl == c, own, other)
    sum_gate, sum_up = [share_rows(add_up(t).reshape(rows, units // 2), c) for t in (gate, up)]
    (joint[-1],) = tie((joint[-1],), sum_gate, sum_up, sum_down)
    gains = gains.reshape(-1)
    both = joined((first, second, joint)).reshape(rows, 3 * quarter)
    n = rows // 2
    own = pick(c, both[:n], both[n:])
    other = swap(pick(c, both[n:], both[:n]).astype(BF16), "c").astype(F32)
    first, second = pick(c, own, other), pick(c, other, own)
    q_width, kv_width = pairs * group * size, pairs * size
    ends_of = [0, quarter, quarter + q_width, quarter + q_width + kv_width, quarter + q_width + 2 * kv_width]
    sum_out, sum_query, sum_key, sum_value = [
        jnp.concatenate([first[:, low:high], second[:, low:high]], axis=1)
        for low, high in zip(ends_of[:-1], ends_of[1:])
    ]
    stays = c == x
    output = jnp.where(stays, output, results_other[:local].astype(F32))
    d_inputs = jnp.where(stays, d_inputs, results_other[local:].astype(F32))
    return (
        output[None],
        d_inputs[None],
        gains[:d],
        sum_query,
        sum_key,
        sum_value,
        gains[2 * d : 2 * d + size],
        gains[2 * d + size :],
        sum_out,
        gains[d : 2 * d],
        sum_gate,
        sum_up,
        sum_down,
    )


def solution(mesh):
    rows, shards = mesh.shape["dp"], mesh.shape["seq"]
    if rows == 16 and shards == 2:
        body = pair_body
        mesh = Mesh(mesh.devices.reshape(2, 2, 2, 2, 2), AXES)
        dp, seq = AXES[:4], "x"
    else:
        body = general_body
        dp, seq = "dp", "seq"
    return jax.shard_map(
        body,
        mesh=mesh,
        in_specs=(P(dp, seq, None), P(dp, seq, None), P(dp, None)) + (P(),) * 11,
        out_specs=(P(dp, seq, None), P(dp, seq, None), P())
        + (P(dp, seq),) * 3
        + (P(), P(), P(dp, seq), P())
        + (P(dp, seq),) * 3,
        check_vma=False,
    )
```
